32 devices in a mesh: dp: 4 (over y, x), fsdp: 8 (over z, core).
Axes of the slice: x: 2, y: 2, z: 4, core: 2. Of those that a mesh axis runs over, the one named last changes fastest.
Arguments:
- tokens: bfloat16 [8192, 1088], P(('dp', 'fsdp')), may hold values from -6 to 6
- qkv_weight: bfloat16 [1088, 3264], P('dp', 'fsdp'), may hold values from -0.1875 to 0.1875
- out_weight: bfloat16 [1088, 1088], P('dp', 'fsdp'), may hold values from -1.5 to 1.5
- fc_weight: bfloat16 [1088, 4352], P('dp', 'fsdp'), may hold values from -0.1875 to 0.1875
- proj_weight: bfloat16 [4352, 1088], P('dp', 'fsdp'), may hold values from -0.09375 to 0.09375
- norm_params: bfloat16 [4, 1088], P(None, 'dp')
- grad_out: bfloat16 [8192, 1088], P(('dp', 'fsdp')), may hold values from -6 to 6
- dealt_lengths: int32 [4, 2, 4], P('dp'), may hold values from 1 to 512, 1024 in all within a row
- seq_order: int32 [4, 8], P('dp'), may hold values from 0 to 7, each once within a row
Outputs:
- activations: bfloat16 [8192, 1088], P(('dp', 'fsdp'))
- input_grad: bfloat16 [8192, 1088], P(('dp', 'fsdp'))
- grad_qkv: float32 [1088, 3264], P('dp', 'fsdp')
- grad_attn_out: float32 [1088, 1088], P('dp', 'fsdp')
- grad_fc: float32 [1088, 4352], P('dp', 'fsdp')
- grad_proj: float32 [4352, 1088], P('dp', 'fsdp')
- grad_norms: float32 [4, 1088], P(None, 'dp')
The draws below stay inside these ranges and needn't reach their ends.
Inputs may be any that keep to these rules, and one draw needn't show every extreme that they name: `dealt_lengths`: the 4 lengths of each micro-batch of each dp group add up to 1024. `seq_order`: each dp group's row is a permutation of its 8 arrival indices; dealt sequence k belongs to micro-batch k // 4.
All inputs are finite; a program needn't handle non-finite values.
Results may differ from the reference program's by a relative error of at most 0.019.
Values may be sent and summed in bfloat16 or wider, within the bound.
No kernel may reach another device: no remote copies, remote signals or barrier semaphores. Data moves between devices by JAX's collectives and lax.ppermute only.
A program may use at most 256 MiB of HBM per device.

```python
import math
import jax
import jax.numpy as jnp
import numpy as np
from jax import lax

HEAD_DIM = 64
FF = 4352
D = 1088
TOK_MB = 128
MB = 2
SEQ_BIN = 4
TOK_DEV = 256
BIN = 1024
TOKENS = 8192
NSEQ_G = 8
LONGEST = 512
N_DP = 4
N_FSDP = 8


def draw_norm_params(key, part):
    base = jax.random.normal(key, (4, D), jnp.float32)
    row_ids = jnp.arange(4)[:, None]
    return jnp.where(row_ids % 2 == 0, 1.0 + 0.2 * base, 0.3 * base).astype(jnp.bfloat16)


def block_scale(stream_key, dims, cuts, smallest, high):
    def one(dim, blocks):
        draws = jax.random.uniform(jax.random.fold_in(jax.random.fold_in(stream_key, 6), dim), (blocks,), jnp.float32, smallest / len(cuts), high / len(cuts))
        return jnp.repeat(jnp.exp(draws), dims[dim] // blocks).reshape((-1,) + (1,) * (len(dims) - dim - 1))

    factor_of = one(*cuts[0])
    for cut in cuts[1:]:
        factor_of = factor_of * one(*cut)
    return factor_of


def profile(number_of, total, limit, slope):
    portions = [(1 << 20) // math.isqrt(standing ** slope) + 1 for standing in range(2, number_of + 1)]
    spare, given = total - limit - (number_of - 1), [1] * (number_of - 1)
    while spare > 0:
        candidates = [i for i in range(number_of - 1) if given[i] < limit]
        mass, budget = sum([portions[i] for i in candidates]), spare
        for i in candidates:
            extra = min(limit - given[i], max(1, budget * portions[i] // mass), spare)
            given[i] = given[i] + extra
            spare = spare - extra
    return np.array([limit] + given)


def ragged(stream_key, number_of, total, most, skew):
    if number_of == 2:
        one = jax.random.randint(stream_key, (), max(1, total - most), min(most, total - 1) + 1)
        return jnp.stack([one, total - one])
    tallies = jnp.asarray(profile(number_of, total, most, skew), jnp.int32)
    couples = (number_of - 1) // 2
    source_of, taker = tallies[1:1 + 2 * couples:2], tallies[2:2 + 2 * couples:2]
    slack = jnp.minimum(source_of - 1, most - taker)
    passed = jax.random.randint(jax.random.fold_in(stream_key, 1), (couples,), 0, 1 << 20) % (slack + 1)
    tallies = tallies.at[1:1 + 2 * couples:2].set(source_of - passed).at[2:2 + 2 * couples:2].set(taker + passed)
    return tallies[jax.random.permutation(jax.random.fold_in(stream_key, 2), number_of)]


def bell_draw(own_key, extent, spread, limit, cuts=(), held_as=jnp.bfloat16):
    level = block_scale(own_key, extent, cuts, -0.22, 0.18) if cuts else 1.0
    drawn = jax.random.normal(own_key, extent, jnp.float32) * spread * level
    return jnp.minimum(jnp.maximum(drawn, -limit), limit).astype(held_as)


def setup_inputs(seed: int = 0) -> dict:
    splits = jax.random.split(jax.random.key(seed), 10)
    return {
        "tokens": bell_draw(splits[0], (TOKENS, D), 1.0, 6.0, ((0, 32),)),
        "qkv_weight": bell_draw(splits[1], (D, 3 * D), D ** -0.5, 0.1875, ((0, 4), (1, 8))),
        "out_weight": bell_draw(splits[2], (D, D), (max(1, D // 64)) ** -0.5, 1.5, ((0, 4), (1, 8))),
        "fc_weight": bell_draw(splits[3], (D, FF), D ** -0.5, 0.1875, ((0, 4), (1, 8))),
        "proj_weight": bell_draw(splits[4], (FF, D), FF ** -0.5, 0.09375, ((0, 4), (1, 8))),
        "norm_params": draw_norm_params(jax.random.fold_in(splits[9], 71), 0),
        "grad_out": bell_draw(splits[6], (TOKENS, D), 1.0, 6.0, ((0, 32),)),
        "dealt_lengths": jax.vmap(lambda own: ragged(own, SEQ_BIN, BIN, LONGEST, 2))(jax.random.split(splits[7], N_DP * MB)).reshape((N_DP, MB, SEQ_BIN)).astype(jnp.int32),
        "seq_order": jax.vmap(lambda own: jax.random.permutation(own, NSEQ_G))(jax.random.split(splits[8], N_DP)).reshape((N_DP, NSEQ_G)).astype(jnp.int32),
    }


eps = 1e-05
neg_big = -1e+30

@jax.custom_vjp
def low(v):
    return lax.optimization_barrier(v.astype(jnp.bfloat16)).astype(jnp.float32)

@jax.custom_vjp
def low_back(v):
    return v

def low_keep(v):
    return (low(v), None)

def low_pass(kept, grad):
    return (grad,)

def back_keep(v):
    return (v, None)

def back_low(kept, grad):
    return (low(grad),)
low.defvjp(low_keep, low_pass)
low_back.defvjp(back_keep, back_low)

def normalize(values, gain, shift):
    center = lax.optimization_barrier(jnp.mean(values, axis=-1, keepdims=True))
    centered = values - center
    variance = lax.optimization_barrier(jnp.mean(centered * centered, axis=-1, keepdims=True))
    return centered * lax.rsqrt(variance + eps) * gain + shift

def matmul(left, right):
    return jnp.dot(left, right, precision=lax.Precision.HIGHEST, preferred_element_type=jnp.float32)

def segment_pick(positions, starts, table):
    above = (positions[:, None] >= starts[None, :]).astype(jnp.int32)
    after = jnp.concatenate([above[:, 1:], jnp.zeros_like(above[:, :1])], axis=1)
    return lax.optimization_barrier(jnp.sum((above - after) * table[None, :], axis=1)).astype(jnp.int32)

def deal_maps(lengths, deal_order, bin_rows):
    batches, seq_count = lengths.shape
    seq_total = batches * seq_count
    bin_ends = jnp.cumsum(lengths, axis=1).astype(jnp.int32)
    offsets = (bin_rows * jnp.arange(batches, dtype=jnp.int32))[:, None]
    dealt_start = (bin_ends - lengths + offsets).reshape(seq_total).astype(jnp.int32)
    flat_lengths = lengths.reshape(seq_total)
    matches = (deal_order[:, None] == jnp.arange(seq_total, dtype=jnp.int32)[None, :]).astype(jnp.int32)
    arrival_len = lax.optimization_barrier(jnp.sum(matches * flat_lengths[:, None], axis=0)).astype(jnp.int32)
    arrival_start = (jnp.cumsum(arrival_len) - arrival_len).astype(jnp.int32)
    arrival_of_dealt = lax.optimization_barrier(jnp.sum(matches * arrival_start[None, :], axis=1)).astype(jnp.int32)
    dealt_of_arrival = lax.optimization_barrier(jnp.sum(matches * dealt_start[:, None], axis=0)).astype(jnp.int32)
    return (dealt_start, arrival_start, arrival_of_dealt, dealt_of_arrival)

def layer_block(inputs, qkv_full, out_full, fc_full, proj_full, norms, seq_starts):
    bin_rows, model_width = inputs.shape
    head_count = model_width // HEAD_DIM
    score_scale = HEAD_DIM ** (-0.5)
    normed = low(normalize(inputs, norms[0], norms[1]))
    projected = matmul(normed, qkv_full)
    queries = low_back(low(projected[:, :model_width])).reshape(bin_rows, head_count, HEAD_DIM)
    all_keys = low_back(low(projected[:, model_width:2 * model_width])).reshape(bin_rows, head_count, HEAD_DIM)
    values = low_back(low(projected[:, 2 * model_width:])).reshape(bin_rows, head_count, HEAD_DIM)
    positions = jnp.arange(bin_rows, dtype=jnp.int32)
    block_rows = min(512, bin_rows)
    block_count = bin_rows // block_rows

    def one_block(block_args):
        query_block, pos_block, start_block = block_args
        raw_scores = jnp.einsum('rhd,khd->hrk', query_block, all_keys, precision=lax.Precision.HIGHEST)
        allowed = (positions[None, :] >= start_block[:, None]) & (positions[None, :] <= pos_block[:, None])
        scores = low_back(jnp.where(allowed[None], raw_scores * score_scale, neg_big))
        log_total = jax.nn.logsumexp(scores, axis=-1, keepdims=True)
        probs = low(jnp.exp(scores - log_total))
        return jnp.einsum('hrk,khd->rhd', probs, values, precision=lax.Precision.HIGHEST)
    attended = lax.map(jax.checkpoint(one_block), (queries.reshape(block_count, block_rows, head_count, HEAD_DIM), positions.reshape(block_count, block_rows), seq_starts.reshape(block_count, block_rows)))
    attended = low_back(low(attended.reshape(bin_rows, model_width)))
    middle = inputs + low_back(matmul(attended, out_full))
    normed_two = low(normalize(middle, norms[2], norms[3]))
    hidden_pre = low_back(matmul(normed_two, fc_full))
    activated = low(jax.nn.gelu(hidden_pre, approximate=False))
    return middle + matmul(activated, proj_full)

def reference(tokens, qkv_weight, out_weight, fc_weight, proj_weight, norm_params, grad_out, dealt_lengths, seq_order):
    group_rows = N_FSDP * TOK_DEV
    bin_rows = N_FSDP * TOK_MB
    model_width = tokens.shape[1]
    weight_set = (qkv_weight.astype(jnp.float32), out_weight.astype(jnp.float32), fc_weight.astype(jnp.float32), proj_weight.astype(jnp.float32), norm_params.astype(jnp.float32))

    def one_group(running, group_args):
        group_tokens, group_cot, lengths, deal_order = group_args
        dealt_start, arrival_start, arrival_of_dealt, dealt_of_arrival = deal_maps(lengths, deal_order, bin_rows)
        dealt_ids = jnp.arange(MB * bin_rows, dtype=jnp.int32)
        source_ids = dealt_ids + segment_pick(dealt_ids, dealt_start, arrival_of_dealt - dealt_start)
        seq_starts = segment_pick(dealt_ids, dealt_start, dealt_start) - dealt_ids // bin_rows * bin_rows
        dealt_in = jnp.take(group_tokens, source_ids, axis=0).reshape(MB, bin_rows, model_width)
        dealt_cot = jnp.take(group_cot, source_ids, axis=0).reshape(MB, bin_rows, model_width)

        def one_bin(totals, bin_args):
            bin_in, bin_cot, bin_starts = bin_args

            def forward_fn(inputs, qkv_full, out_full, fc_full, proj_full, norms):
                return layer_block(inputs, qkv_full, out_full, fc_full, proj_full, norms, bin_starts)
            result, pullback = jax.vjp(forward_fn, bin_in.astype(jnp.float32), weight_set[0], weight_set[1], weight_set[2], weight_set[3], weight_set[4])
            gradients = pullback(bin_cot.astype(jnp.float32))
            totals = tuple((totals[member] + gradients[member + 1] for member in range(5)))
            return (totals, (result.astype(jnp.bfloat16), gradients[0].astype(jnp.bfloat16)))
        running, (bin_out, bin_grad) = lax.scan(one_bin, running, (dealt_in, dealt_cot, seq_starts.reshape(MB, bin_rows)))
        arrival_ids = jnp.arange(group_rows, dtype=jnp.int32)
        home_ids = arrival_ids + segment_pick(arrival_ids, arrival_start, dealt_of_arrival - arrival_start)
        out_home = jnp.take(bin_out.reshape(MB * bin_rows, model_width), home_ids, axis=0)
        grad_home = jnp.take(bin_grad.reshape(MB * bin_rows, model_width), home_ids, axis=0)
        return (running, (out_home, grad_home))
    starting = tuple((jnp.zeros_like(weight_arr) for weight_arr in weight_set))
    totals, (home_outs, home_grads) = lax.scan(one_group, starting, (tokens.reshape(N_DP, group_rows, model_width), grad_out.reshape(N_DP, group_rows, model_width), dealt_lengths, seq_order))
    return (home_outs.reshape(TOKENS, model_width), home_grads.reshape(TOKENS, model_width), totals[0], totals[1], totals[2], totals[3], totals[4])
```

```python
import functools
import math

import jax
import jax.numpy as jnp
from jax import lax
from jax.experimental import pallas as pl
from jax.experimental.pallas import tpu as pltpu
from jax.sharding import PartitionSpec as P

HEAD_DIM = 64
EPS = 1e-05
NEG = -1e30
F32 = jnp.float32
BF16 = jnp.bfloat16
VMEM_ALL = 60 * 2**20

ANY = pl.BlockSpec(memory_space=pl.ANY)
VM = pl.BlockSpec(memory_space=pltpu.VMEM)
SM = pl.BlockSpec(memory_space=pltpu.SMEM)


def call(kernel, outs, in_specs, scratch=(), flops=0, nbytes=0):
    return pl.pallas_call(
        kernel,
        out_shape=tuple(jax.ShapeDtypeStruct(s, d) for s, d in outs),
        in_specs=list(in_specs),
        out_specs=tuple(VM for _ in outs),
        scratch_shapes=list(scratch),
        compiler_params=pltpu.CompilerParams(vmem_limit_bytes=VMEM_ALL),
        cost_estimate=pl.CostEstimate(flops=flops, bytes_accessed=nbytes, transcendentals=0),
    )


def dot(a, b, ca, cb):
    return lax.dot_general(a, b, (((ca,), (cb,)), ((), ())), preferred_element_type=F32)


def nn(a, b):
    return dot(a, b, 1, 0)


def nt(a, b):
    return dot(a, b, 1, 1)


def tn(a, b):
    return dot(a, b, 0, 0)


def split_cols(lo, hi, width):
    pieces = []
    while lo < hi:
        which, start = divmod(lo, width)
        stop = min(width, start + hi - lo)
        pieces.append((which, start, stop))
        lo += stop - start
    return pieces


def pack_attn_kernel(wq_ref, wo_ref, out_ref):
    half = wq_ref.shape[0] // 2
    out_ref[...] = jnp.concatenate(
        [wq_ref[:half, :], wo_ref[:half, :], wq_ref[half:, :], wo_ref[half:, :]], axis=1
    )


def pack_ffn_first_kernel(fc_ref, proj_ref, fct_ref, projt_ref):
    half = fc_ref.shape[1] // 2
    for h in range(2):
        fct_ref[h] = fc_ref[:, h * half : (h + 1) * half].astype(F32).T.astype(BF16)
    rows = proj_ref.shape[0] // 2
    for s in range(2):
        projt_ref[s] = proj_ref[s * rows : (s + 1) * rows, :].astype(F32).T.astype(BF16)


def pack_ffn_second_kernel(pos_ref, fct_ref, projt_ref, got_ref, send_ref, keep_ref):
    x, c = pos_ref[0], pos_ref[1]
    own = projt_ref[c]
    got = got_ref[...]
    rows, wide = own.shape
    half = wide // 2
    top = jnp.where(c == 0, own, got)
    low = jnp.where(c == 0, got, own)
    both = jnp.concatenate([top, low], axis=0)
    first, second = both[:, :half], both[:, half:]
    send_ref[...] = jnp.concatenate([fct_ref[1 - x], jnp.where(x == 0, second, first)], axis=1)
    keep_ref[...] = jnp.concatenate([fct_ref[x], jnp.where(x == 0, first, second)], axis=1)


def pack_ffn_third_kernel(pos_ref, keep_ref, got_ref, out_ref):
    x = pos_ref[0]
    keep, got = keep_ref[...], got_ref[...]
    first = jnp.where(x == 0, keep, got)
    second = jnp.where(x == 0, got, keep)
    h = keep.shape[1] // 2
    out_ref[...] = jnp.concatenate(
        [first[:, :h], second[:, :h], first[:, h:], second[:, h:]], axis=1
    )


def place(pieces, buf, sem, slots):
    copies = [
        pltpu.make_async_copy(piece, buf.at[slot], sem.at[i])
        for i, (piece, slot) in enumerate(zip(pieces, slots))
    ]
    for copy in copies:
        copy.start()
    for copy in copies:
        copy.wait()


def assemble_attn_kernel(keys, dims, pos_ref, *refs):
    n_dp, n_f, nq, no = dims
    pieces = refs[: len(keys)]
    w_refs = refs[len(keys) : len(keys) + 3]
    wo_ref, buf, sem = refs[len(keys) + 3 :]
    dp, f = pos_ref[2], pos_ref[3]
    slots = []
    for dy, dx, dz, dc in keys:
        slots.append((dp ^ (2 * dy + dx)) * n_f + (f ^ (2 * dz + dc)))
    place(pieces, buf, sem, slots)
    half = buf.shape[1]
    wide = nq + no
    width = wo_ref.shape[1]
    for d in range(n_dp):
        for h in range(2):
            row = (2 * d + h) * half
            base = h * wide
            for part in range(3):
                vals = [
                    buf[d * n_f + which][:, base + lo : base + hi]
                    for which, lo, hi in split_cols(part * width, (part + 1) * width, nq)
                ]
                w_refs[part][row : row + half, :] = jnp.concatenate(vals, axis=1)
            wo_ref[row : row + half, :] = jnp.concatenate(
                [buf[d * n_f + g][:, base + nq : base + wide] for g in range(n_f)], axis=1
            )


def assemble_ffn_kernel(keys, dims, pos_ref, *refs):
    n_y, n_z = dims
    pieces = refs[: len(keys)]
    fct_ref, projt_ref, buf, sem = refs[len(keys) :]
    dp, f = pos_ref[2], pos_ref[3]
    slots = [((dp >> 1) ^ dy) * n_z + ((f >> 1) ^ dz) for dy, dz in keys]
    place(pieces, buf, sem, slots)
    rows, wide = buf.shape[1:]
    half = wide // 2
    for z in range(n_z):
        vals = [buf[y * n_z + z] for y in range(n_y)]
        fct_ref[z * rows : (z + 1) * rows, :] = jnp.concatenate(
            [v[:, :half] for v in vals], axis=1
        )
        projt_ref[z * rows : (z + 1) * rows, :] = jnp.concatenate(
            [v[:, half:] for v in vals], axis=1
        )


def pack_attn_grads_kernel(dims, pos_ref, gq_ref, gk_ref, gv_ref, go_ref, out_ref):
    n_dp, n_f, nq, no = dims
    n_y, n_z = n_dp // 2, n_f // 2
    dp, f = pos_ref[2], pos_ref[3]
    parts = (gq_ref, gk_ref, gv_ref)
    width = go_ref.shape[1]
    half = out_ref.shape[1]
    for d in range(n_dp):
        for g in range(n_f):
            vals = []
            for h in range(2):
                row = (2 * d + h) * half
                for which, lo, hi in split_cols(g * nq, (g + 1) * nq, width):
                    vals.append(parts[which][row : row + half, lo:hi])
                vals.append(go_ref[row : row + half, g * no : (g + 1) * no])
            rd, rf = dp ^ d, f ^ g
            slot = (((rf & 1) * n_z + (rf >> 1)) * n_y + (rd >> 1)) * 2 + (rd & 1)
            out_ref[slot] = jnp.concatenate(vals, axis=1)


def pack_ffn_grads_kernel(dims, pos_ref, gfc_ref, gproj_ref, out_ref):
    n_y, n_z = dims
    dp, f = pos_ref[2], pos_ref[3]
    rows, wide = out_ref.shape[1:]
    half = wide // 2
    for y in range(n_y):
        for z in range(n_z):
            slot = ((dp >> 1) ^ y) * n_z + ((f >> 1) ^ z)
            out_ref[slot] = jnp.concatenate(
                [
                    gfc_ref[z * rows : (z + 1) * rows, y * half : (y + 1) * half],
                    gproj_ref[z * rows : (z + 1) * rows, y * half : (y + 1) * half],
                ],
                axis=1,
            )


def total(refs):
    acc = refs[0][...].astype(F32)
    for ref in refs[1:]:
        acc = acc + ref[...].astype(F32)
    return acc


def unpack_attn_kernel(count, *refs):
    gq_ref, go_ref = refs[count:]
    summed = total(refs[:count])
    half = summed.shape[0]
    nq, no = gq_ref.shape[1], go_ref.shape[1]
    for h in range(2):
        base = h * (nq + no)
        gq_ref[h * half : (h + 1) * half, :] = summed[:, base : base + nq]
        go_ref[h * half : (h + 1) * half, :] = summed[:, base + nq : base + nq + no]


def unpack_ffn_first_kernel(count, pos_ref, *refs):
    send_ref, keep_ref = refs[count:]
    x = pos_ref[0]
    summed = total(refs[:count])
    q = summed.shape[1] // 4
    first = jnp.concatenate([summed[:, :q], summed[:, 2 * q : 3 * q]], axis=1)
    second = jnp.concatenate([summed[:, q : 2 * q], summed[:, 3 * q :]], axis=1)
    send_ref[...] = jnp.where(x == 0, second, first).astype(BF16)
    keep_ref[...] = jnp.where(x == 0, first, second)


def unpack_ffn_second_kernel(pos_ref, keep_ref, got_ref, gfc_ref, send_ref, hold_ref):
    x, c = pos_ref[0], pos_ref[1]
    keep, got = keep_ref[...], got_ref[...].astype(F32)
    h = keep.shape[1] // 2
    rows = keep.shape[0] // 2
    first = jnp.where(x == 0, keep, got)
    second = jnp.where(x == 0, got, keep)
    gfc_ref[...] = jnp.concatenate([first[:, :h].T, second[:, :h].T], axis=1)
    both = jnp.concatenate([first[:, h:], second[:, h:]], axis=1)
    top, low = both[:rows, :], both[rows:, :]
    send_ref[...] = jnp.where(c == 0, low, top).astype(BF16)
    hold_ref[...] = jnp.where(c == 0, top, low)


def unpack_ffn_third_kernel(pos_ref, hold_ref, got_ref, gproj_ref):
    c = pos_ref[1]
    hold, got = hold_ref[...], got_ref[...].astype(F32)
    rows = hold.shape[1]
    gproj_ref[:rows, :] = jnp.where(c == 0, hold, got).T
    gproj_ref[rows:, :] = jnp.where(c == 0, got, hold).T


def fill_bias(start_ref, bias_ref):
    keys, rows = bias_ref.shape
    key_ids = lax.broadcasted_iota(jnp.int32, (keys, rows), 0)
    row_ids = lax.broadcasted_iota(jnp.int32, (keys, rows), 1) + (keys - rows)
    allowed = (key_ids >= start_ref[...]) & (key_ids <= row_ids)
    bias_ref[...] = jnp.where(allowed, 0.0, NEG)


def head_slices(width):
    pairs = width // (2 * HEAD_DIM)
    return pairs, width - pairs * 2 * HEAD_DIM


def attn_fwd_kernel(q_ref, k_ref, v_ref, start_ref, o_ref, lse_ref, qt, vt, ot, bias):
    width = q_ref.shape[1]
    fill_bias(start_ref, bias)
    qt[...] = (q_ref[...].astype(F32) * HEAD_DIM ** (-0.5)).T.astype(BF16)
    vt[...] = v_ref[...].astype(F32).T.astype(BF16)
    pairs, rest = head_slices(width)

    def one(keys, queries, values, row, head):
        scores = nn(keys, queries) + bias[...]
        peak = jnp.max(scores, axis=0, keepdims=True)
        terms = jnp.exp(scores - peak)
        summed = jnp.sum(terms, axis=0, keepdims=True)
        ot[pl.ds(row, HEAD_DIM), :] = nn(values, terms.astype(BF16)) / summed
        lse_ref[pl.ds(head, 1), :] = peak + jnp.log(summed)

    def pair(p, _):
        at = pl.multiple_of(p * 128, 128)
        keys = k_ref[:, pl.ds(at, 128)]
        queries = qt[pl.ds(at, 128), :]
        rows = lax.broadcasted_iota(jnp.int32, queries.shape, 0)
        for h in range(2):
            row = pl.multiple_of(at + h * HEAD_DIM, HEAD_DIM)
            one(
                keys,
                jnp.where((rows < HEAD_DIM) == (h == 0), queries, jnp.zeros_like(queries)),
                vt[pl.ds(row, HEAD_DIM), :],
                row,
                2 * p + h,
            )
        return 0

    lax.fori_loop(0, pairs, pair, 0)
    if rest:
        at = pairs * 128
        one(k_ref[:, at:], qt[at:, :], vt[at:, :], at, 2 * pairs)
    o_ref[...] = ot[...].T.astype(BF16)


def attn_bwd_kernel(
    q_ref, k_ref, v_ref, do_ref, lse_ref, start_ref, dq_ref, dk_ref, dv_ref, qt, dot_s, kt, dqt, bias
):
    width = q_ref.shape[1]
    scale = HEAD_DIM ** (-0.5)
    fill_bias(start_ref, bias)
    qt[...] = (q_ref[...].astype(F32) * scale).T.astype(BF16)
    dot_s[...] = do_ref[...].astype(F32).T.astype(BF16)
    kt[...] = k_ref[...].astype(F32).T.astype(BF16)
    pairs, rest = head_slices(width)

    def one(keys, values, queries_t, douts_t, keys_t, queries, douts, row, head):
        scores = nn(keys, queries_t) + bias[...]
        probs = jnp.exp(scores - lse_ref[pl.ds(head, 1), :])
        dprobs = nn(values, douts_t)
        delta = jnp.sum(probs * dprobs, axis=0, keepdims=True)
        dscores = (probs * (dprobs - delta)).astype(BF16)
        dqt[pl.ds(row, HEAD_DIM), :] = nn(keys_t, dscores)
        return nn(dscores, queries), nn(probs.astype(BF16), douts)

    def scaled(values):
        return (values.astype(F32) * scale).astype(BF16)

    def pair(p, _):
        at = pl.multiple_of(p * 128, 128)
        keys = k_ref[:, pl.ds(at, 128)]
        values = v_ref[:, pl.ds(at, 128)]
        queries = scaled(q_ref[:, pl.ds(at, 128)])
        douts = do_ref[:, pl.ds(at, 128)]
        queries_t = qt[pl.ds(at, 128), :]
        douts_t = dot_s[pl.ds(at, 128), :]
        rows = lax.broadcasted_iota(jnp.int32, queries_t.shape, 0)
        lanes = lax.broadcasted_iota(jnp.int32, queries.shape, 1)
        dk_sum = dv_sum = None
        for h in range(2):
            row = pl.multiple_of(at + h * HEAD_DIM, HEAD_DIM)
            in_rows = (rows < HEAD_DIM) == (h == 0)
            in_lanes = (lanes < HEAD_DIM) == (h == 0)
            zero_t, zero = jnp.zeros_like(queries_t), jnp.zeros_like(queries)
            dk_part, dv_part = one(
                keys,
                values,
                jnp.where(in_rows, queries_t, zero_t),
                jnp.where(in_rows, douts_t, zero_t),
                kt[pl.ds(row, HEAD_DIM), :],
                jnp.where(in_lanes, queries, zero),
                jnp.where(in_lanes, douts, zero),
                row,
                2 * p + h,
            )
            dk_sum = dk_part if h == 0 else dk_sum + dk_part
            dv_sum = dv_part if h == 0 else dv_sum + dv_part
        dk_ref[:, pl.ds(at, 128)] = dk_sum.astype(BF16)
        dv_ref[:, pl.ds(at, 128)] = dv_sum.astype(BF16)
        return 0

    lax.fori_loop(0, pairs, pair, 0)
    if rest:
        at = pairs * 128
        dk_part, dv_part = one(
            k_ref[:, at:],
            v_ref[:, at:],
            qt[at:, :],
            dot_s[at:, :],
            kt[at:, :],
            scaled(q_ref[:, at:]),
            do_ref[:, at:],
            at,
            2 * pairs,
        )
        dk_ref[:, at:] = dk_part.astype(BF16)
        dv_ref[:, at:] = dv_part.astype(BF16)
    dq_ref[...] = (dqt[...].T * scale).astype(BF16)


def xhat_of(values):
    center = jnp.mean(values, axis=-1, keepdims=True)
    centered = values - center
    variance = jnp.mean(centered * centered, axis=-1, keepdims=True)
    factor = lax.rsqrt(variance + EPS)
    return centered * factor, factor


def norm_back(grads, gain, xhat, factor):
    e = grads * gain
    return factor * (
        e
        - jnp.mean(e, axis=-1, keepdims=True)
        - xhat * jnp.mean(e * xhat, axis=-1, keepdims=True)
    )


def add(*terms):
    acc = terms[0].astype(F32)
    for term in terms[1:]:
        acc = acc + term.astype(F32)
    return acc


def segment_starts(dealt_lengths, seq_order, first_row, rows):
    lengths = dealt_lengths[0].reshape(-1)
    order = seq_order[0]
    count = lengths.shape[0]
    arrival = jnp.arange(count, dtype=jnp.int32)
    before = (order[:, None] < arrival[None, :]).astype(jnp.int32)
    begins = jnp.sum(before * lengths[:, None], axis=0)
    ids = first_row + jnp.arange(rows, dtype=jnp.int32)
    reached = begins[:, None] <= ids[None, :]
    return jnp.max(jnp.where(reached, begins[:, None], 0), axis=0)


def per_device(
    tokens,
    qkv_weight,
    out_weight,
    fc_weight,
    proj_weight,
    norm_params,
    grad_out,
    dealt_lengths,
    seq_order,
):
    n_dp, n_f = lax.axis_size("dp"), lax.axis_size("fsdp")
    n_y, n_z = n_dp // 2, n_f // 2
    dp, f = lax.axis_index("dp"), lax.axis_index("fsdp")
    x, c = dp & 1, f & 1
    pos = jnp.stack([x, c, dp, f]).astype(jnp.int32)
    tok, width = tokens.shape
    seq_longest = n_f * tok // dealt_lengths.shape[1] // 2
    halo = -(-seq_longest // tok)
    halo += halo % 2

    def xor(value, axis, bits):
        size = n_dp if axis == "dp" else n_f
        return lax.ppermute(value, axis, [(i, i ^ bits) for i in range(size)])

    def to_core(value):
        return xor(value, "fsdp", 1)

    def to_x(value):
        return xor(value, "dp", 1)

    def to_y(value, k):
        return xor(value, "dp", 2 * k)

    def to_z(value, k):
        return xor(value, "fsdp", 2 * k)

    k_rows, nq = qkv_weight.shape
    no = out_weight.shape[1]
    block = (k_rows // 2, 2 * (nq + no))
    (own_attn,) = call(pack_attn_kernel, [(block, BF16)], [VM, VM])(qkv_weight, out_weight)
    attn = {(0, 0, 0, 0): own_attn}
    for dz in range(1, n_z):
        attn[0, 0, dz, 0] = to_z(own_attn, dz)
    for dz in range(n_z):
        for dy in range(1, n_y):
            attn[dy, 0, dz, 0] = to_y(attn[0, 0, dz, 0], dy)
    for dz in range(n_z):
        for dy in range(n_y):
            attn[dy, 1, dz, 0] = to_x(attn[dy, 0, dz, 0])
    for key in list(attn):
        attn[key[:3] + (1,)] = to_core(attn[key])

    up = [(i, i + 2) for i in range(n_f - 2)]
    even = [tokens]
    for _ in range(halo // 2):
        even.append(lax.ppermute(even[-1], "fsdp", up))
    rows_before = []
    for distance in range(1, halo + 1):
        if distance % 2:
            near = distance // 2
            rows_before.append(to_core(jnp.where(c == 0, even[near], even[near + 1])))
        else:
            rows_before.append(even[distance // 2])
    x_rows = jnp.concatenate(rows_before[::-1] + [tokens], axis=0)

    norm_pieces = [norm_params] + [xor(norm_params, "dp", r) for r in range(1, n_dp)]
    norms = jnp.concatenate(
        [
            sum(
                jnp.where((dp ^ r) == j, piece.astype(F32), 0.0)
                for r, piece in enumerate(norm_pieces)
            )
            for j in range(n_dp)
        ],
        axis=1,
    )

    ff_half = fc_weight.shape[1] // 2
    sub = proj_weight.shape[0] // 4
    fct, projt = call(
        pack_ffn_first_kernel,
        [((2, ff_half, k_rows), BF16), ((2, no, 2 * sub), BF16)],
        [VM, VM],
    )(fc_weight, proj_weight)
    got = to_core(lax.dynamic_index_in_dim(projt, 1 - c, keepdims=False))
    send, keep = call(
        pack_ffn_second_kernel,
        [((ff_half, k_rows + sub), BF16)] * 2,
        [SM, VM, VM, VM],
    )(pos, fct, projt, got)
    (own_ffn,) = call(
        pack_ffn_third_kernel, [((ff_half, 2 * (k_rows + sub)), BF16)], [SM, VM, VM]
    )(pos, keep, to_x(send))
    ffn = {(0, 0): own_ffn}
    for dz in range(1, n_z):
        ffn[0, dz] = to_z(own_ffn, dz)
    for dz in range(n_z):
        for dy in range(1, n_y):
            ffn[dy, dz] = to_y(ffn[0, dz], dy)

    def share(value):
        far = to_x(value)
        return [value, to_core(value), far, to_core(far)]

    gz_rows = jnp.concatenate(share(grad_out), axis=0)

    keys = sorted(attn)
    square = ((width, width), BF16)
    dims = (n_dp, n_f, nq, no)
    wq, wk, wv, wo = call(
        functools.partial(assemble_attn_kernel, keys, dims),
        [square] * 4,
        [SM] + [ANY] * len(keys),
        [
            pltpu.VMEM((len(keys),) + block, BF16),
            pltpu.SemaphoreType.DMA((len(keys),)),
        ],
    )(pos, *[attn[key] for key in keys])
    xhat_one, factor_one = xhat_of(x_rows.astype(F32))
    normed = (xhat_one * norms[0] + norms[1]).astype(BF16)
    normed_own = normed[halo * tok :]
    queries = nn(normed_own, wq).astype(BF16)
    all_keys = nn(normed, wk).astype(BF16)
    values = nn(normed, wv).astype(BF16)
    span = (halo + 1) * tok
    starts = segment_starts(dealt_lengths, seq_order, f * tok, tok) - (f - halo) * tok
    starts = starts.reshape(1, tok).astype(jnp.int32)
    heads = width // HEAD_DIM
    attended, lse = call(
        attn_fwd_kernel,
        [((tok, width), BF16), ((heads, tok), F32)],
        [VM] * 4,
        [
            pltpu.VMEM((width, tok), BF16),
            pltpu.VMEM((width, span), BF16),
            pltpu.VMEM((width, tok), F32),
            pltpu.VMEM((span, tok), F32),
        ],
        flops=4 * span * tok * width,
    )(queries, all_keys, values, starts)
    middle = tokens.astype(F32) + nn(attended, wo)
    xhat_two, factor_two = xhat_of(middle)
    normed_two = (xhat_two * norms[2] + norms[3]).astype(BF16)

    n2_rows = jnp.concatenate(share(normed_two), axis=0)
    ffn_keys = sorted(ffn)
    fct_full, projt_full = call(
        functools.partial(assemble_ffn_kernel, ffn_keys, (n_y, n_z)),
        [((n_z * ff_half, n_y * 2 * k_rows), BF16), ((n_z * 2 * no, n_y * 2 * sub), BF16)],
        [SM] + [ANY] * len(ffn_keys),
        [
            pltpu.VMEM((len(ffn_keys),) + own_ffn.shape, BF16),
            pltpu.SemaphoreType.DMA((len(ffn_keys),)),
        ],
    )(pos, *[ffn[key] for key in ffn_keys])
    hidden = nt(n2_rows, fct_full)
    cdf = 0.5 * (1.0 + lax.erf(hidden * math.sqrt(0.5)))
    slope = cdf + hidden * jnp.exp(-0.5 * hidden * hidden) * (1.0 / math.sqrt(2.0 * math.pi))
    activated = (hidden * cdf).astype(BF16)
    dhidden = (nn(gz_rows, projt_full) * slope).astype(BF16)

    def unshare(parts):
        own, sib, far, far_sib = [parts[i * tok : (i + 1) * tok] for i in range(4)]
        far = add(far, to_core(far_sib)).astype(BF16)
        return add(own, to_core(sib), to_x(far))

    dn2 = unshare(nn(dhidden, fct_full).astype(BF16))
    grad_fct = tn(dhidden, n2_rows).astype(BF16)
    grad_projt = tn(gz_rows, activated).astype(BF16)
    (ffn_grads,) = call(
        functools.partial(pack_ffn_grads_kernel, (n_y, n_z)),
        [((n_y * n_z,) + own_ffn.shape, BF16)],
        [SM, VM, VM],
    )(pos, grad_fct, grad_projt)
    ffn_parts = []
    for dz in list(range(1, n_z)) + [0]:
        part = add(ffn_grads[dz], *[to_y(ffn_grads[dy * n_z + dz], dy) for dy in range(1, n_y)])
        part = part.astype(BF16)
        ffn_parts.append(to_z(part, dz) if dz else part)
    send, keep = call(
        functools.partial(unpack_ffn_first_kernel, n_z),
        [((ff_half, k_rows + sub), BF16), ((ff_half, k_rows + sub), F32)],
        [SM] + [VM] * n_z,
    )(pos, *ffn_parts)
    grad_fc, send, hold = call(
        unpack_ffn_second_kernel,
        [(fc_weight.shape, F32), ((no, 2 * sub), BF16), ((no, 2 * sub), F32)],
        [SM, VM, VM],
    )(pos, keep, to_x(send))
    (grad_proj,) = call(unpack_ffn_third_kernel, [(proj_weight.shape, F32)], [SM, VM, VM])(
        pos, hold, to_core(send)
    )
    activations = (middle + unshare(nt(activated, projt_full).astype(BF16))).astype(BF16)

    dx1 = grad_out.astype(F32) + norm_back(dn2, norms[2], xhat_two, factor_two)
    dy = dx1.astype(BF16)
    dattended = nt(dy, wo).astype(BF16)
    dq, dk, dv = call(
        attn_bwd_kernel,
        [((tok, width), BF16), ((span, width), BF16), ((span, width), BF16)],
        [VM] * 6,
        [
            pltpu.VMEM((width, tok), BF16),
            pltpu.VMEM((width, tok), BF16),
            pltpu.VMEM((width, span), BF16),
            pltpu.VMEM((width, tok), F32),
            pltpu.VMEM((span, tok), F32),
        ],
        flops=10 * span * tok * width,
    )(queries, all_keys, values, dattended, lse, starts)
    (attn_grads,) = call(
        functools.partial(pack_attn_grads_kernel, dims),
        [((n_dp * n_f,) + block, BF16)],
        [SM] + [VM] * 4,
    )(
        pos,
        tn(normed_own, dq).astype(BF16),
        tn(normed, dk).astype(BF16),
        tn(normed, dv).astype(BF16),
        tn(attended, dy).astype(BF16),
    )
    attn_grads = attn_grads.reshape((2, n_z, n_y, 2) + block)
    attn_parts = []
    for dz in list(range(1, n_z)) + [0]:
        part = add(attn_grads[0, dz], to_core(attn_grads[1, dz])).astype(BF16)
        part = add(part[:, 0], to_x(part[:, 1])).astype(BF16)
        part = add(part[0], *[to_y(part[dy_], dy_) for dy_ in range(1, n_y)]).astype(BF16)
        attn_parts.append(to_z(part, dz) if dz else part)
    grad_qkv, grad_attn_out = call(
        functools.partial(unpack_attn_kernel, n_z),
        [(qkv_weight.shape, F32), (out_weight.shape, F32)],
        [VM] * n_z,
    )(*attn_parts)

    cut = halo * tok
    dn1_halo = (nt(dk[:cut], wk) + nt(dv[:cut], wv)).astype(BF16)
    dn1 = nt(dq, wq) + nt(dk[cut:], wk) + nt(dv[cut:], wv)
    down = [(i + 2, i) for i in range(n_f - 2)]

    def back(distance):
        return dn1_halo[cut - distance * tok : cut - (distance - 1) * tok]

    carried = [None] * (halo // 2 + 1)
    for near in range(halo // 2):
        got = to_core(back(2 * near + 1)).astype(F32)
        for level, wanted in ((near, 1), (near + 1, 0)):
            term = jnp.where(c != wanted, got, 0.0)
            carried[level] = term if carried[level] is None else carried[level] + term
    coming = None
    for level in range(halo // 2, 0, -1):
        out = back(2 * level).astype(F32) + carried[level]
        if coming is not None:
            out = out + coming
        coming = lax.ppermute(out.astype(BF16), "fsdp", down).astype(F32)
    dn1 = dn1 + carried[0] + coming
    xhat_own, factor_own = xhat_one[cut:], factor_one[cut:]
    input_grad = (dx1 + norm_back(dn1, norms[0], xhat_own, factor_own)).astype(BF16)
    norm_grads = jnp.stack(
        [
            jnp.sum(dn1 * xhat_own, axis=0),
            jnp.sum(dn1, axis=0),
            jnp.sum(dn2 * xhat_two, axis=0),
            jnp.sum(dn2, axis=0),
        ]
    )
    bit = 1
    while bit < n_f:
        norm_grads = norm_grads + xor(norm_grads, "fsdp", bit)
        bit *= 2
    bit = 1
    while bit < n_dp:
        norm_grads = norm_grads + xor(norm_grads, "dp", bit)
        bit *= 2
    norm_grads = lax.dynamic_slice_in_dim(norm_grads, dp * k_rows, k_rows, axis=1)
    return (activations, input_grad, grad_qkv, grad_attn_out, grad_fc, grad_proj, norm_grads)


def solution(mesh):
    in_specs = (
        P(("dp", "fsdp"), None),
        P("dp", "fsdp"),
        P("dp", "fsdp"),
        P("dp", "fsdp"),
        P("dp", "fsdp"),
        P(None, "dp"),
        P(("dp", "fsdp"), None),
        P("dp", None, None),
        P("dp", None),
    )
    out_specs = (
        P(("dp", "fsdp"), None),
        P(("dp", "fsdp"), None),
        P("dp", "fsdp"),
        P("dp", "fsdp"),
        P("dp", "fsdp"),
        P("dp", "fsdp"),
        P(None, "dp"),
    )
    return jax.shard_map(
        per_device, mesh=mesh, in_specs=in_specs, out_specs=out_specs, check_vma=False
    )
```

```python
import functools
import math

import jax
import jax.numpy as jnp
from jax import lax
from jax.experimental import pallas as pl
from jax.experimental.pallas import tpu as pltpu
from jax.sharding import PartitionSpec as P

HEAD_DIM = 64
EPS = 1e-05
NEG = -1e30
F32 = jnp.float32
BF16 = jnp.bfloat16
VMEM_ALL = 60 * 2**20

ANY = pl.BlockSpec(memory_space=pl.ANY)
VM = pl.BlockSpec(memory_space=pltpu.VMEM)
SM = pl.BlockSpec(memory_space=pltpu.SMEM)


def call(kernel, outs, in_specs, scratch=(), flops=0, nbytes=0):
    return pl.pallas_call(
        kernel,
        out_shape=tuple(jax.ShapeDtypeStruct(s, d) for s, d in outs),
        in_specs=list(in_specs),
        out_specs=tuple(VM for _ in outs),
        scratch_shapes=list(scratch),
        compiler_params=pltpu.CompilerParams(vmem_limit_bytes=VMEM_ALL),
        cost_estimate=pl.CostEstimate(flops=flops, bytes_accessed=nbytes, transcendentals=0),
    )


def dot(a, b, ca, cb):
    return lax.dot_general(a, b, (((ca,), (cb,)), ((), ())), preferred_element_type=F32)


def nn(a, b):
    return dot(a, b, 1, 0)


def nt(a, b):
    return dot(a, b, 1, 1)


def tn(a, b):
    return dot(a, b, 0, 0)


def split_cols(lo, hi, width):
    pieces = []
    while lo < hi:
        which, start = divmod(lo, width)
        stop = min(width, start + hi - lo)
        pieces.append((which, start, stop))
        lo += stop - start
    return pieces


def pack_attn_kernel(wq_ref, wo_ref, first_ref, second_ref):
    half = wq_ref.shape[0] // 2
    row = 0
    for out_ref in (first_ref, second_ref):
        rows = out_ref.shape[0]
        vals = []
        for h in range(2):
            at = h * half + row
            vals += [wq_ref[at : at + rows, :], wo_ref[at : at + rows, :]]
        out_ref[...] = jnp.concatenate(vals, axis=1)
        row += rows


def pack_ffn_first_kernel(fc_ref, proj_ref, fct_ref, projt_ref):
    half = fc_ref.shape[1] // 2
    for h in range(2):
        fct_ref[h] = fc_ref[:, h * half : (h + 1) * half].astype(F32).T.astype(BF16)
    rows = proj_ref.shape[0] // 2
    for s in range(2):
        projt_ref[s] = proj_ref[s * rows : (s + 1) * rows, :].astype(F32).T.astype(BF16)


def pack_ffn_second_kernel(pos_ref, fct_ref, projt_ref, got_ref, send_ref, keep_ref):
    x, c = pos_ref[0], pos_ref[1]
    own = projt_ref[c]
    got = got_ref[...]
    rows, wide = own.shape
    half = wide // 2
    top = jnp.where(c == 0, own, got)
    low = jnp.where(c == 0, got, own)
    both = jnp.concatenate([top, low], axis=0)
    first, second = both[:, :half], both[:, half:]
    send_ref[...] = jnp.concatenate([fct_ref[1 - x], jnp.where(x == 0, second, first)], axis=1)
    keep_ref[...] = jnp.concatenate([fct_ref[x], jnp.where(x == 0, first, second)], axis=1)


def pack_ffn_third_kernel(pos_ref, keep_ref, got_ref, out_ref):
    x = pos_ref[0]
    keep, got = keep_ref[...], got_ref[...]
    first = jnp.where(x == 0, keep, got)
    second = jnp.where(x == 0, got, keep)
    h = keep.shape[1] // 2
    out_ref[...] = jnp.concatenate(
        [first[:, :h], second[:, :h], first[:, h:], second[:, h:]], axis=1
    )


def place(pieces, buf, sem, slots):
    copies = [
        pltpu.make_async_copy(piece, buf.at[slot], sem.at[i])
        for i, (piece, slot) in enumerate(zip(pieces, slots))
    ]
    for copy in copies:
        copy.start()
    for copy in copies:
        copy.wait()


def assemble_attn_kernel(keys, dims, pos_ref, *refs):
    n_dp, n_f, nq, no = dims
    n_z = n_f // 2
    stacks = refs[: len(keys)]
    w_refs = refs[len(keys) : len(keys) + 3]
    wo_ref, first, second, sem = refs[len(keys) + 3 :]
    dp, f = pos_ref[2], pos_ref[3]
    copies = []
    for i, (part, dy, dx, dc) in enumerate(keys):
        buf = (first, second)[part]
        for dz in range(n_z):
            slot = (dp ^ (2 * dy + dx)) * n_f + (f ^ (2 * dz + dc))
            copies.append(
                pltpu.make_async_copy(stacks[i].at[dz], buf.at[slot], sem.at[i * n_z + dz])
            )
    for copy in copies:
        copy.start()
    for copy in copies:
        copy.wait()
    half = first.shape[1] + second.shape[1]
    wide = nq + no
    width = wo_ref.shape[1]
    for d in range(n_dp):
        for h in range(2):
            row = (2 * d + h) * half
            base = h * wide
            for buf in (first, second):
                rows = buf.shape[1]
                for part in range(3):
                    vals = [
                        buf[d * n_f + which][:, base + lo : base + hi]
                        for which, lo, hi in split_cols(part * width, (part + 1) * width, nq)
                    ]
                    w_refs[part][row : row + rows, :] = jnp.concatenate(vals, axis=1)
                wo_ref[row : row + rows, :] = jnp.concatenate(
                    [buf[d * n_f + g][:, base + nq : base + wide] for g in range(n_f)], axis=1
                )
                row += rows


def assemble_ffn_kernel(keys, dims, pos_ref, *refs):
    n_y, n_z = dims
    pieces = refs[: len(keys)]
    fct_ref, projt_ref, buf, sem = refs[len(keys) :]
    dp, f = pos_ref[2], pos_ref[3]
    slots = [((dp >> 1) ^ dy) * n_z + ((f >> 1) ^ dz) for dy, dz in keys]
    place(pieces, buf, sem, slots)
    rows, wide = buf.shape[1:]
    half = wide // 2
    for z in range(n_z):
        vals = [buf[y * n_z + z] for y in range(n_y)]
        fct_ref[z * rows : (z + 1) * rows, :] = jnp.concatenate(
            [v[:, :half] for v in vals], axis=1
        )
        projt_ref[z * rows : (z + 1) * rows, :] = jnp.concatenate(
            [v[:, half:] for v in vals], axis=1
        )


def pack_attn_grads_kernel(dims, pos_ref, gq_ref, gk_ref, gv_ref, go_ref, first_ref, second_ref):
    n_dp, n_f, nq, no = dims
    n_y, n_z = n_dp // 2, n_f // 2
    dp, f = pos_ref[2], pos_ref[3]
    parts = (gq_ref, gk_ref, gv_ref)
    width = go_ref.shape[1]
    half = first_ref.shape[1] + second_ref.shape[1]
    for d in range(n_dp):
        for g in range(n_f):
            rd, rf = dp ^ d, f ^ g
            dy, dx, dz, dc = rd >> 1, rd & 1, rf >> 1, rf & 1
            slots = (((dc * 2 + dx) * n_y + dy) * n_z + dz, ((dc * n_y + dy) * 2 + dx) * n_z + dz)
            start = 0
            for out_ref, slot in zip((first_ref, second_ref), slots):
                rows = out_ref.shape[1]
                vals = []
                for h in range(2):
                    row = (2 * d + h) * half + start
                    for which, lo, hi in split_cols(g * nq, (g + 1) * nq, width):
                        vals.append(parts[which][row : row + rows, lo:hi])
                    vals.append(go_ref[row : row + rows, g * no : (g + 1) * no])
                out_ref[slot] = jnp.concatenate(vals, axis=1)
                start += rows


def pack_ffn_grads_kernel(dims, pos_ref, gfc_ref, gproj_ref, out_ref):
    n_y, n_z = dims
    dp, f = pos_ref[2], pos_ref[3]
    rows, wide = out_ref.shape[1:]
    half = wide // 2
    for y in range(n_y):
        for z in range(n_z):
            slot = ((dp >> 1) ^ y) * n_z + ((f >> 1) ^ z)
            out_ref[slot] = jnp.concatenate(
                [
                    gfc_ref[z * rows : (z + 1) * rows, y * half : (y + 1) * half],
                    gproj_ref[z * rows : (z + 1) * rows, y * half : (y + 1) * half],
                ],
                axis=1,
            )


def total(refs):
    acc = refs[0][...].astype(F32)
    for ref in refs[1:]:
        acc = acc + ref[...].astype(F32)
    return acc


def unpack_attn_kernel(count, *refs):
    gq_ref, go_ref = refs[2 * count :]
    half = gq_ref.shape[0] // 2
    nq, no = gq_ref.shape[1], go_ref.shape[1]
    start = 0
    for part in range(2):
        summed = total(refs[part * count : (part + 1) * count])
        rows = summed.shape[0]
        for h in range(2):
            base = h * (nq + no)
            row = h * half + start
            gq_ref[row : row + rows, :] = summed[:, base : base + nq]
            go_ref[row : row + rows, :] = summed[:, base + nq : base + nq + no]
        start += rows


def unpack_ffn_first_kernel(count, pos_ref, *refs):
    send_ref, keep_ref = refs[count:]
    x = pos_ref[0]
    summed = total(refs[:count])
    q = summed.shape[1] // 4
    first = jnp.concatenate([summed[:, :q], summed[:, 2 * q : 3 * q]], axis=1)
    second = jnp.concatenate([summed[:, q : 2 * q], summed[:, 3 * q :]], axis=1)
    send_ref[...] = jnp.where(x == 0, second, first).astype(BF16)
    keep_ref[...] = jnp.where(x == 0, first, second)


def unpack_ffn_second_kernel(pos_ref, keep_ref, got_ref, gfc_ref, send_ref, hold_ref):
    x, c = pos_ref[0], pos_ref[1]
    keep, got = keep_ref[...], got_ref[...].astype(F32)
    h = keep.shape[1] // 2
    rows = keep.shape[0] // 2
    first = jnp.where(x == 0, keep, got)
    second = jnp.where(x == 0, got, keep)
    gfc_ref[...] = jnp.concatenate([first[:, :h].T, second[:, :h].T], axis=1)
    both = jnp.concatenate([first[:, h:], second[:, h:]], axis=1)
    top, low = both[:rows, :], both[rows:, :]
    send_ref[...] = jnp.where(c == 0, low, top).astype(BF16)
    hold_ref[...] = jnp.where(c == 0, top, low)


def unpack_ffn_third_kernel(pos_ref, hold_ref, got_ref, gproj_ref):
    c = pos_ref[1]
    hold, got = hold_ref[...], got_ref[...].astype(F32)
    rows = hold.shape[1]
    gproj_ref[:rows, :] = jnp.where(c == 0, hold, got).T
    gproj_ref[rows:, :] = jnp.where(c == 0, got, hold).T


def fill_bias(start_ref, bias_ref):
    keys, rows = bias_ref.shape
    key_ids = lax.broadcasted_iota(jnp.int32, (keys, rows), 0)
    row_ids = lax.broadcasted_iota(jnp.int32, (keys, rows), 1) + (keys - rows)
    allowed = (key_ids >= start_ref[...]) & (key_ids <= row_ids)
    bias_ref[...] = jnp.where(allowed, 0.0, NEG)


def head_slices(width):
    pairs = width // (2 * HEAD_DIM)
    return pairs, width - pairs * 2 * HEAD_DIM


def attn_fwd_kernel(q_ref, k_ref, v_ref, start_ref, o_ref, lse_ref, qt, vt, ot, bias):
    width = q_ref.shape[1]
    fill_bias(start_ref, bias)
    qt[...] = (q_ref[...].astype(F32) * HEAD_DIM ** (-0.5)).T.astype(BF16)
    vt[...] = v_ref[...].astype(F32).T.astype(BF16)
    pairs, rest = head_slices(width)

    def one(keys, queries, values, row, head):
        scores = nn(keys, queries) + bias[...]
        peak = jnp.max(scores, axis=0, keepdims=True)
        terms = jnp.exp(scores - peak)
        summed = jnp.sum(terms, axis=0, keepdims=True)
        ot[pl.ds(row, HEAD_DIM), :] = nn(values, terms.astype(BF16)) / summed
        lse_ref[pl.ds(head, 1), :] = peak + jnp.log(summed)

    def pair(p, _):
        at = pl.multiple_of(p * 128, 128)
        keys = k_ref[:, pl.ds(at, 128)]
        queries = qt[pl.ds(at, 128), :]
        rows = lax.broadcasted_iota(jnp.int32, queries.shape, 0)
        for h in range(2):
            row = pl.multiple_of(at + h * HEAD_DIM, HEAD_DIM)
            one(
                keys,
                jnp.where((rows < HEAD_DIM) == (h == 0), queries, jnp.zeros_like(queries)),
                vt[pl.ds(row, HEAD_DIM), :],
                row,
                2 * p + h,
            )
        return 0

    lax.fori_loop(0, pairs, pair, 0)
    if rest:
        at = pairs * 128
        one(k_ref[:, at:], qt[at:, :], vt[at:, :], at, 2 * pairs)
    o_ref[...] = ot[...].T.astype(BF16)


def attn_bwd_kernel(
    q_ref, k_ref, v_ref, do_ref, lse_ref, start_ref, dq_ref, dk_ref, dv_ref, qt, dot_s, kt, dqt, bias
):
    width = q_ref.shape[1]
    scale = HEAD_DIM ** (-0.5)
    fill_bias(start_ref, bias)
    qt[...] = (q_ref[...].astype(F32) * scale).T.astype(BF16)
    dot_s[...] = do_ref[...].astype(F32).T.astype(BF16)
    kt[...] = k_ref[...].astype(F32).T.astype(BF16)
    pairs, rest = head_slices(width)

    def one(keys, values, queries_t, douts_t, keys_t, queries, douts, row, head):
        scores = nn(keys, queries_t) + bias[...]
        probs = jnp.exp(scores - lse_ref[pl.ds(head, 1), :])
        dprobs = nn(values, douts_t)
        delta = jnp.sum(probs * dprobs, axis=0, keepdims=True)
        dscores = (probs * (dprobs - delta)).astype(BF16)
        dqt[pl.ds(row, HEAD_DIM), :] = nn(keys_t, dscores)
        return nn(dscores, queries), nn(probs.astype(BF16), douts)

    def scaled(values):
        return (values.astype(F32) * scale).astype(BF16)

    def pair(p, _):
        at = pl.multiple_of(p * 128, 128)
        keys = k_ref[:, pl.ds(at, 128)]
        values = v_ref[:, pl.ds(at, 128)]
        queries = scaled(q_ref[:, pl.ds(at, 128)])
        douts = do_ref[:, pl.ds(at, 128)]
        queries_t = qt[pl.ds(at, 128), :]
        douts_t = dot_s[pl.ds(at, 128), :]
        rows = lax.broadcasted_iota(jnp.int32, queries_t.shape, 0)
        lanes = lax.broadcasted_iota(jnp.int32, queries.shape, 1)
        dk_sum = dv_sum = None
        for h in range(2):
            row = pl.multiple_of(at + h * HEAD_DIM, HEAD_DIM)
            in_rows = (rows < HEAD_DIM) == (h == 0)
            in_lanes = (lanes < HEAD_DIM) == (h == 0)
            zero_t, zero = jnp.zeros_like(queries_t), jnp.zeros_like(queries)
            dk_part, dv_part = one(
                keys,
                values,
                jnp.where(in_rows, queries_t, zero_t),
                jnp.where(in_rows, douts_t, zero_t),
                kt[pl.ds(row, HEAD_DIM), :],
                jnp.where(in_lanes, queries, zero),
                jnp.where(in_lanes, douts, zero),
                row,
                2 * p + h,
            )
            dk_sum = dk_part if h == 0 else dk_sum + dk_part
            dv_sum = dv_part if h == 0 else dv_sum + dv_part
        dk_ref[:, pl.ds(at, 128)] = dk_sum.astype(BF16)
        dv_ref[:, pl.ds(at, 128)] = dv_sum.astype(BF16)
        return 0

    lax.fori_loop(0, pairs, pair, 0)
    if rest:
        at = pairs * 128
        dk_part, dv_part = one(
            k_ref[:, at:],
            v_ref[:, at:],
            qt[at:, :],
            dot_s[at:, :],
            kt[at:, :],
            scaled(q_ref[:, at:]),
            do_ref[:, at:],
            at,
            2 * pairs,
        )
        dk_ref[:, at:] = dk_part.astype(BF16)
        dv_ref[:, at:] = dv_part.astype(BF16)
    dq_ref[...] = (dqt[...].T * scale).astype(BF16)


def xhat_of(values):
    center = jnp.mean(values, axis=-1, keepdims=True)
    centered = values - center
    variance = jnp.mean(centered * centered, axis=-1, keepdims=True)
    factor = lax.rsqrt(variance + EPS)
    return centered * factor, factor


def norm_back(grads, gain, xhat, factor):
    e = grads * gain
    return factor * (
        e
        - jnp.mean(e, axis=-1, keepdims=True)
        - xhat * jnp.mean(e * xhat, axis=-1, keepdims=True)
    )


def add(*terms):
    acc = terms[0].astype(F32)
    for term in terms[1:]:
        acc = acc + term.astype(F32)
    return acc


def segment_starts(dealt_lengths, seq_order, first_row, rows):
    lengths = dealt_lengths[0].reshape(-1)
    order = seq_order[0]
    count = lengths.shape[0]
    arrival = jnp.arange(count, dtype=jnp.int32)
    before = (order[:, None] < arrival[None, :]).astype(jnp.int32)
    begins = jnp.sum(before * lengths[:, None], axis=0)
    ids = first_row + jnp.arange(rows, dtype=jnp.int32)
    reached = begins[:, None] <= ids[None, :]
    return jnp.max(jnp.where(reached, begins[:, None], 0), axis=0)


class Clock:
    def __init__(self):
        self.fence = ()

    def __call__(self, value):
        if not self.fence:
            return value
        return lax.optimization_barrier((value, self.fence))[0]

    def tick(self, *done):
        self.fence = tuple(done)


def per_device(
    tokens,
    qkv_weight,
    out_weight,
    fc_weight,
    proj_weight,
    norm_params,
    grad_out,
    dealt_lengths,
    seq_order,
):
    n_dp, n_f = lax.axis_size("dp"), lax.axis_size("fsdp")
    n_y, n_z = n_dp // 2, n_f // 2
    dp, f = lax.axis_index("dp"), lax.axis_index("fsdp")
    x, c = dp & 1, f & 1
    pos = jnp.stack([x, c, dp, f]).astype(jnp.int32)
    tok, width = tokens.shape
    seq_longest = n_f * tok // dealt_lengths.shape[1] // 2
    halo = -(-seq_longest // tok)
    halo += halo % 2

    def xor(value, axis, bits):
        size = n_dp if axis == "dp" else n_f
        return lax.ppermute(value, axis, [(i, i ^ bits) for i in range(size)])

    def to_core(value):
        return xor(value, "fsdp", 1)

    def to_x(value):
        return xor(value, "dp", 1)

    def to_y(value, k):
        return xor(value, "dp", 2 * k)

    def to_z(value, k):
        return xor(value, "fsdp", 2 * k)

    now = Clock()

    k_rows, nq = qkv_weight.shape
    no = out_weight.shape[1]
    block = (k_rows // 2, 2 * (nq + no))
    first_rows = (block[0] // 2 + 7) // 8 * 8
    cuts = (first_rows, block[0] - first_rows)
    own_first, own_second = call(
        pack_attn_kernel, [((rows, block[1]), BF16) for rows in cuts], [VM, VM]
    )(qkv_weight, out_weight)
    ff_half = fc_weight.shape[1] // 2
    sub = proj_weight.shape[0] // 4

    others_z, others_y = range(1, n_z), range(1, n_y)
    firsts = [own_first] + [to_z(own_first, dz) for dz in others_z]
    fct, projt = call(
        pack_ffn_first_kernel,
        [((2, ff_half, k_rows), BF16), ((2, no, 2 * sub), BF16)],
        [VM, VM],
    )(fc_weight, proj_weight)
    got = to_core(lax.dynamic_index_in_dim(projt, 1 - c, keepdims=False))
    send, keep = call(
        pack_ffn_second_kernel,
        [((ff_half, k_rows + sub), BF16)] * 2,
        [SM, VM, VM, VM],
    )(pos, fct, projt, got)
    got = to_x(send)
    now.tick(*firsts, got)

    stack = {(0, 0, 0): jnp.stack(firsts)}
    own_second = now(own_second)
    seconds = [own_second] + [to_z(own_second, dz) for dz in others_z]
    for dy in others_y:
        stack[0, dy, 0] = to_y(stack[0, 0, 0], dy)
    stack[0, 0, 1] = to_x(stack[0, 0, 0])
    (own_ffn,) = call(
        pack_ffn_third_kernel, [((ff_half, 2 * (k_rows + sub)), BF16)], [SM, VM, VM]
    )(pos, keep, got)
    now.tick(*seconds, *stack.values(), own_ffn)

    stack[1, 0, 0] = jnp.stack(seconds)
    stack[1, 0, 1] = to_x(stack[1, 0, 0])
    for dy in others_y:
        stack[1, dy, 0] = to_y(stack[1, 0, 0], dy)
    up = [(i, i + 2) for i in range(n_f - 2)]
    even = [now(tokens)]
    for _ in range(halo // 2):
        even.append(lax.ppermute(even[-1], "fsdp", up))
    norm_pieces = [norm_params] + [xor(now(norm_params), "dp", r) for r in range(1, n_dp)]
    attn = {}

    def cross(*keys):
        for key in keys:
            value = now(stack[key])
            attn[key + (0,)] = stack[key]
            attn[key + (1,)] = to_core(value)

    cross((0, 0, 0), *[(0, dy, 0) for dy in others_y])
    now.tick(stack[1, 0, 1], *[stack[1, dy, 0] for dy in others_y], even[-1], *attn.values())

    for dy in others_y:
        stack[0, dy, 1] = to_x(now(stack[0, dy, 0]))
        stack[1, dy, 1] = to_y(now(stack[1, 0, 1]), dy)
    ffn = {(0, 0): own_ffn}
    ffn[0, 1] = to_z(now(own_ffn), 1)
    rows_before = []
    for distance in range(1, halo + 1):
        if distance % 2:
            near = distance // 2
            rows_before.append(to_core(now(jnp.where(c == 0, even[near], even[near + 1]))))
        else:
            rows_before.append(even[distance // 2])
    x_rows = jnp.concatenate(rows_before[::-1] + [tokens], axis=0)
    cross((0, 0, 1), (1, 0, 0), (1, 0, 1), *[(1, dy, 0) for dy in others_y])
    norms = jnp.concatenate(
        [
            sum(
                jnp.where((dp ^ r) == j, piece.astype(F32), 0.0)
                for r, piece in enumerate(norm_pieces)
            )
            for j in range(n_dp)
        ],
        axis=1,
    )
    xhat_one, factor_one = xhat_of(x_rows.astype(F32))
    normed = (xhat_one * norms[0] + norms[1]).astype(BF16)
    now.tick(*attn.values(), ffn[0, 1], *stack.values(), normed)

    cross(*[(part, dy, 1) for dy in others_y for part in range(2)])
    for dz in others_z[1:]:
        ffn[0, dz] = to_z(now(own_ffn), dz)
    for dy in others_y:
        ffn[dy, 0] = to_y(now(own_ffn), dy)
    gz_far = to_x(now(grad_out))
    keys = sorted(attn)
    square = ((width, width), BF16)
    dims = (n_dp, n_f, nq, no)
    wq, wk, wv, wo = call(
        functools.partial(assemble_attn_kernel, keys, dims),
        [square] * 4,
        [SM] + [ANY] * len(keys),
        [pltpu.VMEM((n_dp * n_f, rows, block[1]), BF16) for rows in cuts]
        + [pltpu.SemaphoreType.DMA((len(keys) * n_z,))],
    )(pos, *[attn[key] for key in keys])
    normed_own = normed[halo * tok :]
    queries = nn(normed_own, wq).astype(BF16)
    all_keys = nn(normed, wk).astype(BF16)
    values = nn(normed, wv).astype(BF16)
    now.tick(gz_far, queries, all_keys, values, *[ffn[dy, 0] for dy in others_y])

    for dy in others_y:
        ffn[dy, 1] = to_y(now(ffn[0, 1]), dy)
    gz_rows = [grad_out, to_core(now(grad_out)), gz_far, to_core(now(gz_far))]
    gz_rows = jnp.concatenate(gz_rows, axis=0)
    span = (halo + 1) * tok
    starts = segment_starts(dealt_lengths, seq_order, f * tok, tok) - (f - halo) * tok
    starts = starts.reshape(1, tok).astype(jnp.int32)
    heads = width // HEAD_DIM
    attended, lse = call(
        attn_fwd_kernel,
        [((tok, width), BF16), ((heads, tok), F32)],
        [VM] * 4,
        [
            pltpu.VMEM((width, tok), BF16),
            pltpu.VMEM((width, span), BF16),
            pltpu.VMEM((width, tok), F32),
            pltpu.VMEM((span, tok), F32),
        ],
    )(now(queries), all_keys, values, starts)
    middle = tokens.astype(F32) + nn(attended, wo)
    xhat_two, factor_two = xhat_of(middle)
    normed_two = (xhat_two * norms[2] + norms[3]).astype(BF16)
    now.tick(normed_two, gz_rows, *[ffn[dy, 1] for dy in others_y], *[ffn[0, dz] for dz in others_z])

    n2_far = to_x(normed_two)
    n2_sib = to_core(normed_two)
    for dz in others_z[1:-1]:
        for dy in others_y:
            ffn[dy, dz] = to_y(now(ffn[0, dz]), dy)
    now.tick(n2_far, n2_sib, *ffn.values())
    for dy in others_y:
        ffn[dy, n_z - 1] = to_y(now(ffn[0, n_z - 1]), dy)
    n2_rows = [normed_two, n2_sib, n2_far, to_core(now(n2_far))]
    n2_rows = jnp.concatenate(n2_rows, axis=0)

    ffn_keys = sorted(ffn)
    fct_full, projt_full = call(
        functools.partial(assemble_ffn_kernel, ffn_keys, (n_y, n_z)),
        [((n_z * ff_half, n_y * 2 * k_rows), BF16), ((n_z * 2 * no, n_y * 2 * sub), BF16)],
        [SM] + [ANY] * len(ffn_keys),
        [
            pltpu.VMEM((len(ffn_keys),) + own_ffn.shape, BF16),
            pltpu.SemaphoreType.DMA((len(ffn_keys),)),
        ],
    )(pos, *[ffn[key] for key in ffn_keys])
    hidden = nt(n2_rows, fct_full)
    cdf = 0.5 * (1.0 + lax.erf(hidden * math.sqrt(0.5)))
    slope = cdf + hidden * jnp.exp(-0.5 * hidden * hidden) * (1.0 / math.sqrt(2.0 * math.pi))
    activated = (hidden * cdf).astype(BF16)
    dhidden = (nn(gz_rows, projt_full) * slope).astype(BF16)
    dn2_parts = nn(dhidden, fct_full).astype(BF16)

    def members(parts):
        return [parts[i * tok : (i + 1) * tok] for i in range(4)]

    own, sib, far, far_sib = members(dn2_parts)
    far = add(far, to_core(far_sib)).astype(BF16)
    now.tick(far)
    dn2_far = to_x(far)
    dn2_sib = to_core(now(sib))
    dhidden, activated = now((dhidden, activated))
    grad_fct = tn(dhidden, n2_rows).astype(BF16)
    grad_projt = tn(gz_rows, activated).astype(BF16)
    (ffn_grads,) = call(
        functools.partial(pack_ffn_grads_kernel, (n_y, n_z)),
        [((n_y * n_z,) + own_ffn.shape, BF16)],
        [SM, VM, VM],
    )(pos, grad_fct, grad_projt)
    dn2 = add(own, dn2_sib, dn2_far)
    now.tick(ffn_grads, dn2)

    def ffn_over_y(dz):
        return add(
            now(ffn_grads[dz]),
            *[to_y(now(ffn_grads[dy * n_z + dz]), dy) for dy in others_y],
        ).astype(BF16)

    ffn_parts = [ffn_over_y(1)]
    dx1 = grad_out.astype(F32) + norm_back(now(dn2), norms[2], xhat_two, factor_two)
    dy_low = dx1.astype(BF16)
    dattended = nt(dy_low, wo).astype(BF16)
    act_own, act_sib, act_far, act_far_sib = members(
        nt(now(activated), projt_full).astype(BF16)
    )
    act_sib = to_core(act_sib)
    act_far = add(act_far, to_core(act_far_sib)).astype(BF16)
    now.tick(dattended, act_far, act_sib, *ffn_parts)

    act_far = to_x(act_far)
    ffn_parts[0] = to_z(ffn_parts[0], 1)
    ffn_parts.append(ffn_over_y(2))
    dq, dk, dv = call(
        attn_bwd_kernel,
        [((tok, width), BF16), ((span, width), BF16), ((span, width), BF16)],
        [VM] * 6,
        [
            pltpu.VMEM((width, tok), BF16),
            pltpu.VMEM((width, tok), BF16),
            pltpu.VMEM((width, span), BF16),
            pltpu.VMEM((width, tok), F32),
            pltpu.VMEM((span, tok), F32),
        ],
    )(queries, all_keys, values, now(dattended), lse, starts)
    now.tick(dq, dk, dv, act_far, *ffn_parts)

    ffn_parts[1] = to_z(ffn_parts[1], 2)
    ffn_parts += [ffn_over_y(dz) for dz in range(3, n_z)]
    dq, dk, dv = now((dq, dk, dv))
    grads = [
        tn(normed_own, dq).astype(BF16),
        tn(normed, dk).astype(BF16),
        tn(normed, dv).astype(BF16),
        tn(attended, dy_low).astype(BF16),
    ]
    now.tick(*grads, *ffn_parts)
    ffn_parts[2:] = [to_z(now(part), dz) for dz, part in enumerate(ffn_parts[2:], 3)]
    ffn_parts.append(ffn_over_y(0))
    grads_first, grads_second = call(
        functools.partial(pack_attn_grads_kernel, dims),
        [((n_dp * n_f, rows, block[1]), BF16) for rows in cuts],
        [SM] + [VM] * 4,
    )(pos, *now(grads))
    now.tick(grads_first, grads_second, *ffn_parts)

    grads_first = grads_first.reshape((2, 2, n_y, n_z, cuts[0], block[1]))
    grads_second = grads_second.reshape((2, n_y, 2, n_z, cuts[1], block[1]))
    activations = (middle + add(act_own, act_sib, act_far)).astype(BF16)
    from_core = {}

    def core_swap(part, outer):
        value = (grads_first, grads_second)[part][1, outer]
        from_core[part, outer] = to_core(now(value))

    def core_sum(part, outer, inner):
        own = (grads_first, grads_second)[part][0, outer, inner]
        return add(own, from_core[part, outer][inner])

    core_swap(0, 1)
    for dy in others_y:
        core_swap(1, dy)
    now.tick(*from_core.values())

    first_x, first_y, second_y = {}, {}, {}
    for dy in others_y:
        first_x[dy] = to_x(core_sum(0, 1, dy).astype(BF16))
        second_y[dy, 1] = to_y(core_sum(1, dy, 1).astype(BF16), dy)
    core_swap(0, 0)
    core_swap(1, 0)
    send, keep = call(
        functools.partial(unpack_ffn_first_kernel, n_z),
        [((ff_half, k_rows + sub), BF16), ((ff_half, k_rows + sub), F32)],
        [SM] + [VM] * n_z,
    )(pos, *now(ffn_parts))
    cut = halo * tok
    dk, dv, dq = now((dk, dv, dq))
    dn1_halo = (nt(dk[:cut], wk) + nt(dv[:cut], wv)).astype(BF16)
    dn1 = nt(dq, wq) + nt(dk[cut:], wk) + nt(dv[cut:], wv)

    def back(distance):
        return dn1_halo[cut - distance * tok : cut - (distance - 1) * tok]

    carried = [None] * (halo // 2 + 1)
    for near in range(halo // 2):
        got = to_core(back(2 * near + 1)).astype(F32)
        for level, wanted in ((near, 1), (near + 1, 0)):
            term = jnp.where(c != wanted, got, 0.0)
            carried[level] = term if carried[level] is None else carried[level] + term
    outgoing = [back(2 * level).astype(F32) + carried[level] for level in range(1, halo // 2 + 1)]
    now.tick(*first_x.values(), *second_y.values(), *from_core.values(), outgoing, dn1, keep)

    first_x[0] = to_x(core_sum(0, 1, 0).astype(BF16))
    for dy in others_y:
        kept = add(core_sum(0, 0, dy), first_x[dy]).astype(BF16)
        first_y[dy] = to_y(now(kept), dy)
    down = [(i + 2, i) for i in range(n_f - 2)]
    coming = None
    for level in range(halo // 2, 0, -1):
        out = now(outgoing[level - 1])
        if coming is not None:
            out = out + coming
        coming = lax.ppermute(out.astype(BF16), "fsdp", down).astype(F32)
    now.tick(*first_x.values(), *first_y.values(), coming)

    got = to_x(now(send))
    first_sum = add(core_sum(0, 0, 0), first_x[0], *first_y.values()).astype(BF16)
    first_parts = [first_sum[0]] + [to_z(now(first_sum[dz]), dz) for dz in others_z]
    second_far = add(
        core_sum(1, 0, 1), *[second_y[dy, 1] for dy in others_y]
    ).astype(BF16)
    second_x = to_x(now(second_far))
    for dy in others_y:
        second_y[dy, 0] = to_y(now(core_sum(1, dy, 0).astype(BF16)), dy)
    dn1 = now(dn1) + carried[0] + coming
    xhat_own, factor_own = xhat_one[cut:], factor_one[cut:]
    input_grad = (dx1 + norm_back(dn1, norms[0], xhat_own, factor_own)).astype(BF16)
    norm_grads = jnp.stack(
        [
            jnp.sum(dn1 * xhat_own, axis=0),
            jnp.sum(dn1, axis=0),
            jnp.sum(dn2 * xhat_two, axis=0),
            jnp.sum(dn2, axis=0),
        ]
    )
    grad_fc, send, hold = call(
        unpack_ffn_second_kernel,
        [(fc_weight.shape, F32), ((no, 2 * sub), BF16), ((no, 2 * sub), F32)],
        [SM, VM, VM],
    )(pos, keep, got)
    now.tick(*first_parts, second_x, *second_y.values(), norm_grads, send)

    second_sum = add(
        core_sum(1, 0, 0), second_x, *[second_y[dy, 0] for dy in others_y]
    ).astype(BF16)
    second_parts = [second_sum[0]] + [to_z(now(second_sum[dz]), dz) for dz in others_z]
    (grad_proj,) = call(unpack_ffn_third_kernel, [(proj_weight.shape, F32)], [SM, VM, VM])(
        pos, hold, to_core(now(send))
    )
    norm_grads = now(norm_grads)
    bit = 1
    while bit < n_f:
        norm_grads = norm_grads + xor(norm_grads, "fsdp", bit)
        bit *= 2
    bit = 1
    while bit < n_dp:
        norm_grads = norm_grads + xor(norm_grads, "dp", bit)
        bit *= 2
    norm_grads = lax.dynamic_slice_in_dim(norm_grads, dp * k_rows, k_rows, axis=1)
    grad_qkv, grad_attn_out = call(
        functools.partial(unpack_attn_kernel, n_z),
        [(qkv_weight.shape, F32), (out_weight.shape, F32)],
        [VM] * (2 * n_z),
    )(*first_parts, *second_parts)
    return (activations, input_grad, grad_qkv, grad_attn_out, grad_fc, grad_proj, norm_grads)


def solution(mesh):
    in_specs = (
        P(("dp", "fsdp"), None),
        P("dp", "fsdp"),
        P("dp", "fsdp"),
        P("dp", "fsdp"),
        P("dp", "fsdp"),
        P(None, "dp"),
        P(("dp", "fsdp"), None),
        P("dp", None, None),
        P("dp", None),
    )
    out_specs = (
        P(("dp", "fsdp"), None),
        P(("dp", "fsdp"), None),
        P("dp", "fsdp"),
        P("dp", "fsdp"),
        P("dp", "fsdp"),
        P("dp", "fsdp"),
        P(None, "dp"),
    )
    return jax.shard_map(
        per_device, mesh=mesh, in_specs=in_specs, out_specs=out_specs, check_vma=False
    )
```

```python
import functools
import math

import jax
import jax.numpy as jnp
from jax import lax
from jax.experimental import pallas as pl
from jax.experimental.pallas import tpu as pltpu
from jax.sharding import PartitionSpec as P

HEAD_DIM = 64
EPS = 1e-05
NEG = -1e30
F32 = jnp.float32
BF16 = jnp.bfloat16
VMEM_ALL = 60 * 2**20

ANY = pl.BlockSpec(memory_space=pl.ANY)
VM = pl.BlockSpec(memory_space=pltpu.VMEM)
SM = pl.BlockSpec(memory_space=pltpu.SMEM)


def call(kernel, outs, in_specs, scratch=()):
    return pl.pallas_call(
        kernel,
        name=getattr(kernel, "func", kernel).__name__,
        out_shape=tuple(jax.ShapeDtypeStruct(s, d) for s, d in outs),
        in_specs=list(in_specs),
        out_specs=tuple(VM for _ in outs),
        scratch_shapes=list(scratch),
        compiler_params=pltpu.CompilerParams(vmem_limit_bytes=VMEM_ALL),
        cost_estimate=pl.CostEstimate(flops=0, bytes_accessed=0, transcendentals=0),
    )


def dot(a, b, ca, cb):
    return lax.dot_general(a, b, (((ca,), (cb,)), ((), ())), preferred_element_type=F32)


def nn(a, b):
    return dot(a, b, 1, 0)


def nt(a, b):
    return dot(a, b, 1, 1)


def tn(a, b):
    return dot(a, b, 0, 0)


def repeat(count, looped, body):
    if not looped:
        for i in range(count):
            body(i)
        return

    def step(i, carry):
        body(i)
        return carry

    lax.fori_loop(0, count, step, 0)


def split_cols(lo, hi, width):
    pieces = []
    while lo < hi:
        which, start = divmod(lo, width)
        stop = min(width, start + hi - lo)
        pieces.append((which, start, stop))
        lo += stop - start
    return pieces


def pack_attn_kernel(wq_ref, wo_ref, first_ref, second_ref):
    half = wq_ref.shape[0] // 2
    rows = first_ref.shape[0]
    wo = wo_ref[...].astype(F32).T.astype(BF16)
    for out_ref, row in ((first_ref, 0), (second_ref, half - rows)):
        vals = []
        for h in range(2):
            at = h * half + row
            vals += [wq_ref[at : at + rows, :], wo[at : at + rows, :]]
        out_ref[...] = jnp.concatenate(vals, axis=1)


def pack_ffn_first_kernel(pos_ref, fc_ref, projt_ref, send_ref, keep_ref):
    x = pos_ref[0]
    half = fc_ref.shape[1] // 2
    sub = projt_ref.shape[1] // 4
    sides = []
    for h in range(2):
        fct = fc_ref[:, h * half : (h + 1) * half].astype(F32).T
        projt = [
            projt_ref[:, (2 * s + h) * sub : (2 * s + h + 1) * sub].astype(F32) for s in range(2)
        ]
        sides.append(jnp.concatenate([fct, jnp.concatenate(projt, axis=0)], axis=1))
    send_ref[...] = jnp.where(x == 0, sides[1], sides[0]).astype(BF16)
    keep_ref[...] = jnp.where(x == 0, sides[0], sides[1]).astype(BF16)


def pack_ffn_second_kernel(pos_ref, keep_ref, got_ref, fct_ref, send_ref, hold_ref):
    x, c = pos_ref[0], pos_ref[1]
    keep, got = keep_ref[...], got_ref[...]
    first = jnp.where(x == 0, keep, got)
    second = jnp.where(x == 0, got, keep)
    k = fct_ref.shape[1] // 2
    rows = send_ref.shape[0]
    fct_ref[...] = jnp.concatenate([first[:, :k], second[:, :k]], axis=1)
    projt = jnp.concatenate([first[:, k:], second[:, k:]], axis=1)
    top, low = projt[:rows, :], projt[rows:, :]
    send_ref[...] = jnp.where(c == 0, low, top)
    hold_ref[...] = jnp.where(c == 0, top, low)


def pack_ffn_third_kernel(pos_ref, fct_ref, hold_ref, got_ref, out_ref):
    c = pos_ref[1]
    hold, got = hold_ref[...], got_ref[...]
    top = jnp.where(c == 0, hold, got)
    low = jnp.where(c == 0, got, hold)
    projt = jnp.concatenate([top, low], axis=0)
    out_ref[...] = jnp.concatenate([fct_ref[...], projt], axis=1)


def place(pieces, buf, sem, slots):
    copies = [
        pltpu.make_async_copy(piece, buf.at[slot], sem.at[i])
        for i, (piece, slot) in enumerate(zip(pieces, slots))
    ]
    for copy in copies:
        copy.start()
    for copy in copies:
        copy.wait()


def assemble_attn_kernel(stacks, dims, pos_ref, *refs):
    n_dp, n_f, nq, no = dims
    n_z = n_f // 2
    ins = refs[: len(stacks)]
    w_refs = refs[len(stacks) : len(stacks) + 3]
    wo_ref, buf, sem = refs[len(stacks) + 3 :]
    dp, f = pos_ref[2], pos_ref[3]
    copies = []
    for ref, groups in zip(ins, stacks):
        for i, (part, dy, dx, dc) in enumerate(groups):
            for dz in range(n_z):
                slot = (dp ^ (2 * dy + dx)) * n_f + (f ^ (2 * dz + dc))
                copies.append(
                    pltpu.make_async_copy(
                        ref.at[i * n_z + dz], buf.at[part, slot], sem.at[len(copies)]
                    )
                )
    for copy in copies:
        copy.start()
    for copy in copies:
        copy.wait()
    rows = buf.shape[2]
    wide = nq + no
    width = wo_ref.shape[1]
    half = width // n_dp // 2
    for d in range(n_dp):
        for h in range(2):
            base = h * wide
            for part, skip in ((0, 0), (1, 2 * rows - half)):
                row = (2 * d + h) * half + part * rows
                stop = row + rows - skip
                for third in range(3):
                    vals = [
                        buf[part, d * n_f + which][skip:, base + lo : base + hi]
                        for which, lo, hi in split_cols(third * width, (third + 1) * width, nq)
                    ]
                    w_refs[third][row:stop, :] = jnp.concatenate(vals, axis=1)
                wo_ref[row:stop, :] = jnp.concatenate(
                    [
                        buf[part, d * n_f + g][skip:, base + nq : base + wide]
                        for g in range(n_f)
                    ],
                    axis=1,
                )


def assemble_ffn_kernel(keys, dims, pos_ref, *refs):
    n_y, n_z = dims
    pieces = refs[: len(keys)]
    fct_ref, projt_ref, buf, sem = refs[len(keys) :]
    dp, f = pos_ref[2], pos_ref[3]
    slots = [((dp >> 1) ^ dy) * n_z + ((f >> 1) ^ dz) for dy, dz in keys]
    place(pieces, buf, sem, slots)
    rows, wide = buf.shape[1:]
    half = wide // 2
    for z in range(n_z):
        vals = [buf[y * n_z + z] for y in range(n_y)]
        fct_ref[z * rows : (z + 1) * rows, :] = jnp.concatenate(
            [v[:, :half] for v in vals], axis=1
        )
        projt_ref[z * rows : (z + 1) * rows, :] = jnp.concatenate(
            [v[:, half:] for v in vals], axis=1
        )


def attn_grads_kernel(dims, pos_ref, *refs):
    n_dp, n_f, nq, no = dims
    n_z = n_f // 2
    c, dp, f = pos_ref[1], pos_ref[2], pos_ref[3]
    n1_ref, ob_ref, dq_ref, dk_ref, dv_ref, dy_ref = refs[:6]
    outs_by_x, (n1t, obt) = (refs[6:8], refs[8:10]), refs[10:]
    n1t[...] = n1_ref[...].astype(F32).T.astype(BF16)
    obt[...] = ob_ref[...].astype(F32).T.astype(BF16)
    width = n1t.shape[0]
    k_rows = width // n_dp
    half = k_rows // 2
    rows = refs[6].shape[1]
    own = n1t.shape[1] - dq_ref.shape[0]

    def one(dy, dx):
        keep_ref, send_ref = outs_by_x[dx]
        at = pl.ds(((2 * dy + dx) ^ dp) * k_rows, k_rows)
        left = n1t[at, :]
        parts = [
            nn(left[:, own:], dq_ref[...]).astype(BF16),
            nn(left, dk_ref[...]).astype(BF16),
            nn(left, dv_ref[...]).astype(BF16),
        ]
        outs = nn(obt[at, :], dy_ref[...]).astype(BF16)
        for k in range(n_z):
            for part in range(2):
                both = []
                for g in (2 * k, 2 * k + 1):
                    vals = []
                    for h in range(2):
                        row = h * half + part * (half - rows)
                        for which, lo, hi in split_cols(g * nq, (g + 1) * nq, width):
                            vals.append(parts[which][row : row + rows, lo:hi])
                        vals.append(outs[row : row + rows, g * no : (g + 1) * no])
                    both.append(jnp.concatenate(vals, axis=1))
                slot = (part * n_dp // 2 + dy) * n_z + ((f >> 1) ^ k)
                keep_ref[slot] = jnp.where(c == 0, both[0], both[1])
                send_ref[slot] = jnp.where(c == 0, both[1], both[0])

    for dx in range(2):
        repeat(n_dp // 2, k_rows % 16 == 0, functools.partial(one, dx=dx))


def qkv_kernel(n1_ref, wq_ref, wk_ref, wv_ref, q_ref, k_ref, v_ref):
    tok = q_ref.shape[0]
    first = n1_ref.shape[0] - tok
    q_ref[...] = nn(n1_ref[first:, :], wq_ref[...]).astype(BF16)

    def one(i):
        at = pl.ds(pl.multiple_of(i * tok, tok), tok)
        k_ref[at, :] = nn(n1_ref[at, :], wk_ref[...]).astype(BF16)
        v_ref[at, :] = nn(n1_ref[at, :], wv_ref[...]).astype(BF16)

    repeat(n1_ref.shape[0] // tok, True, one)


def dn1_kernel(
    dq_ref, dk_ref, dv_ref, wq_ref, wk_ref, wv_ref, x_ref, own_ref, halo_ref, sums_ref
):
    tok = dq_ref.shape[0]
    cut = halo_ref.shape[0]
    sums_ref[...] = jnp.zeros(sums_ref.shape, F32)

    def tally(grads, at):
        xhat, _ = xhat_of(x_ref[at, :].astype(F32))
        sums_ref[0:1, :] += jnp.sum(grads * xhat, axis=0, keepdims=True)
        sums_ref[1:2, :] += jnp.sum(grads, axis=0, keepdims=True)

    def rows_of(at):
        return nt(dk_ref[at, :], wk_ref[...]) + nt(dv_ref[at, :], wv_ref[...])

    def step(r, carry):
        at = pl.ds(pl.multiple_of(r * tok, tok), tok)
        grads = rows_of(at)
        halo_ref[at, :] = grads.astype(BF16)
        tally(grads, at)
        return carry

    lax.fori_loop(0, cut // tok, step, 0)
    last = pl.ds(cut, tok)
    grads = nt(dq_ref[...], wq_ref[...]) + rows_of(last)
    own_ref[...] = grads
    tally(grads, last)


def ffn_kernel(*refs):
    n2_refs, gz_refs = refs[:4], refs[4:8]
    fct_ref, projt_ref, act_ref, dh_ref = refs[8:12]
    dn2_refs = refs[12:]
    tok = n2_refs[0].shape[0]
    for i in range(4):
        at = slice(i * tok, (i + 1) * tok)
        hidden = nt(n2_refs[i][...], fct_ref[...])
        cdf = 0.5 * (1.0 + lax.erf(hidden * math.sqrt(0.5)))
        act_ref[at, :] = (hidden * cdf).astype(BF16)
        slope = cdf + hidden * jnp.exp(-0.5 * hidden * hidden) * (1.0 / math.sqrt(2.0 * math.pi))
        dh_ref[at, :] = (nn(gz_refs[i][...], projt_ref[...]) * slope).astype(BF16)
        dn2_refs[i][...] = nn(dh_ref[at, :], fct_ref[...]).astype(BF16)


def ffn_grads_kernel(dims, pos_ref, dh_ref, *refs):
    n2_refs, gz_refs = refs[:4], refs[4:8]
    act_ref, out_ref, dht, gzt, n2_ref = refs[8:]
    n_y, n_z = dims
    tok = n2_refs[0].shape[0]
    dp, f = pos_ref[2], pos_ref[3]
    rows, wide = out_ref.shape[1:]
    half = wide // 2
    dht[...] = dh_ref[...].astype(F32).T.astype(BF16)
    for i in range(4):
        at = slice(i * tok, (i + 1) * tok)
        gzt[:, at] = gz_refs[i][...].astype(F32).T.astype(BF16)
        n2_ref[at, :] = n2_refs[i][...]

    def one(z):
        at = pl.ds(z * rows, rows)
        gfc = nn(dht[at, :], n2_ref[...]).astype(BF16)
        gproj = nn(gzt[at, :], act_ref[...]).astype(BF16)
        for y in range(n_y):
            slot = ((dp >> 1) ^ y) * n_z + ((f >> 1) ^ z)
            lanes = slice(y * half, (y + 1) * half)
            out_ref[slot] = jnp.concatenate([gfc[:, lanes], gproj[:, lanes]], axis=1)

    repeat(n_z, rows % 16 == 0, one)


def total(refs):
    acc = refs[0][...].astype(F32)
    for ref in refs[1:]:
        acc = acc + ref[...].astype(F32)
    return acc


def unpack_attn_kernel(count, rows, *refs):
    gq_ref, got_ref, go_ref = refs[count:]
    half = gq_ref.shape[0] // 2
    nq, no = gq_ref.shape[1], go_ref.shape[1]
    for part in range(2):
        summed = total([ref.at[part * rows : (part + 1) * rows] for ref in refs[:count]])
        skip = part * (2 * rows - half)
        for h in range(2):
            base = h * (nq + no)
            row = h * half + part * rows
            stop = row + rows - skip
            gq_ref[row:stop, :] = summed[skip:, base : base + nq]
            go_ref[row:stop, :] = summed[skip:, base + nq : base + nq + no]
    got_ref[...] = go_ref[...].T


def unpack_ffn_first_kernel(pos_ref, own_ref, up_ref, down_ref, send_ref, keep_ref):
    x, f = pos_ref[0], pos_ref[3]
    up = jnp.where(f >= 2, up_ref[...].astype(F32), 0.0)
    summed = own_ref[...].astype(F32) + up + down_ref[...].astype(F32)
    q = summed.shape[1] // 4
    first = jnp.concatenate([summed[:, :q], summed[:, 2 * q : 3 * q]], axis=1)
    second = jnp.concatenate([summed[:, q : 2 * q], summed[:, 3 * q :]], axis=1)
    send_ref[...] = jnp.where(x == 0, second, first).astype(BF16)
    keep_ref[...] = jnp.where(x == 0, first, second)


def unpack_ffn_second_kernel(pos_ref, keep_ref, got_ref, gfc_ref, send_ref, hold_ref):
    x, c = pos_ref[0], pos_ref[1]
    keep, got = keep_ref[...], got_ref[...].astype(F32)
    h = keep.shape[1] // 2
    rows = keep.shape[0] // 2
    first = jnp.where(x == 0, keep, got)
    second = jnp.where(x == 0, got, keep)
    gfc_ref[...] = jnp.concatenate([first[:, :h].T, second[:, :h].T], axis=1)
    both = jnp.concatenate([first[:, h:], second[:, h:]], axis=1)
    top, low = both[:rows, :], both[rows:, :]
    send_ref[...] = jnp.where(c == 0, low, top).astype(BF16)
    hold_ref[...] = jnp.where(c == 0, top, low)


def unpack_ffn_third_kernel(pos_ref, hold_ref, got_ref, gprojt_ref):
    c = pos_ref[1]
    hold, got = hold_ref[...], got_ref[...].astype(F32)
    gprojt_ref[...] = jnp.concatenate(
        [jnp.where(c == 0, hold, got), jnp.where(c == 0, got, hold)], axis=1
    )


def finish_kernel(
    middle_ref,
    act_own_ref,
    act_sib_ref,
    act_far_ref,
    dx1_ref,
    dn1_ref,
    near_ref,
    coming_ref,
    x_ref,
    norms_ref,
    act_ref,
    grad_ref,
):
    act_ref[...] = (middle_ref[...] + total((act_own_ref, act_sib_ref, act_far_ref))).T.astype(BF16)
    dn1 = total((dn1_ref, near_ref, coming_ref))
    xhat, factor = xhat_of(x_ref[...].astype(F32))
    grads = dx1_ref[...] + norm_back(dn1, norms_ref[0:1, :], xhat, factor)
    grad_ref[...] = grads.T.astype(BF16)


def fill_bias(start_ref, bias_ref):
    keys, rows = bias_ref.shape
    key_ids = lax.broadcasted_iota(jnp.int32, (keys, rows), 0)
    row_ids = lax.broadcasted_iota(jnp.int32, (keys, rows), 1) + (keys - rows)
    allowed = (key_ids >= start_ref[...]) & (key_ids <= row_ids)
    bias_ref[...] = jnp.where(allowed, 0.0, NEG)


def head_slices(width):
    pairs = width // (2 * HEAD_DIM)
    return pairs, width - pairs * 2 * HEAD_DIM


def attn_fwd_kernel(
    q_ref,
    k_ref,
    v_ref,
    start_ref,
    x_ref,
    wo_ref,
    norms_ref,
    o_ref,
    lse_ref,
    middle_ref,
    n2_ref,
    qt,
    vt,
    ot,
    bias,
):
    width = q_ref.shape[1]
    fill_bias(start_ref, bias)
    qt[...] = (q_ref[...].astype(F32) * HEAD_DIM ** (-0.5)).T.astype(BF16)
    vt[...] = v_ref[...].astype(F32).T.astype(BF16)
    pairs, rest = head_slices(width)

    def one(keys, queries, values, row, head):
        scores = nn(keys, queries) + bias[...]
        peak = jnp.max(scores, axis=0, keepdims=True)
        terms = jnp.exp(scores - peak)
        summed = jnp.sum(terms, axis=0, keepdims=True)
        ot[pl.ds(row, HEAD_DIM), :] = nn(values, terms.astype(BF16)) / summed
        lse_ref[pl.ds(head, 1), :] = peak + jnp.log(summed)

    def pair(p, _):
        at = pl.multiple_of(p * 128, 128)
        keys = k_ref[:, pl.ds(at, 128)]
        queries = qt[pl.ds(at, 128), :]
        rows = lax.broadcasted_iota(jnp.int32, queries.shape, 0)
        for h in range(2):
            row = pl.multiple_of(at + h * HEAD_DIM, HEAD_DIM)
            one(
                keys,
                jnp.where((rows < HEAD_DIM) == (h == 0), queries, jnp.zeros_like(queries)),
                vt[pl.ds(row, HEAD_DIM), :],
                row,
                2 * p + h,
            )
        return 0

    lax.fori_loop(0, pairs, pair, 0)
    if rest:
        at = pairs * 128
        one(k_ref[:, at:], qt[at:, :], vt[at:, :], at, 2 * pairs)
    o_ref[...] = ot[...].T.astype(BF16)
    middle = x_ref[...].astype(F32) + nn(o_ref[...], wo_ref[...])
    middle_ref[...] = middle
    xhat, _ = xhat_of(middle)
    n2_ref[...] = (xhat * norms_ref[2:3, :] + norms_ref[3:4, :]).astype(BF16)


def attn_bwd_kernel(
    dn2_own_ref,
    dn2_sib_ref,
    dn2_far_ref,
    gz_ref,
    middle_ref,
    norms_ref,
    wo_ref,
    q_ref,
    k_ref,
    v_ref,
    lse_ref,
    start_ref,
    act_ref,
    projt_ref,
    dx1_ref,
    dy_ref,
    sums_ref,
    dq_ref,
    dk_ref,
    dv_ref,
    act_own_ref,
    act_far_ref,
    act_sib_ref,
    act_far_sib_ref,
    do_ref,
    qt,
    dot_s,
    kt,
    dqt,
    bias,
):
    width = q_ref.shape[1]
    scale = HEAD_DIM ** (-0.5)
    dn2 = total((dn2_own_ref, dn2_sib_ref, dn2_far_ref))
    xhat, factor = xhat_of(middle_ref[...])
    sums_ref[0:1, :] = jnp.sum(dn2 * xhat, axis=0, keepdims=True)
    sums_ref[1:2, :] = jnp.sum(dn2, axis=0, keepdims=True)
    dx1 = gz_ref[...].astype(F32) + norm_back(dn2, norms_ref[2:3, :], xhat, factor)
    dx1_ref[...] = dx1
    dy_ref[...] = dx1.astype(BF16)
    do_ref[...] = nt(dy_ref[...], wo_ref[...]).astype(BF16)
    fill_bias(start_ref, bias)
    qt[...] = (q_ref[...].astype(F32) * scale).T.astype(BF16)
    dot_s[...] = do_ref[...].astype(F32).T.astype(BF16)
    kt[...] = k_ref[...].astype(F32).T.astype(BF16)
    pairs, rest = head_slices(width)

    def one(keys, values, queries_t, douts_t, keys_t, queries, douts, row, head):
        scores = nn(keys, queries_t) + bias[...]
        probs = jnp.exp(scores - lse_ref[pl.ds(head, 1), :])
        dprobs = nn(values, douts_t)
        delta = jnp.sum(probs * dprobs, axis=0, keepdims=True)
        dscores = (probs * (dprobs - delta)).astype(BF16)
        dqt[pl.ds(row, HEAD_DIM), :] = nn(keys_t, dscores)
        return nn(dscores, queries), nn(probs.astype(BF16), douts)

    def scaled(values):
        return (values.astype(F32) * scale).astype(BF16)

    def pair(p, _):
        at = pl.multiple_of(p * 128, 128)
        keys = k_ref[:, pl.ds(at, 128)]
        values = v_ref[:, pl.ds(at, 128)]
        queries = scaled(q_ref[:, pl.ds(at, 128)])
        douts = do_ref[:, pl.ds(at, 128)]
        queries_t = qt[pl.ds(at, 128), :]
        douts_t = dot_s[pl.ds(at, 128), :]
        rows = lax.broadcasted_iota(jnp.int32, queries_t.shape, 0)
        lanes = lax.broadcasted_iota(jnp.int32, queries.shape, 1)
        dk_sum = dv_sum = None
        for h in range(2):
            row = pl.multiple_of(at + h * HEAD_DIM, HEAD_DIM)
            in_rows = (rows < HEAD_DIM) == (h == 0)
            in_lanes = (lanes < HEAD_DIM) == (h == 0)
            zero_t, zero = jnp.zeros_like(queries_t), jnp.zeros_like(queries)
            dk_part, dv_part = one(
                keys,
                values,
                jnp.where(in_rows, queries_t, zero_t),
                jnp.where(in_rows, douts_t, zero_t),
                kt[pl.ds(row, HEAD_DIM), :],
                jnp.where(in_lanes, queries, zero),
                jnp.where(in_lanes, douts, zero),
                row,
                2 * p + h,
            )
            dk_sum = dk_part if h == 0 else dk_sum + dk_part
            dv_sum = dv_part if h == 0 else dv_sum + dv_part
        dk_ref[:, pl.ds(at, 128)] = dk_sum.astype(BF16)
        dv_ref[:, pl.ds(at, 128)] = dv_sum.astype(BF16)
        return 0

    lax.fori_loop(0, pairs, pair, 0)
    if rest:
        at = pairs * 128
        dk_part, dv_part = one(
            k_ref[:, at:],
            v_ref[:, at:],
            qt[at:, :],
            dot_s[at:, :],
            kt[at:, :],
            scaled(q_ref[:, at:]),
            do_ref[:, at:],
            at,
            2 * pairs,
        )
        dk_ref[:, at:] = dk_part.astype(BF16)
        dv_ref[:, at:] = dv_part.astype(BF16)
    dq_ref[...] = (dqt[...].T * scale).astype(BF16)
    tok = q_ref.shape[0]
    for i, y_ref in enumerate((act_own_ref, act_far_ref, act_sib_ref, act_far_sib_ref)):
        y_ref[...] = nt(act_ref[i * tok : (i + 1) * tok, :], projt_ref[...]).astype(BF16)


def xhat_of(values):
    center = jnp.mean(values, axis=-1, keepdims=True)
    centered = values - center
    variance = jnp.mean(centered * centered, axis=-1, keepdims=True)
    factor = lax.rsqrt(variance + EPS)
    return centered * factor, factor


def norm_back(grads, gain, xhat, factor):
    e = grads * gain
    return factor * (
        e
        - jnp.mean(e, axis=-1, keepdims=True)
        - xhat * jnp.mean(e * xhat, axis=-1, keepdims=True)
    )


def add(*terms):
    acc = terms[0].astype(F32)
    for term in terms[1:]:
        acc = acc + term.astype(F32)
    return acc


def segment_starts(dealt_lengths, seq_order, first_row, rows):
    lengths = dealt_lengths[0].reshape(-1)
    order = seq_order[0]
    count = lengths.shape[0]
    arrival = jnp.arange(count, dtype=jnp.int32)
    before = (order[:, None] < arrival[None, :]).astype(jnp.int32)
    begins = jnp.sum(before * lengths[:, None], axis=0)
    ids = first_row + jnp.arange(rows, dtype=jnp.int32)
    reached = begins[:, None] <= ids[None, :]
    return jnp.max(jnp.where(reached, begins[:, None], 0), axis=0)


def tiled(value):
    if value.ndim == 2 and value.shape[0] % 128 == 0 and value.shape[1] % 128:
        return value.reshape(value.shape[0] // 8, 8, value.shape[1])
    return value


def barrier(value, fence):
    leaves, tree = jax.tree.flatten(value)
    kept = lax.optimization_barrier(([tiled(v) for v in leaves], fence))[0]
    return tree.unflatten([k.reshape(v.shape) for k, v in zip(kept, leaves)])


def permute(value, axis, pairs):
    return lax.ppermute(tiled(value), axis, pairs).reshape(value.shape)


class Clock:
    def __init__(self):
        self.fence = ()

    def __call__(self, value):
        if not self.fence:
            return value
        return barrier(value, self.fence)

    def tick(self, *done):
        self.fence = tuple(tiled(v) for v in jax.tree.leaves(done))


def per_device(
    tokens,
    qkv_weight,
    out_weight,
    fc_weight,
    proj_weight,
    norm_params,
    grad_out,
    dealt_lengths,
    seq_order,
):
    n_dp, n_f = lax.axis_size("dp"), lax.axis_size("fsdp")
    n_y, n_z = n_dp // 2, n_f // 2
    dp, f = lax.axis_index("dp"), lax.axis_index("fsdp")
    x, c = dp & 1, f & 1
    pos = jnp.stack([x, c, dp, f]).astype(jnp.int32)
    tok, width = tokens.shape
    seq_longest = n_f * tok // dealt_lengths.shape[1] // 2
    halo = -(-seq_longest // tok)
    halo += halo % 2

    now = Clock()

    def run(*args, **kwargs):
        made = call(*args, **kwargs)
        return lambda *operands: made(*now(operands))

    def xor(value, axis, bits):
        size = n_dp if axis == "dp" else n_f
        return permute(now(value), axis, [(i, i ^ bits) for i in range(size)])

    def to_core(value):
        return xor(value, "fsdp", 1)

    def to_x(value):
        return xor(value, "dp", 1)

    def to_y(value, k):
        return xor(value, "dp", 2 * k)

    def to_z(value, k):
        return xor(value, "fsdp", 2 * k)

    def along_z(value, step, senders):
        pairs = [(2 * z + i, 2 * (z + step) + i) for z in senders for i in range(2)]
        return permute(now(value), "fsdp", pairs)

    def joined(*values):
        return jnp.concatenate(values, axis=0)

    z_at = f >> 1
    others_z, others_y = range(1, n_z), range(1, n_y)

    def by_z(choose):
        choices = [choose(z) for z in range(n_z)]
        value = choices[0]
        for z in range(1, n_z):
            if choices[z] is not choices[z - 1]:
                value = jnp.where(z_at >= z, choices[z], value)
        return value

    k_rows, nq = qkv_weight.shape
    no = out_weight.shape[1]
    half, wide = k_rows // 2, 2 * (nq + no)
    rows = (half // 2 + 7) // 8 * 8
    own_first, own_second = run(pack_attn_kernel, [((rows, wide), BF16)] * 2, [VM, VM])(
        qkv_weight, out_weight.T
    )
    now.tick(own_first, own_second)

    firsts = [own_first] + [to_z(own_first, dz) for dz in others_z]
    ff_half = fc_weight.shape[1] // 2
    sub = proj_weight.shape[0] // 4
    send, keep = run(
        pack_ffn_first_kernel, [((ff_half, k_rows + sub), BF16)] * 2, [SM, VM, VM])(pos, fc_weight, proj_weight.T)
    got = to_x(send)
    norm_x = to_x(norm_params)
    now.tick(firsts, got, norm_x)

    stack = {(0, 0, 0): jnp.stack(firsts)}
    seconds = [own_second] + [to_z(own_second, dz) for dz in others_z]
    for dy in others_y:
        stack[0, dy, 0] = to_y(stack[0, 0, 0], dy)
    stack[0, 0, 1] = to_x(stack[0, 0, 0])
    fct, send, hold = run(
        pack_ffn_second_kernel,
        [((ff_half, 2 * k_rows), BF16)] + [((no, 2 * sub), BF16)] * 2,
        [SM, VM, VM])(pos, keep, got)
    now.tick(seconds, stack, send)

    got = to_core(send)
    norm_pairs = jnp.stack([norm_params, norm_x])
    norm_pairs = [norm_pairs] + [to_y(norm_pairs, dy) for dy in others_y]
    stack[1, 0, 0] = jnp.stack(seconds)
    stack[1, 0, 1] = to_x(stack[1, 0, 0])
    for dy in others_y:
        stack[1, dy, 0] = to_y(stack[1, 0, 0], dy)
    even = [tokens]
    for _ in range(halo // 2):
        even.append(along_z(even[-1], 1, range(n_z - 1)))
    stacks, arrays = [], []

    def cross(*keys):
        stacks.extend([(key + (0,),) for key in keys])
        arrays.extend(stack[key] for key in keys)
        stacks.append(tuple(key + (1,) for key in keys))
        arrays.append(to_core(joined(*[stack[key] for key in keys])))

    cross((0, 0, 0), *[(0, dy, 0) for dy in others_y])
    (own_ffn,) = run(
        pack_ffn_third_kernel, [((ff_half, 2 * (k_rows + sub)), BF16)], [SM, VM, VM, VM])(pos, fct, hold, got)
    now.tick(stack, even[-1], arrays[-1], own_ffn, norm_pairs)

    ups, downs, ffn = [own_ffn], [own_ffn], {(0, 0): own_ffn}

    def ffn_over_z(t):
        ups.append(along_z(ups[-1], 1, range(t - 1, n_z - 1)))
        downs.append(along_z(downs[-1], -1, range(1, n_z - t + 1)))

    def pick(t):
        return by_z(lambda z: ups[z - (z ^ t)] if z ^ t < z else downs[(z ^ t) - z])

    for dy in others_y:
        stack[0, dy, 1] = to_x(stack[0, dy, 0])
        stack[1, dy, 1] = to_y(stack[1, 0, 1], dy)
    rows_before = []
    for distance in range(1, halo + 1):
        if distance % 2:
            near = distance // 2
            rows_before.append(to_core(jnp.where(c == 0, even[near], even[near + 1])))
        else:
            rows_before.append(even[distance // 2])
    x_rows = joined(*rows_before[::-1], tokens)
    cross((0, 0, 1), (1, 0, 0), (1, 0, 1), *[(1, dy, 0) for dy in others_y])
    norms = jnp.concatenate(
        [
            sum(
                jnp.where((dp ^ r) == j, norm_pairs[r >> 1][r & 1].astype(F32), 0.0)
                for r in range(n_dp)
            )
            for j in range(n_dp)
        ],
        axis=1,
    )
    xhat_one, factor_one = xhat_of(x_rows.astype(F32))
    normed = (xhat_one * norms[0] + norms[1]).astype(BF16)
    now.tick(arrays[-1], stack, normed)

    cross(*[(part, dy, 1) for dy in others_y for part in range(2)])
    now.tick(arrays[-1])
    ffn_over_z(1)
    for dy in others_y:
        ffn[dy, 0] = to_y(own_ffn, dy)
    gz_far = to_x(grad_out)
    gz_sib = to_core(grad_out)
    square = ((width, width), BF16)
    dims = (n_dp, n_f, nq, no)
    wq, wk, wv, wo = run(
        functools.partial(assemble_attn_kernel, stacks, dims),
        [square] * 4,
        [SM] + [ANY] * len(arrays),
        [
            pltpu.VMEM((2, n_dp * n_f, rows, wide), BF16),
            pltpu.SemaphoreType.DMA((2 * n_dp * n_f,)),
        ])(pos, *arrays)
    now.tick(wq, wk, wv, wo, ups, downs, ffn, gz_far, gz_sib)

    ffn[0, 1] = pick(1)
    ffn_over_z(2)
    for dy in others_y:
        ffn[dy, 1] = to_y(ffn[0, 1], dy)
    gz_far_sib = to_core(gz_far)
    queries, all_keys, values = run(
        qkv_kernel, [((tok, width), BF16)] + [(normed.shape, BF16)] * 2, [VM] * 4)(normed, wq, wk, wv)
    now.tick(queries, all_keys, values, ups, downs, ffn, gz_far_sib)

    ffn[0, 2] = pick(2)
    for t in others_z[2:]:
        ffn_over_z(t)
    for dy in others_y:
        ffn[dy, 2] = to_y(ffn[0, 2], dy)
    span = (halo + 1) * tok
    starts = segment_starts(dealt_lengths, seq_order, f * tok, tok) - (f - halo) * tok
    starts = starts.reshape(1, tok).astype(jnp.int32)
    heads = width // HEAD_DIM
    attended, lse, middle, normed_two = run(
        attn_fwd_kernel,
        [((tok, width), BF16), ((heads, tok), F32), ((tok, width), F32), ((tok, width), BF16)],
        [VM] * 7,
        [
            pltpu.VMEM((width, tok), BF16),
            pltpu.VMEM((width, span), BF16),
            pltpu.VMEM((width, tok), F32),
            pltpu.VMEM((span, tok), F32),
        ])(queries, all_keys, values, starts, tokens, wo, norms)
    now.tick(attended, lse, middle, normed_two, ups, downs, ffn)

    n2_far = to_x(normed_two)
    n2_sib = to_core(normed_two)
    for t in others_z[2:]:
        ffn[0, t] = pick(t)
        for dy in others_y:
            ffn[dy, t] = to_y(ffn[0, t], dy)
    now.tick(n2_far, n2_sib, ffn)
    n2_far_sib = to_core(n2_far)
    n2_rows = [normed_two, n2_far, n2_sib, n2_far_sib]
    gz_rows = [grad_out, gz_far, gz_sib, gz_far_sib]

    ffn_keys = sorted(ffn)
    fct_full, projt_full = run(
        functools.partial(assemble_ffn_kernel, ffn_keys, (n_y, n_z)),
        [((n_z * ff_half, n_y * 2 * k_rows), BF16), ((n_z * 2 * no, n_y * 2 * sub), BF16)],
        [SM] + [ANY] * len(ffn_keys),
        [
            pltpu.VMEM((len(ffn_keys),) + own_ffn.shape, BF16),
            pltpu.SemaphoreType.DMA((len(ffn_keys),)),
        ])(pos, *[ffn[key] for key in ffn_keys])
    ff = fct_full.shape[0]
    activated, dhidden, own, far, sib, far_sib = run(
        ffn_kernel,
        [((4 * tok, ff), BF16)] * 2 + [((tok, width), BF16)] * 4,
        [VM] * 10)(*n2_rows, *gz_rows, fct_full, projt_full)
    now.tick(activated, dhidden, own, far, sib, far_sib)
    far = add(far, to_core(far_sib)).astype(BF16)
    now.tick(far)

    dn2_far = to_x(far)
    dn2_sib = to_core(sib)
    (ffn_grads,) = run(
        functools.partial(ffn_grads_kernel, (n_y, n_z)),
        [((n_y * n_z,) + own_ffn.shape, BF16)],
        [SM] + [VM] * 10,
        [
            pltpu.VMEM((n_z * ff_half, 4 * tok), BF16),
            pltpu.VMEM((width, 4 * tok), BF16),
            pltpu.VMEM((4 * tok, width), BF16),
        ])(pos, dhidden, *n2_rows, *gz_rows, activated)
    now.tick(ffn_grads, dn2_far, dn2_sib)

    part_of = {}

    def ffn_over_y(dz):
        part_of[dz] = add(
            ffn_grads[dz], *[to_y(ffn_grads[dy * n_z + dz], dy) for dy in others_y]
        ).astype(BF16)

    for dz in others_z[::-1][:-1]:
        ffn_over_y(dz)
    big, small = (span, width), (tok, width)
    dx1, dy_low, norm_sums, dq, dk, dv, act_own, act_far, act_sib, act_far_sib = run(
        attn_bwd_kernel,
        [(small, F32), (small, BF16), ((2, width), F32), (small, BF16), (big, BF16), (big, BF16)]
        + [(small, BF16)] * 4,
        [VM] * 14,
        [
            pltpu.VMEM(small, BF16),
            pltpu.VMEM((width, tok), BF16),
            pltpu.VMEM((width, tok), BF16),
            pltpu.VMEM((width, span), BF16),
            pltpu.VMEM((width, tok), F32),
            pltpu.VMEM((span, tok), F32),
        ])(own, dn2_sib, dn2_far, grad_out, middle, norms, wo, queries, all_keys, values, lse, starts, activated, projt_full)
    now.tick(dq, dk, dv, part_of, act_own, act_far, act_sib, act_far_sib)

    carry = [None, None]

    def ffn_back_z(s):
        reach = n_z - s
        for way, (step, senders) in enumerate(
            ((1, range(0, s)), (-1, range(n_z - s, n_z)))
        ):
            value = by_z(
                lambda z: part_of[z ^ (z + step * reach)]
                if 0 <= z + step * reach < n_z
                else part_of[n_z - 1]
            )
            if carry[way] is not None:
                value = add(value, carry[way]).astype(BF16)
            carry[way] = along_z(value, step, senders)

    next_y = [to_y(ffn_grads[dy * n_z + 1], dy) for dy in others_y]
    act_far_sib = to_core(act_far_sib)
    count = 2 * n_y * n_z
    block = ((count, rows, wide), BF16)
    keeps, sent, gots = {}, {}, {}
    keeps[0], sent[0], keeps[1], sent[1] = run(
        functools.partial(attn_grads_kernel, dims),
        [block] * 4,
        [SM] + [VM] * 6,
        [pltpu.VMEM((width, span), BF16), pltpu.VMEM((width, tok), BF16)],
    )(pos, normed, attended, dq, dk, dv, dy_low)
    now.tick(keeps, sent, next_y, act_far_sib)

    gots[1], gots[0] = to_core(sent[1]), to_core(sent[0])
    act_sib = to_core(act_sib)
    ffn_back_z(1)

    def core_sum(part, dy, dx, count=1):
        at = (part * n_y + dy) * n_z
        stop = at + count * n_z
        return add(keeps[dx][at:stop], gots[dx][at:stop])

    x_send = core_sum(0, 0, 1, n_y).astype(BF16)
    y_send = [core_sum(1, dy, 1).astype(BF16) for dy in others_y]
    now.tick(x_send, y_send, gots, act_sib)

    last_y = [to_y(ffn_grads[dy * n_z], dy) for dy in others_y]
    got_x = to_x(x_send)
    got_y = [to_y(value, dy) for dy, value in zip(others_y, y_send)]
    for s in range(2, n_z - 1):
        ffn_back_z(s)
    cut = halo * tok
    dn1, dn1_halo, norm_first = run(
        dn1_kernel, [(small, F32), ((cut, width), BF16), ((2, width), F32)], [VM] * 7
    )(dq, dk, dv, wq, wk, wv, x_rows)
    norm_rows = -(-4 * width // wide // 8) * 8

    def with_norms(value, norms):
        extra = norms.astype(BF16).reshape(-1, wide)
        extra = jnp.pad(extra, ((0, norm_rows - extra.shape[0]), (0, 0)))
        extra = jnp.broadcast_to(extra, value.shape[:-2] + extra.shape)
        return jnp.concatenate([value, extra], axis=-2)

    def norms_of(value):
        return value[0, -norm_rows:][: 4 * width // wide].reshape(4, width).astype(F32)

    now.tick(got_x, got_y, carry, dn1, dn1_halo, norm_first, last_y)
    got_x, got_y, dn1, dn1_halo, norm_first, last_y, next_y, act_far_sib = now(
        (got_x, got_y, dn1, dn1_halo, norm_first, last_y, next_y, act_far_sib)
    )
    part_of[1] = add(ffn_grads[1], *next_y).astype(BF16)
    part_of[0] = add(ffn_grads[0], *last_y).astype(BF16)

    norm_grads = joined(norm_first, norm_sums)
    first_x = [got_x[dy * n_z : (dy + 1) * n_z] for dy in range(n_y)]
    both = []
    for dy in others_y:
        value = [add(core_sum(0, dy, 0), first_x[dy]), core_sum(1, dy, 0)]
        value = jnp.concatenate([v.astype(BF16) for v in value], axis=1)
        both.append(to_y(with_norms(value, norm_grads), dy))
    act_far = add(act_far, act_far_sib).astype(BF16)
    second_x = add(core_sum(1, 0, 1), *got_y).astype(BF16)
    got_x = to_x(joined(second_x.reshape(-1, wide), act_far.reshape(-1, wide)))
    if n_z > 2:
        ffn_back_z(n_z - 1)
    def back(distance):
        return dn1_halo[cut - distance * tok : cut - (distance - 1) * tok]

    carried = [None] * (halo // 2 + 1)
    for near in range(halo // 2):
        got = to_core(back(2 * near + 1)).astype(F32)
        for level, wanted in ((near, 1), (near + 1, 0)):
            term = jnp.where(c != wanted, got, 0.0)
            carried[level] = term if carried[level] is None else carried[level] + term
    outgoing = [back(2 * level).astype(F32) + carried[level] for level in range(1, halo // 2 + 1)]
    coming = None
    for level in range(halo // 2, 0, -1):
        out = outgoing[level - 1]
        if coming is not None:
            out = out + coming
        coming = along_z(out.astype(BF16), -1, range(1, n_z)).astype(F32)
    now.tick(got_x, both, carry, coming)
    got_x, both, coming = now((got_x, both, coming))
    act_far = got_x[n_z * rows :].reshape(small)
    second_x = got_x[: n_z * rows].reshape(n_z, rows, wide)
    send, keep = run(
        unpack_ffn_first_kernel,
        [((ff_half, k_rows + sub), BF16), ((ff_half, k_rows + sub), F32)],
        [SM] + [VM] * 3,
    )(pos, part_of[0], *carry)
    norm_grads = norm_grads + sum(norms_of(value) for value in both)
    first_sum = add(core_sum(0, 0, 0), first_x[0], *[value[:, :rows] for value in both])
    second_sum = add(
        core_sum(1, 0, 0), second_x, *[value[:, rows : 2 * rows] for value in both]
    )
    sums = jnp.concatenate([first_sum.astype(BF16), second_sum.astype(BF16)], axis=1)
    sums = with_norms(sums, norm_grads)
    now.tick(sums)

    got = to_x(send)
    parts = [sums[0]] + [to_z(sums[dz], dz) for dz in others_z]
    activations, input_grad = run(finish_kernel, [((width, tok), BF16)] * 2, [VM] * 10)(
        middle,
        act_own,
        act_sib,
        act_far,
        dx1,
        dn1,
        carried[0].astype(BF16),
        coming.astype(BF16),
        tokens,
        norms,
    )
    grad_fc, send, hold = run(
        unpack_ffn_second_kernel,
        [(fc_weight.shape, F32), ((no, 2 * sub), BF16), ((no, 2 * sub), F32)],
        [SM, VM, VM])(pos, keep, got)
    (grad_proj,) = run(unpack_ffn_third_kernel, [(proj_weight.shape[::-1], F32)], [SM, VM, VM])(
        pos, hold, to_core(send)
    )
    parts = barrier(parts, (grad_fc, grad_proj, activations, input_grad))
    norm_grads = sum(norms_of(part[None]) for part in parts)
    norm_grads = norm_grads + lax.ppermute(norm_grads, "fsdp", [(i, i ^ 1) for i in range(n_f)])
    norm_grads = norm_grads + lax.ppermute(norm_grads, "dp", [(i, i ^ 1) for i in range(n_dp)])
    norm_grads = lax.dynamic_slice_in_dim(norm_grads, dp * k_rows, k_rows, axis=1)
    grad_qkv, grad_attn_out = run(
        functools.partial(unpack_attn_kernel, n_z, rows),
        [(qkv_weight.shape, F32), (out_weight.shape[::-1], F32)],
        [VM] * n_z,
        [pltpu.VMEM(out_weight.shape, F32)],
    )(*parts)
    return (activations.T, input_grad.T, grad_qkv, grad_attn_out.T, grad_fc, grad_proj.T, norm_grads)


def solution(mesh):
    in_specs = (
        P(("dp", "fsdp"), None),
        P("dp", "fsdp"),
        P("dp", "fsdp"),
        P("dp", "fsdp"),
        P("dp", "fsdp"),
        P(None, "dp"),
        P(("dp", "fsdp"), None),
        P("dp", None, None),
        P("dp", None),
    )
    out_specs = (
        P(("dp", "fsdp"), None),
        P(("dp", "fsdp"), None),
        P("dp", "fsdp"),
        P("dp", "fsdp"),
        P("dp", "fsdp"),
        P("dp", "fsdp"),
        P(None, "dp"),
    )
    return jax.shard_map(
        per_device, mesh=mesh, in_specs=in_specs, out_specs=out_specs, check_vma=False
    )
```

```python
import functools
import math

import jax
import jax.numpy as jnp
from jax import lax
from jax.experimental import pallas as pl
from jax.experimental.pallas import tpu as pltpu
from jax.sharding import PartitionSpec as P

HEAD_DIM = 64
EPS = 1e-05
NEG = -1e30
F32 = jnp.float32
BF16 = jnp.bfloat16
VMEM_ALL = 60 * 2**20

ANY = pl.BlockSpec(memory_space=pl.ANY)
VM = pl.BlockSpec(memory_space=pltpu.VMEM)
SM = pl.BlockSpec(memory_space=pltpu.SMEM)


def call(kernel, outs, in_specs, scratch=()):
    return pl.pallas_call(
        kernel,
        name=getattr(kernel, "func", kernel).__name__,
        out_shape=tuple(jax.ShapeDtypeStruct(s, d) for s, d in outs),
        in_specs=list(in_specs),
        out_specs=tuple(VM for _ in outs),
        scratch_shapes=list(scratch),
        compiler_params=pltpu.CompilerParams(vmem_limit_bytes=VMEM_ALL),
        cost_estimate=pl.CostEstimate(flops=0, bytes_accessed=0, transcendentals=0),
    )


def dot(a, b, ca, cb):
    return lax.dot_general(a, b, (((ca,), (cb,)), ((), ())), preferred_element_type=F32)


def nn(a, b):
    return dot(a, b, 1, 0)


def nt(a, b):
    return dot(a, b, 1, 1)


def tn(a, b):
    return dot(a, b, 0, 0)


def repeat(count, looped, body):
    if not looped:
        for i in range(count):
            body(i)
        return

    def step(i, carry):
        body(i)
        return carry

    lax.fori_loop(0, count, step, 0)


def split_cols(lo, hi, width):
    pieces = []
    while lo < hi:
        which, start = divmod(lo, width)
        stop = min(width, start + hi - lo)
        pieces.append((which, start, stop))
        lo += stop - start
    return pieces


def pack_attn_kernel(wq_ref, wo_ref, first_ref, second_ref):
    half = wq_ref.shape[0] // 2
    rows = first_ref.shape[0]
    wo = wo_ref[...].astype(F32).T.astype(BF16)
    for out_ref, row in ((first_ref, 0), (second_ref, half - rows)):
        vals = []
        for h in range(2):
            at = h * half + row
            vals += [wq_ref[at : at + rows, :], wo[at : at + rows, :]]
        out_ref[...] = jnp.concatenate(vals, axis=1)


def pack_ffn_first_kernel(pos_ref, fc_ref, projt_ref, send_ref, keep_ref):
    x = pos_ref[0]
    half = fc_ref.shape[1] // 2
    sub = projt_ref.shape[1] // 4
    sides = []
    for h in range(2):
        fct = fc_ref[:, h * half : (h + 1) * half].astype(F32).T
        projt = [
            projt_ref[:, (2 * s + h) * sub : (2 * s + h + 1) * sub].astype(F32) for s in range(2)
        ]
        sides.append(jnp.concatenate([fct, jnp.concatenate(projt, axis=0)], axis=1))
    send_ref[...] = jnp.where(x == 0, sides[1], sides[0]).astype(BF16)
    keep_ref[...] = jnp.where(x == 0, sides[0], sides[1]).astype(BF16)


def pack_ffn_second_kernel(pos_ref, keep_ref, got_ref, fct_ref, send_ref, hold_ref):
    x, c = pos_ref[0], pos_ref[1]
    keep, got = keep_ref[...], got_ref[...]
    first = jnp.where(x == 0, keep, got)
    second = jnp.where(x == 0, got, keep)
    k = fct_ref.shape[1] // 2
    rows = send_ref.shape[0]
    fct_ref[...] = jnp.concatenate([first[:, :k], second[:, :k]], axis=1)
    projt = jnp.concatenate([first[:, k:], second[:, k:]], axis=1)
    top, low = projt[:rows, :], projt[rows:, :]
    send_ref[...] = jnp.where(c == 0, low, top)
    hold_ref[...] = jnp.where(c == 0, top, low)


def pack_ffn_third_kernel(pos_ref, fct_ref, hold_ref, got_ref, out_ref):
    c = pos_ref[1]
    hold, got = hold_ref[...], got_ref[...]
    top = jnp.where(c == 0, hold, got)
    low = jnp.where(c == 0, got, hold)
    projt = jnp.concatenate([top, low], axis=0)
    out_ref[...] = jnp.concatenate([fct_ref[...], projt], axis=1)


def place(pieces, buf, sem, slots):
    copies = [
        pltpu.make_async_copy(piece, buf.at[slot], sem.at[i])
        for i, (piece, slot) in enumerate(zip(pieces, slots))
    ]
    for copy in copies:
        copy.start()
    for copy in copies:
        copy.wait()


def assemble_attn_kernel(stacks, dims, pos_ref, *refs):
    n_dp, n_f, nq, no = dims
    n_z = n_f // 2
    ins = refs[: len(stacks)]
    w_refs = refs[len(stacks) : len(stacks) + 3]
    wo_ref, buf, sem = refs[len(stacks) + 3 :]
    dp, f = pos_ref[2], pos_ref[3]
    copies = []
    for ref, groups in zip(ins, stacks):
        for i, (part, dy, dx, dc) in enumerate(groups):
            for dz in range(n_z):
                slot = (dp ^ (2 * dy + dx)) * n_f + (f ^ (2 * dz + dc))
                copies.append(
                    pltpu.make_async_copy(
                        ref.at[i * n_z + dz], buf.at[part, slot], sem.at[len(copies)]
                    )
                )
    for copy in copies:
        copy.start()
    for copy in copies:
        copy.wait()
    rows = buf.shape[2]
    wide = nq + no
    width = wo_ref.shape[1]
    half = width // n_dp // 2
    for d in range(n_dp):
        for h in range(2):
            base = h * wide
            for part, skip in ((0, 0), (1, 2 * rows - half)):
                row = (2 * d + h) * half + part * rows
                stop = row + rows - skip
                for third in range(3):
                    vals = [
                        buf[part, d * n_f + which][skip:, base + lo : base + hi]
                        for which, lo, hi in split_cols(third * width, (third + 1) * width, nq)
                    ]
                    w_refs[third][row:stop, :] = jnp.concatenate(vals, axis=1)
                wo_ref[row:stop, :] = jnp.concatenate(
                    [
                        buf[part, d * n_f + g][skip:, base + nq : base + wide]
                        for g in range(n_f)
                    ],
                    axis=1,
                )


def assemble_ffn_kernel(keys, dims, pos_ref, *refs):
    n_y, n_z = dims
    pieces = refs[: len(keys)]
    fct_ref, projt_ref, buf, sem = refs[len(keys) :]
    dp, f = pos_ref[2], pos_ref[3]
    slots = [((dp >> 1) ^ dy) * n_z + ((f >> 1) ^ dz) for dy, dz in keys]
    place(pieces, buf, sem, slots)
    rows, wide = buf.shape[1:]
    half = wide // 2
    for z in range(n_z):
        vals = [buf[y * n_z + z] for y in range(n_y)]
        fct_ref[z * rows : (z + 1) * rows, :] = jnp.concatenate(
            [v[:, :half] for v in vals], axis=1
        )
        projt_ref[z * rows : (z + 1) * rows, :] = jnp.concatenate(
            [v[:, half:] for v in vals], axis=1
        )


def attn_grads_kernel(dims, pos_ref, *refs):
    n_dp, n_f, nq, no = dims
    n_z = n_f // 2
    c, dp, f = pos_ref[1], pos_ref[2], pos_ref[3]
    n1_ref, ob_ref, dq_ref, dk_ref, dv_ref, dy_ref = refs[:6]
    outs_by_x, (n1t, obt) = (refs[6:8], refs[8:10]), refs[10:]
    n1t[...] = n1_ref[...].astype(F32).T.astype(BF16)
    obt[...] = ob_ref[...].astype(F32).T.astype(BF16)
    width = n1t.shape[0]
    k_rows = width // n_dp
    half = k_rows // 2
    rows = refs[6].shape[1]
    own = n1t.shape[1] - dq_ref.shape[0]

    def one(dy, dx):
        keep_ref, send_ref = outs_by_x[dx]
        at = pl.ds(((2 * dy + dx) ^ dp) * k_rows, k_rows)
        left = n1t[at, :]
        parts = [
            nn(left[:, own:], dq_ref[...]).astype(BF16),
            nn(left, dk_ref[...]).astype(BF16),
            nn(left, dv_ref[...]).astype(BF16),
        ]
        outs = nn(obt[at, :], dy_ref[...]).astype(BF16)
        for k in range(n_z):
            for part in range(2):
                both = []
                for g in (2 * k, 2 * k + 1):
                    vals = []
                    for h in range(2):
                        row = h * half + part * (half - rows)
                        for which, lo, hi in split_cols(g * nq, (g + 1) * nq, width):
                            vals.append(parts[which][row : row + rows, lo:hi])
                        vals.append(outs[row : row + rows, g * no : (g + 1) * no])
                    both.append(jnp.concatenate(vals, axis=1))
                slot = (part * n_dp // 2 + dy) * n_z + ((f >> 1) ^ k)
                keep_ref[slot] = jnp.where(c == 0, both[0], both[1])
                send_ref[slot] = jnp.where(c == 0, both[1], both[0])

    for dx in range(2):
        repeat(n_dp // 2, k_rows % 16 == 0, functools.partial(one, dx=dx))


def qkv_kernel(n1_ref, wq_ref, wk_ref, wv_ref, q_ref, k_ref, v_ref):
    tok = q_ref.shape[0]
    first = n1_ref.shape[0] - tok
    q_ref[...] = nn(n1_ref[first:, :], wq_ref[...]).astype(BF16)

    def one(i):
        at = pl.ds(pl.multiple_of(i * tok, tok), tok)
        k_ref[at, :] = nn(n1_ref[at, :], wk_ref[...]).astype(BF16)
        v_ref[at, :] = nn(n1_ref[at, :], wv_ref[...]).astype(BF16)

    repeat(n1_ref.shape[0] // tok, True, one)


def dn1_kernel(
    dq_ref, dk_ref, dv_ref, wq_ref, wk_ref, wv_ref, x_ref, own_ref, halo_ref, sums_ref
):
    tok = dq_ref.shape[0]
    cut = halo_ref.shape[0]
    sums_ref[...] = jnp.zeros(sums_ref.shape, F32)

    def tally(grads, at):
        xhat, _ = xhat_of(x_ref[at, :].astype(F32))
        sums_ref[0:1, :] += jnp.sum(grads * xhat, axis=0, keepdims=True)
        sums_ref[1:2, :] += jnp.sum(grads, axis=0, keepdims=True)

    def rows_of(at):
        return nt(dk_ref[at, :], wk_ref[...]) + nt(dv_ref[at, :], wv_ref[...])

    def step(r, carry):
        at = pl.ds(pl.multiple_of(r * tok, tok), tok)
        grads = rows_of(at)
        halo_ref[at, :] = grads.astype(BF16)
        tally(grads, at)
        return carry

    lax.fori_loop(0, cut // tok, step, 0)
    last = pl.ds(cut, tok)
    grads = nt(dq_ref[...], wq_ref[...]) + rows_of(last)
    own_ref[...] = grads
    tally(grads, last)


def members_of(tok):
    return [slice(i * tok, (i + 1) * tok) for i in range(4)]


def ffn_kernel(*refs):
    n2_refs, gz_refs = refs[:4], refs[4:8]
    fct_ref, projt_ref, act_ref, dh_ref = refs[8:12]
    dn2_refs = refs[12:16]
    n2s, gzs, dn2s = refs[16:]
    tok = n2_refs[0].shape[0]
    for i, at in enumerate(members_of(tok)):
        n2s[at, :] = n2_refs[i][...]
        gzs[at, :] = gz_refs[i][...]

    def one(i):
        at = pl.ds(pl.multiple_of(i * tok, tok), tok)
        hidden = nt(n2s[at, :], fct_ref[...])
        cdf = 0.5 * (1.0 + lax.erf(hidden * math.sqrt(0.5)))
        act_ref[at, :] = (hidden * cdf).astype(BF16)
        slope = cdf + hidden * jnp.exp(-0.5 * hidden * hidden) * (1.0 / math.sqrt(2.0 * math.pi))
        dh_ref[at, :] = (nn(gzs[at, :], projt_ref[...]) * slope).astype(BF16)
        dn2s[at, :] = nn(dh_ref[at, :], fct_ref[...]).astype(BF16)

    repeat(4, True, one)
    for dn2_ref, at in zip(dn2_refs, members_of(tok)):
        dn2_ref[...] = dn2s[at, :]


def ffn_grads_kernel(dims, pos_ref, dh_ref, *refs):
    n2_refs, gz_refs = refs[:4], refs[4:8]
    act_ref, out_ref, dht, gzt, n2_ref = refs[8:]
    n_y, n_z = dims
    tok = n2_refs[0].shape[0]
    dp, f = pos_ref[2], pos_ref[3]
    rows, wide = out_ref.shape[1:]
    half = wide // 2
    dht[...] = dh_ref[...].astype(F32).T.astype(BF16)
    for i in range(4):
        at = slice(i * tok, (i + 1) * tok)
        gzt[:, at] = gz_refs[i][...].astype(F32).T.astype(BF16)
        n2_ref[at, :] = n2_refs[i][...]

    def one(z):
        at = pl.ds(z * rows, rows)
        gfc = nn(dht[at, :], n2_ref[...]).astype(BF16)
        gproj = nn(gzt[at, :], act_ref[...]).astype(BF16)
        for y in range(n_y):
            slot = ((dp >> 1) ^ y) * n_z + ((f >> 1) ^ z)
            lanes = slice(y * half, (y + 1) * half)
            out_ref[slot] = jnp.concatenate([gfc[:, lanes], gproj[:, lanes]], axis=1)

    repeat(n_z, rows % 16 == 0, one)


def total(refs):
    acc = refs[0][...].astype(F32)
    for ref in refs[1:]:
        acc = acc + ref[...].astype(F32)
    return acc


def unpack_attn_kernel(count, rows, *refs):
    gq_ref, got_ref, go_ref = refs[count:]
    half = gq_ref.shape[0] // 2
    nq, no = gq_ref.shape[1], go_ref.shape[1]
    for part in range(2):
        summed = total([ref.at[part * rows : (part + 1) * rows] for ref in refs[:count]])
        skip = part * (2 * rows - half)
        for h in range(2):
            base = h * (nq + no)
            row = h * half + part * rows
            stop = row + rows - skip
            gq_ref[row:stop, :] = summed[skip:, base : base + nq]
            go_ref[row:stop, :] = summed[skip:, base + nq : base + nq + no]
    got_ref[...] = go_ref[...].T


def unpack_ffn_first_kernel(pos_ref, own_ref, up_ref, down_ref, send_ref, keep_ref):
    x, f = pos_ref[0], pos_ref[3]
    up = jnp.where(f >= 2, up_ref[...].astype(F32), 0.0)
    summed = own_ref[...].astype(F32) + up + down_ref[...].astype(F32)
    q = summed.shape[1] // 4
    first = jnp.concatenate([summed[:, :q], summed[:, 2 * q : 3 * q]], axis=1)
    second = jnp.concatenate([summed[:, q : 2 * q], summed[:, 3 * q :]], axis=1)
    send_ref[...] = jnp.where(x == 0, second, first).astype(BF16)
    keep_ref[...] = jnp.where(x == 0, first, second)


def unpack_ffn_second_kernel(pos_ref, keep_ref, got_ref, gfc_ref, send_ref, hold_ref):
    x, c = pos_ref[0], pos_ref[1]
    keep, got = keep_ref[...], got_ref[...].astype(F32)
    h = keep.shape[1] // 2
    rows = keep.shape[0] // 2
    first = jnp.where(x == 0, keep, got)
    second = jnp.where(x == 0, got, keep)
    gfc_ref[...] = jnp.concatenate([first[:, :h].T, second[:, :h].T], axis=1)
    both = jnp.concatenate([first[:, h:], second[:, h:]], axis=1)
    top, low = both[:rows, :], both[rows:, :]
    send_ref[...] = jnp.where(c == 0, low, top).astype(BF16)
    hold_ref[...] = jnp.where(c == 0, top, low)


def unpack_ffn_third_kernel(pos_ref, hold_ref, got_ref, gprojt_ref):
    c = pos_ref[1]
    hold, got = hold_ref[...], got_ref[...].astype(F32)
    gprojt_ref[...] = jnp.concatenate(
        [jnp.where(c == 0, hold, got), jnp.where(c == 0, got, hold)], axis=1
    )


def finish_kernel(
    middle_ref,
    act_own_ref,
    act_sib_ref,
    act_far_ref,
    dx1_ref,
    dn1_ref,
    near_ref,
    coming_ref,
    x_ref,
    norms_ref,
    act_ref,
    grad_ref,
):
    act_ref[...] = (middle_ref[...] + total((act_own_ref, act_sib_ref, act_far_ref))).T.astype(BF16)
    dn1 = total((dn1_ref, near_ref, coming_ref))
    xhat, factor = xhat_of(x_ref[...].astype(F32))
    grads = dx1_ref[...] + norm_back(dn1, norms_ref[0:1, :], xhat, factor)
    grad_ref[...] = grads.T.astype(BF16)


def fill_bias(start_ref, bias_ref):
    keys, rows = bias_ref.shape
    key_ids = lax.broadcasted_iota(jnp.int32, (keys, rows), 0)
    row_ids = lax.broadcasted_iota(jnp.int32, (keys, rows), 1) + (keys - rows)
    allowed = (key_ids >= start_ref[...]) & (key_ids <= row_ids)
    bias_ref[...] = jnp.where(allowed, 0.0, NEG)


def head_slices(width):
    pairs = width // (2 * HEAD_DIM)
    return pairs, width - pairs * 2 * HEAD_DIM


def attn_fwd_kernel(
    q_ref,
    k_ref,
    v_ref,
    start_ref,
    x_ref,
    wo_ref,
    norms_ref,
    o_ref,
    lse_ref,
    middle_ref,
    n2_ref,
    qt,
    vt,
    ot,
    bias,
):
    width = q_ref.shape[1]
    fill_bias(start_ref, bias)
    qt[...] = (q_ref[...].astype(F32) * HEAD_DIM ** (-0.5)).T.astype(BF16)
    vt[...] = v_ref[...].astype(F32).T.astype(BF16)
    pairs, rest = head_slices(width)

    def one(keys, queries, values, row, head):
        scores = nn(keys, queries) + bias[...]
        peak = jnp.max(scores, axis=0, keepdims=True)
        terms = jnp.exp(scores - peak)
        summed = jnp.sum(terms, axis=0, keepdims=True)
        ot[pl.ds(row, HEAD_DIM), :] = nn(values, terms.astype(BF16)) / summed
        lse_ref[pl.ds(head, 1), :] = peak + jnp.log(summed)

    def pair(p, _):
        at = pl.multiple_of(p * 128, 128)
        keys = k_ref[:, pl.ds(at, 128)]
        queries = qt[pl.ds(at, 128), :]
        rows = lax.broadcasted_iota(jnp.int32, queries.shape, 0)
        for h in range(2):
            row = pl.multiple_of(at + h * HEAD_DIM, HEAD_DIM)
            one(
                keys,
                jnp.where((rows < HEAD_DIM) == (h == 0), queries, jnp.zeros_like(queries)),
                vt[pl.ds(row, HEAD_DIM), :],
                row,
                2 * p + h,
            )
        return 0

    lax.fori_loop(0, pairs, pair, 0)
    if rest:
        at = pairs * 128
        one(k_ref[:, at:], qt[at:, :], vt[at:, :], at, 2 * pairs)
    o_ref[...] = ot[...].T.astype(BF16)
    middle = x_ref[...].astype(F32) + nn(o_ref[...], wo_ref[...])
    middle_ref[...] = middle
    xhat, _ = xhat_of(middle)
    n2_ref[...] = (xhat * norms_ref[2:3, :] + norms_ref[3:4, :]).astype(BF16)


def attn_bwd_kernel(
    dn2_own_ref,
    dn2_sib_ref,
    dn2_far_ref,
    gz_ref,
    middle_ref,
    norms_ref,
    wo_ref,
    q_ref,
    k_ref,
    v_ref,
    lse_ref,
    start_ref,
    act_ref,
    projt_ref,
    dx1_ref,
    dy_ref,
    sums_ref,
    dq_ref,
    dk_ref,
    dv_ref,
    act_own_ref,
    act_far_ref,
    act_sib_ref,
    act_far_sib_ref,
    do_ref,
    qt,
    dot_s,
    kt,
    dqt,
    bias,
    rows_all,
):
    width = q_ref.shape[1]
    scale = HEAD_DIM ** (-0.5)
    dn2 = total((dn2_own_ref, dn2_sib_ref, dn2_far_ref))
    xhat, factor = xhat_of(middle_ref[...])
    sums_ref[0:1, :] = jnp.sum(dn2 * xhat, axis=0, keepdims=True)
    sums_ref[1:2, :] = jnp.sum(dn2, axis=0, keepdims=True)
    dx1 = gz_ref[...].astype(F32) + norm_back(dn2, norms_ref[2:3, :], xhat, factor)
    dx1_ref[...] = dx1
    dy_ref[...] = dx1.astype(BF16)
    do_ref[...] = nt(dy_ref[...], wo_ref[...]).astype(BF16)
    fill_bias(start_ref, bias)
    qt[...] = (q_ref[...].astype(F32) * scale).T.astype(BF16)
    dot_s[...] = do_ref[...].astype(F32).T.astype(BF16)
    kt[...] = k_ref[...].astype(F32).T.astype(BF16)
    pairs, rest = head_slices(width)

    def one(keys, values, queries_t, douts_t, keys_t, queries, douts, row, head):
        scores = nn(keys, queries_t) + bias[...]
        probs = jnp.exp(scores - lse_ref[pl.ds(head, 1), :])
        dprobs = nn(values, douts_t)
        delta = jnp.sum(probs * dprobs, axis=0, keepdims=True)
        dscores = (probs * (dprobs - delta)).astype(BF16)
        dqt[pl.ds(row, HEAD_DIM), :] = nn(keys_t, dscores)
        return nn(dscores, queries), nn(probs.astype(BF16), douts)

    def scaled(values):
        return (values.astype(F32) * scale).astype(BF16)

    def pair(p, _):
        at = pl.multiple_of(p * 128, 128)
        keys = k_ref[:, pl.ds(at, 128)]
        values = v_ref[:, pl.ds(at, 128)]
        queries = scaled(q_ref[:, pl.ds(at, 128)])
        douts = do_ref[:, pl.ds(at, 128)]
        queries_t = qt[pl.ds(at, 128), :]
        douts_t = dot_s[pl.ds(at, 128), :]
        rows = lax.broadcasted_iota(jnp.int32, queries_t.shape, 0)
        lanes = lax.broadcasted_iota(jnp.int32, queries.shape, 1)
        dk_sum = dv_sum = None
        for h in range(2):
            row = pl.multiple_of(at + h * HEAD_DIM, HEAD_DIM)
            in_rows = (rows < HEAD_DIM) == (h == 0)
            in_lanes = (lanes < HEAD_DIM) == (h == 0)
            zero_t, zero = jnp.zeros_like(queries_t), jnp.zeros_like(queries)
            dk_part, dv_part = one(
                keys,
                values,
                jnp.where(in_rows, queries_t, zero_t),
                jnp.where(in_rows, douts_t, zero_t),
                kt[pl.ds(row, HEAD_DIM), :],
                jnp.where(in_lanes, queries, zero),
                jnp.where(in_lanes, douts, zero),
                row,
                2 * p + h,
            )
            dk_sum = dk_part if h == 0 else dk_sum + dk_part
            dv_sum = dv_part if h == 0 else dv_sum + dv_part
        dk_ref[:, pl.ds(at, 128)] = dk_sum.astype(BF16)
        dv_ref[:, pl.ds(at, 128)] = dv_sum.astype(BF16)
        return 0

    lax.fori_loop(0, pairs, pair, 0)
    if rest:
        at = pairs * 128
        dk_part, dv_part = one(
            k_ref[:, at:],
            v_ref[:, at:],
            qt[at:, :],
            dot_s[at:, :],
            kt[at:, :],
            scaled(q_ref[:, at:]),
            do_ref[:, at:],
            at,
            2 * pairs,
        )
        dk_ref[:, at:] = dk_part.astype(BF16)
        dv_ref[:, at:] = dv_part.astype(BF16)
    dq_ref[...] = (dqt[...].T * scale).astype(BF16)
    tok = q_ref.shape[0]

    def forward(i):
        at = pl.ds(pl.multiple_of(i * tok, tok), tok)
        rows_all[at, :] = nt(act_ref[at, :], projt_ref[...]).astype(BF16)

    repeat(4, True, forward)
    y_refs = (act_own_ref, act_far_ref, act_sib_ref, act_far_sib_ref)
    for y_ref, at in zip(y_refs, members_of(tok)):
        y_ref[...] = rows_all[at, :]


def xhat_of(values):
    center = jnp.mean(values, axis=-1, keepdims=True)
    centered = values - center
    variance = jnp.mean(centered * centered, axis=-1, keepdims=True)
    factor = lax.rsqrt(variance + EPS)
    return centered * factor, factor


def norm_back(grads, gain, xhat, factor):
    e = grads * gain
    return factor * (
        e
        - jnp.mean(e, axis=-1, keepdims=True)
        - xhat * jnp.mean(e * xhat, axis=-1, keepdims=True)
    )


def add(*terms):
    acc = terms[0].astype(F32)
    for term in terms[1:]:
        acc = acc + term.astype(F32)
    return acc


def segment_starts(dealt_lengths, seq_order, first_row, rows):
    lengths = dealt_lengths[0].reshape(-1)
    order = seq_order[0]
    count = lengths.shape[0]
    arrival = jnp.arange(count, dtype=jnp.int32)
    before = (order[:, None] < arrival[None, :]).astype(jnp.int32)
    begins = jnp.sum(before * lengths[:, None], axis=0)
    ids = first_row + jnp.arange(rows, dtype=jnp.int32)
    reached = begins[:, None] <= ids[None, :]
    return jnp.max(jnp.where(reached, begins[:, None], 0), axis=0)


def tiled(value):
    if value.ndim == 2 and value.shape[0] % 128 == 0 and value.shape[1] % 128:
        return value.reshape(value.shape[0] // 8, 8, value.shape[1])
    return value


def barrier(value, fence):
    leaves, tree = jax.tree.flatten(value)
    kept = lax.optimization_barrier(([tiled(v) for v in leaves], fence))[0]
    return tree.unflatten([k.reshape(v.shape) for k, v in zip(kept, leaves)])


def permute(value, axis, pairs):
    return lax.ppermute(tiled(value), axis, pairs).reshape(value.shape)


class Clock:
    def __init__(self):
        self.fence = ()

    def __call__(self, value):
        if not self.fence:
            return value
        return barrier(value, self.fence)

    def tick(self, *done):
        self.fence = tuple(tiled(v) for v in jax.tree.leaves(done))


def per_device(
    tokens,
    qkv_weight,
    out_weight,
    fc_weight,
    proj_weight,
    norm_params,
    grad_out,
    dealt_lengths,
    seq_order,
):
    n_dp, n_f = lax.axis_size("dp"), lax.axis_size("fsdp")
    n_y, n_z = n_dp // 2, n_f // 2
    dp, f = lax.axis_index("dp"), lax.axis_index("fsdp")
    x, c = dp & 1, f & 1
    pos = jnp.stack([x, c, dp, f]).astype(jnp.int32)
    tok, width = tokens.shape
    seq_longest = n_f * tok // dealt_lengths.shape[1] // 2
    halo = -(-seq_longest // tok)
    halo += halo % 2

    now = Clock()

    def run(*args, **kwargs):
        made = call(*args, **kwargs)
        return lambda *operands: made(*now(operands))

    def xor(value, axis, bits):
        size = n_dp if axis == "dp" else n_f
        return permute(now(value), axis, [(i, i ^ bits) for i in range(size)])

    def to_core(value):
        return xor(value, "fsdp", 1)

    def to_x(value):
        return xor(value, "dp", 1)

    def to_y(value, k):
        return xor(value, "dp", 2 * k)

    def to_z(value, k):
        return xor(value, "fsdp", 2 * k)

    def along_z(value, step, senders):
        pairs = [(2 * z + i, 2 * (z + step) + i) for z in senders for i in range(2)]
        return permute(now(value), "fsdp", pairs)

    def joined(*values):
        return jnp.concatenate(values, axis=0)

    z_at = f >> 1
    others_z, others_y = range(1, n_z), range(1, n_y)

    def by_z(choose):
        choices = [choose(z) for z in range(n_z)]
        value = choices[0]
        for z in range(1, n_z):
            if choices[z] is not choices[z - 1]:
                value = jnp.where(z_at >= z, choices[z], value)
        return value

    k_rows, nq = qkv_weight.shape
    no = out_weight.shape[1]
    half, wide = k_rows // 2, 2 * (nq + no)
    rows = (half // 2 + 7) // 8 * 8
    own_first, own_second = run(pack_attn_kernel, [((rows, wide), BF16)] * 2, [VM, VM])(
        qkv_weight, out_weight.T
    )
    now.tick(own_first, own_second)

    firsts = [own_first] + [to_z(own_first, dz) for dz in others_z]
    ff_half = fc_weight.shape[1] // 2
    sub = proj_weight.shape[0] // 4
    send, keep = run(
        pack_ffn_first_kernel, [((ff_half, k_rows + sub), BF16)] * 2, [SM, VM, VM])(pos, fc_weight, proj_weight.T)
    got = to_x(send)
    norm_x = to_x(norm_params)
    now.tick(firsts, got, norm_x)

    stack = {(0, 0, 0): jnp.stack(firsts)}
    seconds = [own_second] + [to_z(own_second, dz) for dz in others_z]
    for dy in others_y:
        stack[0, dy, 0] = to_y(stack[0, 0, 0], dy)
    stack[0, 0, 1] = to_x(stack[0, 0, 0])
    fct, send, hold = run(
        pack_ffn_second_kernel,
        [((ff_half, 2 * k_rows), BF16)] + [((no, 2 * sub), BF16)] * 2,
        [SM, VM, VM])(pos, keep, got)
    now.tick(seconds, stack, send)

    got = to_core(send)
    norm_pairs = jnp.stack([norm_params, norm_x])
    norm_pairs = [norm_pairs] + [to_y(norm_pairs, dy) for dy in others_y]
    stack[1, 0, 0] = jnp.stack(seconds)
    stack[1, 0, 1] = to_x(stack[1, 0, 0])
    for dy in others_y:
        stack[1, dy, 0] = to_y(stack[1, 0, 0], dy)
    even = [tokens]
    for _ in range(halo // 2):
        even.append(along_z(even[-1], 1, range(n_z - 1)))
    stacks, arrays = [], []

    def cross(*keys):
        stacks.extend([(key + (0,),) for key in keys])
        arrays.extend(stack[key] for key in keys)
        stacks.append(tuple(key + (1,) for key in keys))
        arrays.append(to_core(joined(*[stack[key] for key in keys])))

    cross((0, 0, 0), *[(0, dy, 0) for dy in others_y])
    (own_ffn,) = run(
        pack_ffn_third_kernel, [((ff_half, 2 * (k_rows + sub)), BF16)], [SM, VM, VM, VM])(pos, fct, hold, got)
    now.tick(stack, even[-1], arrays[-1], own_ffn, norm_pairs)

    ups, downs, ffn = [own_ffn], [own_ffn], {(0, 0): own_ffn}

    def ffn_over_z(t):
        ups.append(along_z(ups[-1], 1, range(t - 1, n_z - 1)))
        downs.append(along_z(downs[-1], -1, range(1, n_z - t + 1)))

    def pick(t):
        return by_z(lambda z: ups[z - (z ^ t)] if z ^ t < z else downs[(z ^ t) - z])

    for dy in others_y:
        stack[0, dy, 1] = to_x(stack[0, dy, 0])
        stack[1, dy, 1] = to_y(stack[1, 0, 1], dy)
    rows_before = []
    for distance in range(1, halo + 1):
        if distance % 2:
            near = distance // 2
            rows_before.append(to_core(jnp.where(c == 0, even[near], even[near + 1])))
        else:
            rows_before.append(even[distance // 2])
    x_rows = joined(*rows_before[::-1], tokens)
    cross((0, 0, 1), (1, 0, 0), (1, 0, 1), *[(1, dy, 0) for dy in others_y])
    norms = jnp.concatenate(
        [
            sum(
                jnp.where((dp ^ r) == j, norm_pairs[r >> 1][r & 1].astype(F32), 0.0)
                for r in range(n_dp)
            )
            for j in range(n_dp)
        ],
        axis=1,
    )
    xhat_one, factor_one = xhat_of(x_rows.astype(F32))
    normed = (xhat_one * norms[0] + norms[1]).astype(BF16)
    now.tick(arrays[-1], stack, normed)

    cross(*[(part, dy, 1) for dy in others_y for part in range(2)])
    now.tick(arrays[-1])
    ffn_over_z(1)
    for dy in others_y:
        ffn[dy, 0] = to_y(own_ffn, dy)
    gz_far = to_x(grad_out)
    gz_sib = to_core(grad_out)
    square = ((width, width), BF16)
    dims = (n_dp, n_f, nq, no)
    wq, wk, wv, wo = run(
        functools.partial(assemble_attn_kernel, stacks, dims),
        [square] * 4,
        [SM] + [ANY] * len(arrays),
        [
            pltpu.VMEM((2, n_dp * n_f, rows, wide), BF16),
            pltpu.SemaphoreType.DMA((2 * n_dp * n_f,)),
        ])(pos, *arrays)
    now.tick(wq, wk, wv, wo, ups, downs, ffn, gz_far, gz_sib)

    ffn[0, 1] = pick(1)
    ffn_over_z(2)
    for dy in others_y:
        ffn[dy, 1] = to_y(ffn[0, 1], dy)
    gz_far_sib = to_core(gz_far)
    queries, all_keys, values = run(
        qkv_kernel, [((tok, width), BF16)] + [(normed.shape, BF16)] * 2, [VM] * 4)(normed, wq, wk, wv)
    now.tick(queries, all_keys, values, ups, downs, ffn, gz_far_sib)

    ffn[0, 2] = pick(2)
    for t in others_z[2:]:
        ffn_over_z(t)
    for dy in others_y:
        ffn[dy, 2] = to_y(ffn[0, 2], dy)
    span = (halo + 1) * tok
    starts = segment_starts(dealt_lengths, seq_order, f * tok, tok) - (f - halo) * tok
    starts = starts.reshape(1, tok).astype(jnp.int32)
    heads = width // HEAD_DIM
    attended, lse, middle, normed_two = run(
        attn_fwd_kernel,
        [((tok, width), BF16), ((heads, tok), F32), ((tok, width), F32), ((tok, width), BF16)],
        [VM] * 7,
        [
            pltpu.VMEM((width, tok), BF16),
            pltpu.VMEM((width, span), BF16),
            pltpu.VMEM((width, tok), F32),
            pltpu.VMEM((span, tok), F32),
        ])(queries, all_keys, values, starts, tokens, wo, norms)
    now.tick(attended, lse, middle, normed_two, ups, downs, ffn)

    n2_far = to_x(normed_two)
    n2_sib = to_core(normed_two)
    for t in others_z[2:]:
        ffn[0, t] = pick(t)
        for dy in others_y:
            ffn[dy, t] = to_y(ffn[0, t], dy)
    now.tick(n2_far, n2_sib, ffn)
    n2_far_sib = to_core(n2_far)
    n2_rows = [normed_two, n2_far, n2_sib, n2_far_sib]
    gz_rows = [grad_out, gz_far, gz_sib, gz_far_sib]

    ffn_keys = sorted(ffn)
    fct_full, projt_full = run(
        functools.partial(assemble_ffn_kernel, ffn_keys, (n_y, n_z)),
        [((n_z * ff_half, n_y * 2 * k_rows), BF16), ((n_z * 2 * no, n_y * 2 * sub), BF16)],
        [SM] + [ANY] * len(ffn_keys),
        [
            pltpu.VMEM((len(ffn_keys),) + own_ffn.shape, BF16),
            pltpu.SemaphoreType.DMA((len(ffn_keys),)),
        ])(pos, *[ffn[key] for key in ffn_keys])
    ff = fct_full.shape[0]
    rows_all = pltpu.VMEM((4 * tok, width), BF16)
    activated, dhidden, own, far, sib, far_sib = run(
        ffn_kernel,
        [((4 * tok, ff), BF16)] * 2 + [((tok, width), BF16)] * 4,
        [VM] * 10,
        [rows_all] * 3,
    )(*n2_rows, *gz_rows, fct_full, projt_full)
    now.tick(activated, dhidden, own, far, sib, far_sib)
    far = add(far, to_core(far_sib)).astype(BF16)
    now.tick(far)

    dn2_far = to_x(far)
    dn2_sib = to_core(sib)
    (ffn_grads,) = run(
        functools.partial(ffn_grads_kernel, (n_y, n_z)),
        [((n_y * n_z,) + own_ffn.shape, BF16)],
        [SM] + [VM] * 10,
        [
            pltpu.VMEM((n_z * ff_half, 4 * tok), BF16),
            pltpu.VMEM((width, 4 * tok), BF16),
            pltpu.VMEM((4 * tok, width), BF16),
        ])(pos, dhidden, *n2_rows, *gz_rows, activated)
    now.tick(ffn_grads, dn2_far, dn2_sib)

    part_of = {}
    far_y = {
        dz: [to_y(ffn_grads[dy * n_z + dz], dy) for dy in others_y] for dz in others_z[::-1][:-1]
    }
    big, small = (span, width), (tok, width)
    dx1, dy_low, norm_sums, dq, dk, dv, act_own, act_far, act_sib, act_far_sib = run(
        attn_bwd_kernel,
        [(small, F32), (small, BF16), ((2, width), F32), (small, BF16), (big, BF16), (big, BF16)]
        + [(small, BF16)] * 4,
        [VM] * 14,
        [
            pltpu.VMEM(small, BF16),
            pltpu.VMEM((width, tok), BF16),
            pltpu.VMEM((width, tok), BF16),
            pltpu.VMEM((width, span), BF16),
            pltpu.VMEM((width, tok), F32),
            pltpu.VMEM((span, tok), F32),
            rows_all,
        ])(own, dn2_sib, dn2_far, grad_out, middle, norms, wo, queries, all_keys, values, lse, starts, activated, projt_full)
    now.tick(dq, dk, dv, far_y, act_own, act_far, act_sib, act_far_sib)

    carry = [None, None]

    def ffn_back_z(s):
        reach = n_z - s
        for way, (step, senders) in enumerate(
            ((1, range(0, s)), (-1, range(n_z - s, n_z)))
        ):
            value = by_z(
                lambda z: part_of[z ^ (z + step * reach)]
                if 0 <= z + step * reach < n_z
                else part_of[n_z - 1]
            )
            if carry[way] is not None:
                value = add(value, carry[way]).astype(BF16)
            carry[way] = along_z(value, step, senders)

    next_y = [to_y(ffn_grads[dy * n_z + 1], dy) for dy in others_y]
    act_far_sib = to_core(act_far_sib)
    count = 2 * n_y * n_z
    block = ((count, rows, wide), BF16)
    keeps, sent, gots = {}, {}, {}
    keeps[0], sent[0], keeps[1], sent[1] = run(
        functools.partial(attn_grads_kernel, dims),
        [block] * 4,
        [SM] + [VM] * 6,
        [pltpu.VMEM((width, span), BF16), pltpu.VMEM((width, tok), BF16)],
    )(pos, normed, attended, dq, dk, dv, dy_low)
    now.tick(keeps, sent, next_y, act_far_sib)

    gots[1], gots[0] = to_core(sent[1]), to_core(sent[0])
    act_sib = to_core(act_sib)
    for dz, pieces in now(far_y).items():
        part_of[dz] = add(ffn_grads[dz], *pieces).astype(BF16)
    ffn_back_z(1)

    def core_sum(part, dy, dx, count=1):
        at = (part * n_y + dy) * n_z
        stop = at + count * n_z
        return add(keeps[dx][at:stop], gots[dx][at:stop])

    x_send = core_sum(0, 0, 1, n_y).astype(BF16)
    y_send = [core_sum(1, dy, 1).astype(BF16) for dy in others_y]
    now.tick(x_send, y_send, gots, act_sib)

    last_y = [to_y(ffn_grads[dy * n_z], dy) for dy in others_y]
    got_x = to_x(x_send)
    got_y = [to_y(value, dy) for dy, value in zip(others_y, y_send)]
    for s in range(2, n_z - 1):
        ffn_back_z(s)
    cut = halo * tok
    dn1, dn1_halo, norm_first = run(
        dn1_kernel, [(small, F32), ((cut, width), BF16), ((2, width), F32)], [VM] * 7
    )(dq, dk, dv, wq, wk, wv, x_rows)
    norm_rows = -(-4 * width // wide // 8) * 8

    def with_norms(value, norms):
        extra = norms.astype(BF16).reshape(-1, wide)
        extra = jnp.pad(extra, ((0, norm_rows - extra.shape[0]), (0, 0)))
        extra = jnp.broadcast_to(extra, value.shape[:-2] + extra.shape)
        return jnp.concatenate([value, extra], axis=-2)

    def norms_of(value):
        return value[0, -norm_rows:][: 4 * width // wide].reshape(4, width).astype(F32)

    now.tick(got_x, got_y, carry, dn1, dn1_halo, norm_first, last_y)
    got_x, got_y, dn1, dn1_halo, norm_first, last_y, next_y, act_far_sib = now(
        (got_x, got_y, dn1, dn1_halo, norm_first, last_y, next_y, act_far_sib)
    )
    part_of[1] = add(ffn_grads[1], *next_y).astype(BF16)
    part_of[0] = add(ffn_grads[0], *last_y).astype(BF16)

    norm_grads = joined(norm_first, norm_sums)
    first_x = [got_x[dy * n_z : (dy + 1) * n_z] for dy in range(n_y)]
    both = []
    for dy in others_y:
        value = [add(core_sum(0, dy, 0), first_x[dy]), core_sum(1, dy, 0)]
        value = jnp.concatenate([v.astype(BF16) for v in value], axis=1)
        both.append(to_y(with_norms(value, norm_grads), dy))
    act_far = add(act_far, act_far_sib).astype(BF16)
    second_x = add(core_sum(1, 0, 1), *got_y).astype(BF16)
    got_x = to_x(joined(second_x.reshape(-1, wide), act_far.reshape(-1, wide)))
    if n_z > 2:
        ffn_back_z(n_z - 1)
    def back(distance):
        return dn1_halo[cut - distance * tok : cut - (distance - 1) * tok]

    carried = [None] * (halo // 2 + 1)
    for near in range(halo // 2):
        got = to_core(back(2 * near + 1)).astype(F32)
        for level, wanted in ((near, 1), (near + 1, 0)):
            term = jnp.where(c != wanted, got, 0.0)
            carried[level] = term if carried[level] is None else carried[level] + term
    outgoing = [back(2 * level).astype(F32) + carried[level] for level in range(1, halo // 2 + 1)]
    coming = None
    for level in range(halo // 2, 0, -1):
        out = outgoing[level - 1]
        if coming is not None:
            out = out + coming
        coming = along_z(out.astype(BF16), -1, range(1, n_z)).astype(F32)
    now.tick(got_x, both, carry, coming)
    got_x, both, coming = now((got_x, both, coming))
    act_far = got_x[n_z * rows :].reshape(small)
    second_x = got_x[: n_z * rows].reshape(n_z, rows, wide)
    send, keep = run(
        unpack_ffn_first_kernel,
        [((ff_half, k_rows + sub), BF16), ((ff_half, k_rows + sub), F32)],
        [SM] + [VM] * 3,
    )(pos, part_of[0], *carry)
    norm_grads = norm_grads + sum(norms_of(value) for value in both)
    first_sum = add(core_sum(0, 0, 0), first_x[0], *[value[:, :rows] for value in both])
    second_sum = add(
        core_sum(1, 0, 0), second_x, *[value[:, rows : 2 * rows] for value in both]
    )
    sums = jnp.concatenate([first_sum.astype(BF16), second_sum.astype(BF16)], axis=1)
    sums = with_norms(sums, norm_grads)
    now.tick(sums)

    got = to_x(send)
    parts = [sums[0]] + [to_z(sums[dz], dz) for dz in others_z]
    activations, input_grad = run(finish_kernel, [((width, tok), BF16)] * 2, [VM] * 10)(
        middle,
        act_own,
        act_sib,
        act_far,
        dx1,
        dn1,
        carried[0].astype(BF16),
        coming.astype(BF16),
        tokens,
        norms,
    )
    grad_fc, send, hold = run(
        unpack_ffn_second_kernel,
        [(fc_weight.shape, F32), ((no, 2 * sub), BF16), ((no, 2 * sub), F32)],
        [SM, VM, VM])(pos, keep, got)
    (grad_proj,) = run(unpack_ffn_third_kernel, [(proj_weight.shape[::-1], F32)], [SM, VM, VM])(
        pos, hold, to_core(send)
    )
    parts = barrier(parts, (grad_fc, grad_proj, activations, input_grad))
    norm_grads = sum(norms_of(part[None]) for part in parts)
    norm_grads = norm_grads + lax.ppermute(norm_grads, "fsdp", [(i, i ^ 1) for i in range(n_f)])
    norm_grads = norm_grads + lax.ppermute(norm_grads, "dp", [(i, i ^ 1) for i in range(n_dp)])
    norm_grads = lax.dynamic_slice_in_dim(norm_grads, dp * k_rows, k_rows, axis=1)
    grad_qkv, grad_attn_out = run(
        functools.partial(unpack_attn_kernel, n_z, rows),
        [(qkv_weight.shape, F32), (out_weight.shape[::-1], F32)],
        [VM] * n_z,
        [pltpu.VMEM(out_weight.shape, F32)],
    )(*parts)
    return (activations.T, input_grad.T, grad_qkv, grad_attn_out.T, grad_fc, grad_proj.T, norm_grads)


def solution(mesh):
    in_specs = (
        P(("dp", "fsdp"), None),
        P("dp", "fsdp"),
        P("dp", "fsdp"),
        P("dp", "fsdp"),
        P("dp", "fsdp"),
        P(None, "dp"),
        P(("dp", "fsdp"), None),
        P("dp", None, None),
        P("dp", None),
    )
    out_specs = (
        P(("dp", "fsdp"), None),
        P(("dp", "fsdp"), None),
        P("dp", "fsdp"),
        P("dp", "fsdp"),
        P("dp", "fsdp"),
        P("dp", "fsdp"),
        P(None, "dp"),
    )
    return jax.shard_map(
        per_device, mesh=mesh, in_specs=in_specs, out_specs=out_specs, check_vma=False
    )
```

```python
import functools
import math

import jax
import jax.numpy as jnp
from jax import lax
from jax.experimental import pallas as pl
from jax.experimental.pallas import tpu as pltpu
from jax.sharding import PartitionSpec as P

HEAD_DIM = 64
EPS = 1e-05
NEG = -1e30
F32 = jnp.float32
BF16 = jnp.bfloat16
VMEM_ALL = 60 * 2**20

ANY = pl.BlockSpec(memory_space=pl.ANY)
VM = pl.BlockSpec(memory_space=pltpu.VMEM)
SM = pl.BlockSpec(memory_space=pltpu.SMEM)


def call(kernel, outs, in_specs, scratch=()):
    return pl.pallas_call(
        kernel,
        name=getattr(kernel, "func", kernel).__name__,
        out_shape=tuple(jax.ShapeDtypeStruct(s, d) for s, d in outs),
        in_specs=list(in_specs),
        out_specs=tuple(VM for _ in outs),
        scratch_shapes=list(scratch),
        compiler_params=pltpu.CompilerParams(vmem_limit_bytes=VMEM_ALL),
        cost_estimate=pl.CostEstimate(flops=0, bytes_accessed=0, transcendentals=0),
    )


def dot(a, b, ca, cb):
    return lax.dot_general(a, b, (((ca,), (cb,)), ((), ())), preferred_element_type=F32)


def nn(a, b):
    return dot(a, b, 1, 0)


def nt(a, b):
    return dot(a, b, 1, 1)


def tn(a, b):
    return dot(a, b, 0, 0)


def repeat(count, looped, body):
    if not looped:
        for i in range(count):
            body(i)
        return

    def step(i, carry):
        body(i)
        return carry

    lax.fori_loop(0, count, step, 0)


def split_cols(lo, hi, width):
    pieces = []
    while lo < hi:
        which, start = divmod(lo, width)
        stop = min(width, start + hi - lo)
        pieces.append((which, start, stop))
        lo += stop - start
    return pieces


def pack_attn_kernel(wq_ref, wo_ref, first_ref, second_ref):
    half = wq_ref.shape[0] // 2
    rows = first_ref.shape[0]
    wo = wo_ref[...].astype(F32).T.astype(BF16)
    for out_ref, row in ((first_ref, 0), (second_ref, half - rows)):
        vals = []
        for h in range(2):
            at = h * half + row
            vals += [wq_ref[at : at + rows, :], wo[at : at + rows, :]]
        out_ref[...] = jnp.concatenate(vals, axis=1)


def pack_ffn_first_kernel(pos_ref, fc_ref, projt_ref, send_ref, keep_ref):
    x = pos_ref[0]
    half = fc_ref.shape[1] // 2
    sub = projt_ref.shape[1] // 4
    sides = []
    for h in range(2):
        fct = fc_ref[:, h * half : (h + 1) * half].astype(F32).T
        projt = [
            projt_ref[:, (2 * s + h) * sub : (2 * s + h + 1) * sub].astype(F32) for s in range(2)
        ]
        sides.append(jnp.concatenate([fct, jnp.concatenate(projt, axis=0)], axis=1))
    send_ref[...] = jnp.where(x == 0, sides[1], sides[0]).astype(BF16)
    keep_ref[...] = jnp.where(x == 0, sides[0], sides[1]).astype(BF16)


def pack_ffn_second_kernel(pos_ref, keep_ref, got_ref, fct_ref, send_ref, hold_ref):
    x, c = pos_ref[0], pos_ref[1]
    keep, got = keep_ref[...], got_ref[...]
    first = jnp.where(x == 0, keep, got)
    second = jnp.where(x == 0, got, keep)
    k = fct_ref.shape[1] // 2
    rows = send_ref.shape[0]
    fct_ref[...] = jnp.concatenate([first[:, :k], second[:, :k]], axis=1)
    projt = jnp.concatenate([first[:, k:], second[:, k:]], axis=1)
    top, low = projt[:rows, :], projt[rows:, :]
    send_ref[...] = jnp.where(c == 0, low, top)
    hold_ref[...] = jnp.where(c == 0, top, low)


def pack_ffn_third_kernel(pos_ref, fct_ref, hold_ref, got_ref, out_ref):
    c = pos_ref[1]
    hold, got = hold_ref[...], got_ref[...]
    top = jnp.where(c == 0, hold, got)
    low = jnp.where(c == 0, got, hold)
    projt = jnp.concatenate([top, low], axis=0)
    out_ref[...] = jnp.concatenate([fct_ref[...], projt], axis=1)


def place(pieces, buf, sem, slots):
    copies = [
        pltpu.make_async_copy(piece, buf.at[slot], sem.at[i])
        for i, (piece, slot) in enumerate(zip(pieces, slots))
    ]
    for copy in copies:
        copy.start()
    for copy in copies:
        copy.wait()


def assemble_attn_kernel(stacks, dims, pos_ref, *refs):
    n_dp, n_f, nq, no = dims
    n_z = n_f // 2
    ins = refs[: len(stacks)]
    w_refs = refs[len(stacks) : len(stacks) + 3]
    wo_ref, buf, sem = refs[len(stacks) + 3 :]
    dp, f = pos_ref[2], pos_ref[3]
    copies = []
    for ref, groups in zip(ins, stacks):
        for i, (part, dy, dx, dc) in enumerate(groups):
            for dz in range(n_z):
                slot = (dp ^ (2 * dy + dx)) * n_f + (f ^ (2 * dz + dc))
                copies.append(
                    pltpu.make_async_copy(
                        ref.at[i * n_z + dz], buf.at[part, slot], sem.at[len(copies)]
                    )
                )
    for copy in copies:
        copy.start()
    for copy in copies:
        copy.wait()
    rows = buf.shape[2]
    wide = nq + no
    width = wo_ref.shape[1]
    half = width // n_dp // 2
    for d in range(n_dp):
        for h in range(2):
            base = h * wide
            for part, skip in ((0, 0), (1, 2 * rows - half)):
                row = (2 * d + h) * half + part * rows
                stop = row + rows - skip
                for third in range(3):
                    vals = [
                        buf[part, d * n_f + which][skip:, base + lo : base + hi]
                        for which, lo, hi in split_cols(third * width, (third + 1) * width, nq)
                    ]
                    w_refs[third][row:stop, :] = jnp.concatenate(vals, axis=1)
                wo_ref[row:stop, :] = jnp.concatenate(
                    [
                        buf[part, d * n_f + g][skip:, base + nq : base + wide]
                        for g in range(n_f)
                    ],
                    axis=1,
                )


def assemble_ffn_kernel(keys, dims, pos_ref, *refs):
    n_y, n_z = dims
    pieces = refs[: len(keys)]
    fct_ref, projt_ref, buf, sem = refs[len(keys) :]
    dp, f = pos_ref[2], pos_ref[3]
    slots = [((dp >> 1) ^ dy) * n_z + ((f >> 1) ^ dz) for dy, dz in keys]
    place(pieces, buf, sem, slots)
    rows, wide = buf.shape[1:]
    half = wide // 2
    for z in range(n_z):
        vals = [buf[y * n_z + z] for y in range(n_y)]
        fct_ref[z * rows : (z + 1) * rows, :] = jnp.concatenate(
            [v[:, :half] for v in vals], axis=1
        )
        projt_ref[z * rows : (z + 1) * rows, :] = jnp.concatenate(
            [v[:, half:] for v in vals], axis=1
        )


def attn_grads_kernel(dims, pos_ref, *refs):
    n_dp, n_f, nq, no = dims
    n_z = n_f // 2
    c, dp, f = pos_ref[1], pos_ref[2], pos_ref[3]
    n1_ref, ob_ref, dq_ref, dk_ref, dv_ref, dy_ref = refs[:6]
    outs_by_x, (n1t, obt) = (refs[6:8], refs[8:10]), refs[10:]
    n1t[...] = n1_ref[...].astype(F32).T.astype(BF16)
    obt[...] = ob_ref[...].astype(F32).T.astype(BF16)
    width = n1t.shape[0]
    k_rows = width // n_dp
    half = k_rows // 2
    rows = refs[6].shape[1]
    own = n1t.shape[1] - dq_ref.shape[0]

    def one(dy, dx):
        keep_ref, send_ref = outs_by_x[dx]
        at = pl.ds(((2 * dy + dx) ^ dp) * k_rows, k_rows)
        left = n1t[at, :]
        parts = [
            nn(left[:, own:], dq_ref[...]).astype(BF16),
            nn(left, dk_ref[...]).astype(BF16),
            nn(left, dv_ref[...]).astype(BF16),
        ]
        outs = nn(obt[at, :], dy_ref[...]).astype(BF16)
        for k in range(n_z):
            for part in range(2):
                both = []
                for g in (2 * k, 2 * k + 1):
                    vals = []
                    for h in range(2):
                        row = h * half + part * (half - rows)
                        for which, lo, hi in split_cols(g * nq, (g + 1) * nq, width):
                            vals.append(parts[which][row : row + rows, lo:hi])
                        vals.append(outs[row : row + rows, g * no : (g + 1) * no])
                    both.append(jnp.concatenate(vals, axis=1))
                slot = (part * n_dp // 2 + dy) * n_z + ((f >> 1) ^ k)
                keep_ref[slot] = jnp.where(c == 0, both[0], both[1])
                send_ref[slot] = jnp.where(c == 0, both[1], both[0])

    for dx in range(2):
        repeat(n_dp // 2, k_rows % 16 == 0, functools.partial(one, dx=dx))


def qkv_kernel(n1_ref, wq_ref, wk_ref, wv_ref, q_ref, k_ref, v_ref):
    tok = q_ref.shape[0]
    first = n1_ref.shape[0] - tok
    q_ref[...] = nn(n1_ref[first:, :], wq_ref[...]).astype(BF16)

    def one(i):
        at = pl.ds(pl.multiple_of(i * tok, tok), tok)
        k_ref[at, :] = nn(n1_ref[at, :], wk_ref[...]).astype(BF16)
        v_ref[at, :] = nn(n1_ref[at, :], wv_ref[...]).astype(BF16)

    repeat(n1_ref.shape[0] // tok, True, one)


def dn1_kernel(
    dq_ref, dk_ref, dv_ref, wq_ref, wk_ref, wv_ref, x_ref, own_ref, halo_ref, sums_ref
):
    tok = dq_ref.shape[0]
    cut = halo_ref.shape[0]
    sums_ref[...] = jnp.zeros(sums_ref.shape, F32)

    def tally(grads, at):
        xhat, _ = xhat_of(x_ref[at, :].astype(F32))
        sums_ref[0:1, :] += jnp.sum(grads * xhat, axis=0, keepdims=True)
        sums_ref[1:2, :] += jnp.sum(grads, axis=0, keepdims=True)

    def rows_of(at):
        return nt(dk_ref[at, :], wk_ref[...]) + nt(dv_ref[at, :], wv_ref[...])

    def step(r, carry):
        at = pl.ds(pl.multiple_of(r * tok, tok), tok)
        grads = rows_of(at)
        halo_ref[at, :] = grads.astype(BF16)
        tally(grads, at)
        return carry

    lax.fori_loop(0, cut // tok, step, 0)
    last = pl.ds(cut, tok)
    grads = nt(dq_ref[...], wq_ref[...]) + rows_of(last)
    own_ref[...] = grads
    tally(grads, last)


def members_of(tok):
    return [slice(i * tok, (i + 1) * tok) for i in range(4)]


def ffn_kernel(*refs):
    n2_refs, gz_refs = refs[:4], refs[4:8]
    fct_ref, projt_ref, act_ref, dh_ref = refs[8:12]
    dn2_refs = refs[12:16]
    n2s, gzs, dn2s = refs[16:]
    tok = n2_refs[0].shape[0]
    for i, at in enumerate(members_of(tok)):
        n2s[at, :] = n2_refs[i][...]
        gzs[at, :] = gz_refs[i][...]

    def one(i):
        at = pl.ds(pl.multiple_of(i * tok, tok), tok)
        hidden = nt(n2s[at, :], fct_ref[...])
        cdf = 0.5 * (1.0 + lax.erf(hidden * math.sqrt(0.5)))
        act_ref[at, :] = (hidden * cdf).astype(BF16)
        slope = cdf + hidden * jnp.exp(-0.5 * hidden * hidden) * (1.0 / math.sqrt(2.0 * math.pi))
        dh_ref[at, :] = (nn(gzs[at, :], projt_ref[...]) * slope).astype(BF16)
        dn2s[at, :] = nn(dh_ref[at, :], fct_ref[...]).astype(BF16)

    repeat(4, True, one)
    for dn2_ref, at in zip(dn2_refs, members_of(tok)):
        dn2_ref[...] = dn2s[at, :]


def ffn_grads_kernel(dims, pos_ref, dh_ref, *refs):
    n2_refs, gz_refs = refs[:4], refs[4:8]
    act_ref, out_ref, dht, gzt, n2_ref = refs[8:]
    n_y, n_z = dims
    tok = n2_refs[0].shape[0]
    dp, f = pos_ref[2], pos_ref[3]
    rows, wide = out_ref.shape[1:]
    half = wide // 2
    dht[...] = dh_ref[...].astype(F32).T.astype(BF16)
    for i in range(4):
        at = slice(i * tok, (i + 1) * tok)
        gzt[:, at] = gz_refs[i][...].astype(F32).T.astype(BF16)
        n2_ref[at, :] = n2_refs[i][...]

    def one(z):
        at = pl.ds(z * rows, rows)
        gfc = nn(dht[at, :], n2_ref[...]).astype(BF16)
        gproj = nn(gzt[at, :], act_ref[...]).astype(BF16)
        for y in range(n_y):
            slot = ((dp >> 1) ^ y) * n_z + ((f >> 1) ^ z)
            lanes = slice(y * half, (y + 1) * half)
            out_ref[slot] = jnp.concatenate([gfc[:, lanes], gproj[:, lanes]], axis=1)

    repeat(n_z, rows % 16 == 0, one)


def total(refs):
    acc = refs[0][...].astype(F32)
    for ref in refs[1:]:
        acc = acc + ref[...].astype(F32)
    return acc


def unpack_attn_kernel(count, rows, *refs):
    gq_ref, got_ref, go_ref = refs[count:]
    half = gq_ref.shape[0] // 2
    nq, no = gq_ref.shape[1], go_ref.shape[1]
    for part in range(2):
        summed = total([ref.at[part * rows : (part + 1) * rows] for ref in refs[:count]])
        skip = part * (2 * rows - half)
        for h in range(2):
            base = h * (nq + no)
            row = h * half + part * rows
            stop = row + rows - skip
            gq_ref[row:stop, :] = summed[skip:, base : base + nq]
            go_ref[row:stop, :] = summed[skip:, base + nq : base + nq + no]
    got_ref[...] = go_ref[...].T


def unpack_ffn_first_kernel(pos_ref, own_ref, up_ref, down_ref, send_ref, keep_ref):
    x, f = pos_ref[0], pos_ref[3]
    up = jnp.where(f >= 2, up_ref[...].astype(F32), 0.0)
    summed = own_ref[...].astype(F32) + up + down_ref[...].astype(F32)
    q = summed.shape[1] // 4
    first = jnp.concatenate([summed[:, :q], summed[:, 2 * q : 3 * q]], axis=1)
    second = jnp.concatenate([summed[:, q : 2 * q], summed[:, 3 * q :]], axis=1)
    send_ref[...] = jnp.where(x == 0, second, first).astype(BF16)
    keep_ref[...] = jnp.where(x == 0, first, second)


def unpack_ffn_second_kernel(pos_ref, keep_ref, got_ref, gfc_ref, send_ref, hold_ref):
    x, c = pos_ref[0], pos_ref[1]
    keep, got = keep_ref[...], got_ref[...].astype(F32)
    h = keep.shape[1] // 2
    rows = keep.shape[0] // 2
    first = jnp.where(x == 0, keep, got)
    second = jnp.where(x == 0, got, keep)
    gfc_ref[...] = jnp.concatenate([first[:, :h].T, second[:, :h].T], axis=1)
    both = jnp.concatenate([first[:, h:], second[:, h:]], axis=1)
    top, low = both[:rows, :], both[rows:, :]
    send_ref[...] = jnp.where(c == 0, low, top).astype(BF16)
    hold_ref[...] = jnp.where(c == 0, top, low)


def unpack_ffn_third_kernel(pos_ref, hold_ref, got_ref, gprojt_ref):
    c = pos_ref[1]
    hold, got = hold_ref[...], got_ref[...].astype(F32)
    gprojt_ref[...] = jnp.concatenate(
        [jnp.where(c == 0, hold, got), jnp.where(c == 0, got, hold)], axis=1
    )


def finish_kernel(
    middle_ref,
    act_own_ref,
    act_sib_ref,
    act_far_ref,
    dx1_ref,
    dn1_ref,
    near_ref,
    coming_ref,
    x_ref,
    norms_ref,
    act_ref,
    grad_ref,
):
    act_ref[...] = (middle_ref[...] + total((act_own_ref, act_sib_ref, act_far_ref))).T.astype(BF16)
    dn1 = total((dn1_ref, near_ref, coming_ref))
    xhat, factor = xhat_of(x_ref[...].astype(F32))
    grads = dx1_ref[...] + norm_back(dn1, norms_ref[0:1, :], xhat, factor)
    grad_ref[...] = grads.T.astype(BF16)


def fill_bias(start_ref, bias_ref):
    keys, rows = bias_ref.shape
    key_ids = lax.broadcasted_iota(jnp.int32, (keys, rows), 0)
    row_ids = lax.broadcasted_iota(jnp.int32, (keys, rows), 1) + (keys - rows)
    allowed = (key_ids >= start_ref[...]) & (key_ids <= row_ids)
    bias_ref[...] = jnp.where(allowed, 0.0, NEG)


def head_slices(width):
    pairs = width // (2 * HEAD_DIM)
    return pairs, width - pairs * 2 * HEAD_DIM


def attn_fwd_kernel(
    q_ref,
    k_ref,
    v_ref,
    start_ref,
    x_ref,
    wo_ref,
    norms_ref,
    o_ref,
    lse_ref,
    middle_ref,
    n2_ref,
    qt,
    vt,
    ot,
    bias,
):
    width = q_ref.shape[1]
    fill_bias(start_ref, bias)
    qt[...] = (q_ref[...].astype(F32) * HEAD_DIM ** (-0.5)).T.astype(BF16)
    vt[...] = v_ref[...].astype(F32).T.astype(BF16)
    pairs, rest = head_slices(width)

    def one(keys, queries, values, row, head):
        scores = nn(keys, queries) + bias[...]
        peak = jnp.max(scores, axis=0, keepdims=True)
        terms = jnp.exp(scores - peak)
        summed = jnp.sum(terms, axis=0, keepdims=True)
        ot[pl.ds(row, HEAD_DIM), :] = nn(values, terms.astype(BF16)) / summed
        lse_ref[pl.ds(head, 1), :] = peak + jnp.log(summed)

    def pair(p, _):
        at = pl.multiple_of(p * 128, 128)
        keys = k_ref[:, pl.ds(at, 128)]
        queries = qt[pl.ds(at, 128), :]
        rows = lax.broadcasted_iota(jnp.int32, queries.shape, 0)
        for h in range(2):
            row = pl.multiple_of(at + h * HEAD_DIM, HEAD_DIM)
            one(
                keys,
                jnp.where((rows < HEAD_DIM) == (h == 0), queries, jnp.zeros_like(queries)),
                vt[pl.ds(row, HEAD_DIM), :],
                row,
                2 * p + h,
            )
        return 0

    lax.fori_loop(0, pairs, pair, 0)
    if rest:
        at = pairs * 128
        one(k_ref[:, at:], qt[at:, :], vt[at:, :], at, 2 * pairs)
    o_ref[...] = ot[...].T.astype(BF16)
    middle = x_ref[...].astype(F32) + nn(o_ref[...], wo_ref[...])
    middle_ref[...] = middle
    xhat, _ = xhat_of(middle)
    n2_ref[...] = (xhat * norms_ref[2:3, :] + norms_ref[3:4, :]).astype(BF16)


def attn_bwd_kernel(
    dn2_own_ref,
    dn2_sib_ref,
    dn2_far_ref,
    gz_ref,
    middle_ref,
    norms_ref,
    wo_ref,
    q_ref,
    k_ref,
    v_ref,
    lse_ref,
    start_ref,
    act_ref,
    projt_ref,
    dx1_ref,
    dy_ref,
    sums_ref,
    dq_ref,
    dk_ref,
    dv_ref,
    act_own_ref,
    act_far_ref,
    act_sib_ref,
    act_far_sib_ref,
    do_ref,
    qt,
    dot_s,
    kt,
    dqt,
    bias,
    rows_all,
):
    width = q_ref.shape[1]
    scale = HEAD_DIM ** (-0.5)
    dn2 = total((dn2_own_ref, dn2_sib_ref, dn2_far_ref))
    xhat, factor = xhat_of(middle_ref[...])
    sums_ref[0:1, :] = jnp.sum(dn2 * xhat, axis=0, keepdims=True)
    sums_ref[1:2, :] = jnp.sum(dn2, axis=0, keepdims=True)
    dx1 = gz_ref[...].astype(F32) + norm_back(dn2, norms_ref[2:3, :], xhat, factor)
    dx1_ref[...] = dx1
    dy_ref[...] = dx1.astype(BF16)
    do_ref[...] = nt(dy_ref[...], wo_ref[...]).astype(BF16)
    fill_bias(start_ref, bias)
    qt[...] = (q_ref[...].astype(F32) * scale).T.astype(BF16)
    dot_s[...] = do_ref[...].astype(F32).T.astype(BF16)
    kt[...] = k_ref[...].astype(F32).T.astype(BF16)
    pairs, rest = head_slices(width)

    def one(keys, values, queries_t, douts_t, keys_t, queries, douts, row, head):
        scores = nn(keys, queries_t) + bias[...]
        probs = jnp.exp(scores - lse_ref[pl.ds(head, 1), :])
        dprobs = nn(values, douts_t)
        delta = jnp.sum(probs * dprobs, axis=0, keepdims=True)
        dscores = (probs * (dprobs - delta)).astype(BF16)
        dqt[pl.ds(row, HEAD_DIM), :] = nn(keys_t, dscores)
        return nn(dscores, queries), nn(probs.astype(BF16), douts)

    def scaled(values):
        return (values.astype(F32) * scale).astype(BF16)

    def pair(p, _):
        at = pl.multiple_of(p * 128, 128)
        keys = k_ref[:, pl.ds(at, 128)]
        values = v_ref[:, pl.ds(at, 128)]
        queries = scaled(q_ref[:, pl.ds(at, 128)])
        douts = do_ref[:, pl.ds(at, 128)]
        queries_t = qt[pl.ds(at, 128), :]
        douts_t = dot_s[pl.ds(at, 128), :]
        rows = lax.broadcasted_iota(jnp.int32, queries_t.shape, 0)
        lanes = lax.broadcasted_iota(jnp.int32, queries.shape, 1)
        dk_sum = dv_sum = None
        for h in range(2):
            row = pl.multiple_of(at + h * HEAD_DIM, HEAD_DIM)
            in_rows = (rows < HEAD_DIM) == (h == 0)
            in_lanes = (lanes < HEAD_DIM) == (h == 0)
            zero_t, zero = jnp.zeros_like(queries_t), jnp.zeros_like(queries)
            dk_part, dv_part = one(
                keys,
                values,
                jnp.where(in_rows, queries_t, zero_t),
                jnp.where(in_rows, douts_t, zero_t),
                kt[pl.ds(row, HEAD_DIM), :],
                jnp.where(in_lanes, queries, zero),
                jnp.where(in_lanes, douts, zero),
                row,
                2 * p + h,
            )
            dk_sum = dk_part if h == 0 else dk_sum + dk_part
            dv_sum = dv_part if h == 0 else dv_sum + dv_part
        dk_ref[:, pl.ds(at, 128)] = dk_sum.astype(BF16)
        dv_ref[:, pl.ds(at, 128)] = dv_sum.astype(BF16)
        return 0

    lax.fori_loop(0, pairs, pair, 0)
    if rest:
        at = pairs * 128
        dk_part, dv_part = one(
            k_ref[:, at:],
            v_ref[:, at:],
            qt[at:, :],
            dot_s[at:, :],
            kt[at:, :],
            scaled(q_ref[:, at:]),
            do_ref[:, at:],
            at,
            2 * pairs,
        )
        dk_ref[:, at:] = dk_part.astype(BF16)
        dv_ref[:, at:] = dv_part.astype(BF16)
    dq_ref[...] = (dqt[...].T * scale).astype(BF16)
    tok = q_ref.shape[0]

    def forward(i):
        at = pl.ds(pl.multiple_of(i * tok, tok), tok)
        rows_all[at, :] = nt(act_ref[at, :], projt_ref[...]).astype(BF16)

    repeat(4, True, forward)
    y_refs = (act_own_ref, act_far_ref, act_sib_ref, act_far_sib_ref)
    for y_ref, at in zip(y_refs, members_of(tok)):
        y_ref[...] = rows_all[at, :]


def xhat_of(values):
    center = jnp.mean(values, axis=-1, keepdims=True)
    centered = values - center
    variance = jnp.mean(centered * centered, axis=-1, keepdims=True)
    factor = lax.rsqrt(variance + EPS)
    return centered * factor, factor


def norm_back(grads, gain, xhat, factor):
    e = grads * gain
    return factor * (
        e
        - jnp.mean(e, axis=-1, keepdims=True)
        - xhat * jnp.mean(e * xhat, axis=-1, keepdims=True)
    )


def add(*terms):
    acc = terms[0].astype(F32)
    for term in terms[1:]:
        acc = acc + term.astype(F32)
    return acc


def segment_starts(dealt_lengths, seq_order, first_row, rows):
    lengths = dealt_lengths[0].reshape(-1)
    order = seq_order[0]
    count = lengths.shape[0]
    arrival = jnp.arange(count, dtype=jnp.int32)
    before = (order[:, None] < arrival[None, :]).astype(jnp.int32)
    begins = jnp.sum(before * lengths[:, None], axis=0)
    ids = first_row + jnp.arange(rows, dtype=jnp.int32)
    reached = begins[:, None] <= ids[None, :]
    return jnp.max(jnp.where(reached, begins[:, None], 0), axis=0)


def tiled(value):
    if value.ndim == 2 and value.shape[0] % 128 == 0 and value.shape[1] % 128:
        return value.reshape(value.shape[0] // 8, 8, value.shape[1])
    return value


def barrier(value, fence):
    leaves, tree = jax.tree.flatten(value)
    kept = lax.optimization_barrier(([tiled(v) for v in leaves], fence))[0]
    return tree.unflatten([k.reshape(v.shape) for k, v in zip(kept, leaves)])


def permute(value, axis, pairs):
    return lax.ppermute(tiled(value), axis, pairs).reshape(value.shape)


class Clock:
    def __init__(self):
        self.fence = ()

    def __call__(self, value):
        if not self.fence:
            return value
        return barrier(value, self.fence)

    def tick(self, *done):
        self.fence = tuple(tiled(v) for v in jax.tree.leaves(done))


def per_device(
    tokens,
    qkv_weight,
    out_weight,
    fc_weight,
    proj_weight,
    norm_params,
    grad_out,
    dealt_lengths,
    seq_order,
):
    n_dp, n_f = lax.axis_size("dp"), lax.axis_size("fsdp")
    n_y, n_z = n_dp // 2, n_f // 2
    dp, f = lax.axis_index("dp"), lax.axis_index("fsdp")
    x, c = dp & 1, f & 1
    pos = jnp.stack([x, c, dp, f]).astype(jnp.int32)
    tok, width = tokens.shape
    seq_longest = n_f * tok // dealt_lengths.shape[1] // 2
    halo = -(-seq_longest // tok)
    halo += halo % 2

    now = Clock()

    def run(*args, **kwargs):
        made = call(*args, **kwargs)
        return lambda *operands: made(*now(operands))

    def xor(value, axis, bits):
        size = n_dp if axis == "dp" else n_f
        return permute(now(value), axis, [(i, i ^ bits) for i in range(size)])

    def to_core(value):
        return xor(value, "fsdp", 1)

    def to_x(value):
        return xor(value, "dp", 1)

    def to_y(value, k):
        return xor(value, "dp", 2 * k)

    def to_z(value, k):
        return xor(value, "fsdp", 2 * k)

    def along_z(value, step, senders):
        pairs = [(2 * z + i, 2 * (z + step) + i) for z in senders for i in range(2)]
        return permute(now(value), "fsdp", pairs)

    def joined(*values):
        return jnp.concatenate(values, axis=0)

    z_at = f >> 1
    others_z, others_y = range(1, n_z), range(1, n_y)

    def by_z(choose):
        choices = [choose(z) for z in range(n_z)]
        value = choices[0]
        for z in range(1, n_z):
            if choices[z] is not choices[z - 1]:
                value = jnp.where(z_at >= z, choices[z], value)
        return value

    k_rows, nq = qkv_weight.shape
    no = out_weight.shape[1]
    half, wide = k_rows // 2, 2 * (nq + no)
    rows = (half // 2 + 7) // 8 * 8
    own_first, own_second = run(pack_attn_kernel, [((rows, wide), BF16)] * 2, [VM, VM])(
        qkv_weight, out_weight.T
    )
    now.tick(own_first, own_second)

    firsts = [own_first] + [to_z(own_first, dz) for dz in others_z]
    ff_half = fc_weight.shape[1] // 2
    sub = proj_weight.shape[0] // 4
    send, keep = run(
        pack_ffn_first_kernel, [((ff_half, k_rows + sub), BF16)] * 2, [SM, VM, VM])(pos, fc_weight, proj_weight.T)
    got = to_x(send)
    norm_x = to_x(norm_params)
    now.tick(firsts, got, norm_x)

    stack = {(0, 0, 0): jnp.stack(firsts)}
    seconds = [own_second] + [to_z(own_second, dz) for dz in others_z]
    for dy in others_y:
        stack[0, dy, 0] = to_y(stack[0, 0, 0], dy)
    stack[0, 0, 1] = to_x(stack[0, 0, 0])
    fct, send, hold = run(
        pack_ffn_second_kernel,
        [((ff_half, 2 * k_rows), BF16)] + [((no, 2 * sub), BF16)] * 2,
        [SM, VM, VM])(pos, keep, got)
    now.tick(seconds, stack, send)

    got = to_core(send)
    norm_pairs = jnp.stack([norm_params, norm_x])
    norm_pairs = [norm_pairs] + [to_y(norm_pairs, dy) for dy in others_y]
    stack[1, 0, 0] = jnp.stack(seconds)
    stack[1, 0, 1] = to_x(stack[1, 0, 0])
    for dy in others_y:
        stack[1, dy, 0] = to_y(stack[1, 0, 0], dy)
    grad_out = now(grad_out)
    even = [tokens]
    for _ in range(halo // 2):
        even.append(along_z(even[-1], 1, range(n_z - 1)))
    stacks, arrays = [], []

    def cross(*keys):
        stacks.extend([(key + (0,),) for key in keys])
        arrays.extend(stack[key] for key in keys)
        stacks.append(tuple(key + (1,) for key in keys))
        arrays.append(to_core(joined(*[stack[key] for key in keys])))

    cross((0, 0, 0), *[(0, dy, 0) for dy in others_y])
    (own_ffn,) = run(
        pack_ffn_third_kernel, [((ff_half, 2 * (k_rows + sub)), BF16)], [SM, VM, VM, VM])(pos, fct, hold, got)
    now.tick(stack, even[-1], arrays[-1], own_ffn, norm_pairs, grad_out)

    ups, downs, ffn = [own_ffn], [own_ffn], {(0, 0): own_ffn}

    def ffn_over_z(t):
        ups.append(along_z(ups[-1], 1, range(t - 1, n_z - 1)))
        downs.append(along_z(downs[-1], -1, range(1, n_z - t + 1)))

    def pick(t):
        return by_z(lambda z: ups[z - (z ^ t)] if z ^ t < z else downs[(z ^ t) - z])

    for dy in others_y:
        stack[0, dy, 1] = to_x(stack[0, dy, 0])
        stack[1, dy, 1] = to_y(stack[1, 0, 1], dy)
    rows_before = []
    for distance in range(1, halo + 1):
        if distance % 2:
            near = distance // 2
            rows_before.append(to_core(jnp.where(c == 0, even[near], even[near + 1])))
        else:
            rows_before.append(even[distance // 2])
    x_rows = joined(*rows_before[::-1], tokens)
    cross((0, 0, 1), (1, 0, 0), (1, 0, 1), *[(1, dy, 0) for dy in others_y])
    norms = jnp.concatenate(
        [
            sum(
                jnp.where((dp ^ r) == j, norm_pairs[r >> 1][r & 1].astype(F32), 0.0)
                for r in range(n_dp)
            )
            for j in range(n_dp)
        ],
        axis=1,
    )
    xhat_one, factor_one = xhat_of(x_rows.astype(F32))
    normed = (xhat_one * norms[0] + norms[1]).astype(BF16)
    now.tick(arrays[-1], stack, normed)

    cross(*[(part, dy, 1) for dy in others_y for part in range(2)])
    now.tick(arrays[-1])
    ffn_over_z(1)
    for dy in others_y:
        ffn[dy, 0] = to_y(own_ffn, dy)
    gz_far = to_x(grad_out)
    gz_sib = to_core(grad_out)
    square = ((width, width), BF16)
    dims = (n_dp, n_f, nq, no)
    wq, wk, wv, wo = run(
        functools.partial(assemble_attn_kernel, stacks, dims),
        [square] * 4,
        [SM] + [ANY] * len(arrays),
        [
            pltpu.VMEM((2, n_dp * n_f, rows, wide), BF16),
            pltpu.SemaphoreType.DMA((2 * n_dp * n_f,)),
        ])(pos, *arrays)
    now.tick(wq, wk, wv, wo, ups, downs, ffn, gz_far, gz_sib)

    ffn[0, 1] = pick(1)
    ffn_over_z(2)
    for dy in others_y:
        ffn[dy, 1] = to_y(ffn[0, 1], dy)
    gz_far_sib = to_core(gz_far)
    queries, all_keys, values = run(
        qkv_kernel, [((tok, width), BF16)] + [(normed.shape, BF16)] * 2, [VM] * 4)(normed, wq, wk, wv)
    now.tick(queries, all_keys, values, ups, downs, ffn, gz_far_sib)

    ffn[0, 2] = pick(2)
    for t in others_z[2:]:
        ffn_over_z(t)
    for dy in others_y:
        ffn[dy, 2] = to_y(ffn[0, 2], dy)
    span = (halo + 1) * tok
    starts = segment_starts(dealt_lengths, seq_order, f * tok, tok) - (f - halo) * tok
    starts = starts.reshape(1, tok).astype(jnp.int32)
    heads = width // HEAD_DIM
    attended, lse, middle, normed_two = run(
        attn_fwd_kernel,
        [((tok, width), BF16), ((heads, tok), F32), ((tok, width), F32), ((tok, width), BF16)],
        [VM] * 7,
        [
            pltpu.VMEM((width, tok), BF16),
            pltpu.VMEM((width, span), BF16),
            pltpu.VMEM((width, tok), F32),
            pltpu.VMEM((span, tok), F32),
        ])(queries, all_keys, values, starts, tokens, wo, norms)
    now.tick(attended, lse, middle, normed_two, ups, downs, ffn)

    n2_far = to_x(normed_two)
    n2_sib = to_core(normed_two)
    for t in others_z[2:]:
        ffn[0, t] = pick(t)
        for dy in others_y:
            ffn[dy, t] = to_y(ffn[0, t], dy)
    now.tick(n2_far, n2_sib, ffn)
    n2_far_sib = to_core(n2_far)
    n2_rows = [normed_two, n2_far, n2_sib, n2_far_sib]
    gz_rows = [grad_out, gz_far, gz_sib, gz_far_sib]

    ffn_keys = sorted(ffn)
    fct_full, projt_full = run(
        functools.partial(assemble_ffn_kernel, ffn_keys, (n_y, n_z)),
        [((n_z * ff_half, n_y * 2 * k_rows), BF16), ((n_z * 2 * no, n_y * 2 * sub), BF16)],
        [SM] + [ANY] * len(ffn_keys),
        [
            pltpu.VMEM((len(ffn_keys),) + own_ffn.shape, BF16),
            pltpu.SemaphoreType.DMA((len(ffn_keys),)),
        ])(pos, *[ffn[key] for key in ffn_keys])
    ff = fct_full.shape[0]
    rows_all = pltpu.VMEM((4 * tok, width), BF16)
    activated, dhidden, own, far, sib, far_sib = run(
        ffn_kernel,
        [((4 * tok, ff), BF16)] * 2 + [((tok, width), BF16)] * 4,
        [VM] * 10,
        [rows_all] * 3,
    )(*n2_rows, *gz_rows, fct_full, projt_full)
    now.tick(activated, dhidden, own, far, sib, far_sib)
    far = add(far, to_core(far_sib)).astype(BF16)
    now.tick(far)

    dn2_far = to_x(far)
    dn2_sib = to_core(sib)
    (ffn_grads,) = run(
        functools.partial(ffn_grads_kernel, (n_y, n_z)),
        [((n_y * n_z,) + own_ffn.shape, BF16)],
        [SM] + [VM] * 10,
        [
            pltpu.VMEM((n_z * ff_half, 4 * tok), BF16),
            pltpu.VMEM((width, 4 * tok), BF16),
            pltpu.VMEM((4 * tok, width), BF16),
        ])(pos, dhidden, *n2_rows, *gz_rows, activated)
    now.tick(ffn_grads, dn2_far, dn2_sib)

    part_of = {}
    far_y = {
        dz: [to_y(ffn_grads[dy * n_z + dz], dy) for dy in others_y] for dz in others_z[::-1][:-1]
    }
    big, small = (span, width), (tok, width)
    dx1, dy_low, norm_sums, dq, dk, dv, act_own, act_far, act_sib, act_far_sib = run(
        attn_bwd_kernel,
        [(small, F32), (small, BF16), ((2, width), F32), (small, BF16), (big, BF16), (big, BF16)]
        + [(small, BF16)] * 4,
        [VM] * 14,
        [
            pltpu.VMEM(small, BF16),
            pltpu.VMEM((width, tok), BF16),
            pltpu.VMEM((width, tok), BF16),
            pltpu.VMEM((width, span), BF16),
            pltpu.VMEM((width, tok), F32),
            pltpu.VMEM((span, tok), F32),
            rows_all,
        ])(own, dn2_sib, dn2_far, grad_out, middle, norms, wo, queries, all_keys, values, lse, starts, activated, projt_full)
    now.tick(dq, dk, dv, far_y, act_own, act_far, act_sib, act_far_sib)

    carry = [None, None]

    def ffn_back_z(s):
        reach = n_z - s
        for way, (step, senders) in enumerate(
            ((1, range(0, s)), (-1, range(n_z - s, n_z)))
        ):
            value = by_z(
                lambda z: part_of[z ^ (z + step * reach)]
                if 0 <= z + step * reach < n_z
                else part_of[n_z - 1]
            )
            if carry[way] is not None:
                value = add(value, carry[way]).astype(BF16)
            carry[way] = along_z(value, step, senders)

    ffn_grads = now(ffn_grads)
    next_y = [to_y(ffn_grads[dy * n_z + 1], dy) for dy in others_y]
    act_far_sib = to_core(act_far_sib)
    count = 2 * n_y * n_z
    block = ((count, rows, wide), BF16)
    keeps, sent, gots = {}, {}, {}
    keeps[0], sent[0], keeps[1], sent[1] = run(
        functools.partial(attn_grads_kernel, dims),
        [block] * 4,
        [SM] + [VM] * 6,
        [pltpu.VMEM((width, span), BF16), pltpu.VMEM((width, tok), BF16)],
    )(pos, normed, attended, dq, dk, dv, dy_low)
    now.tick(keeps, sent, next_y, act_far_sib)

    gots[1], gots[0] = to_core(sent[1]), to_core(sent[0])
    act_sib = to_core(act_sib)
    for dz, pieces in now(far_y).items():
        part_of[dz] = add(ffn_grads[dz], *pieces).astype(BF16)
    ffn_back_z(1)

    def core_sum(part, dy, dx, count=1):
        at = (part * n_y + dy) * n_z
        stop = at + count * n_z
        return add(keeps[dx][at:stop], gots[dx][at:stop])

    x_send = core_sum(0, 0, 1, n_y).astype(BF16)
    y_send = [core_sum(1, dy, 1).astype(BF16) for dy in others_y]
    now.tick(x_send, y_send, gots, act_sib)
    next_y = now(next_y)

    part_of[1] = add(ffn_grads[1], *next_y).astype(BF16)
    last_y = [to_y(ffn_grads[dy * n_z], dy) for dy in others_y]
    got_x = to_x(x_send)
    got_y = [to_y(value, dy) for dy, value in zip(others_y, y_send)]
    for s in range(2, n_z - 1):
        ffn_back_z(s)
    cut = halo * tok
    dn1, dn1_halo, norm_first = run(
        dn1_kernel, [(small, F32), ((cut, width), BF16), ((2, width), F32)], [VM] * 7
    )(dq, dk, dv, wq, wk, wv, x_rows)
    norm_rows = -(-4 * width // wide // 8) * 8

    def with_norms(value, norms):
        extra = norms.astype(BF16).reshape(-1, wide)
        extra = jnp.pad(extra, ((0, norm_rows - extra.shape[0]), (0, 0)))
        extra = jnp.broadcast_to(extra, value.shape[:-2] + extra.shape)
        return jnp.concatenate([value, extra], axis=-2)

    def norms_of(value):
        return value[0, -norm_rows:][: 4 * width // wide].reshape(4, width).astype(F32)

    now.tick(got_x, got_y, carry, dn1, dn1_halo, norm_first, last_y)
    got_x, got_y, dn1, dn1_halo, norm_first, last_y, act_far_sib = now(
        (got_x, got_y, dn1, dn1_halo, norm_first, last_y, act_far_sib)
    )
    part_of[0] = add(ffn_grads[0], *last_y).astype(BF16)

    norm_grads = joined(norm_first, norm_sums)
    first_x = [got_x[dy * n_z : (dy + 1) * n_z] for dy in range(n_y)]
    both = []
    for dy in others_y:
        value = [add(core_sum(0, dy, 0), first_x[dy]), core_sum(1, dy, 0)]
        value = jnp.concatenate([v.astype(BF16) for v in value], axis=1)
        both.append(to_y(with_norms(value, norm_grads), dy))
    act_far = add(act_far, act_far_sib).astype(BF16)
    second_x = add(core_sum(1, 0, 1), *got_y).astype(BF16)
    got_x = to_x(joined(second_x.reshape(-1, wide), act_far.reshape(-1, wide)))
    if n_z > 2:
        ffn_back_z(n_z - 1)
    def back(distance):
        return dn1_halo[cut - distance * tok : cut - (distance - 1) * tok]

    carried = [None] * (halo // 2 + 1)
    for near in range(halo // 2):
        got = to_core(back(2 * near + 1)).astype(F32)
        for level, wanted in ((near, 1), (near + 1, 0)):
            term = jnp.where(c != wanted, got, 0.0)
            carried[level] = term if carried[level] is None else carried[level] + term
    outgoing = [back(2 * level).astype(F32) + carried[level] for level in range(1, halo // 2 + 1)]
    coming = None
    for level in range(halo // 2, 0, -1):
        out = outgoing[level - 1]
        if coming is not None:
            out = out + coming
        coming = along_z(out.astype(BF16), -1, range(1, n_z)).astype(F32)
    now.tick(got_x, both, carry, coming)
    got_x, both, coming = now((got_x, both, coming))
    act_far = got_x[n_z * rows :].reshape(small)
    second_x = got_x[: n_z * rows].reshape(n_z, rows, wide)
    send, keep = run(
        unpack_ffn_first_kernel,
        [((ff_half, k_rows + sub), BF16), ((ff_half, k_rows + sub), F32)],
        [SM] + [VM] * 3,
    )(pos, part_of[0], *carry)
    norm_grads = norm_grads + sum(norms_of(value) for value in both)
    first_sum = add(core_sum(0, 0, 0), first_x[0], *[value[:, :rows] for value in both])
    second_sum = add(
        core_sum(1, 0, 0), second_x, *[value[:, rows : 2 * rows] for value in both]
    )
    sums = jnp.concatenate([first_sum.astype(BF16), second_sum.astype(BF16)], axis=1)
    sums = with_norms(sums, norm_grads)
    now.tick(sums)

    got = to_x(send)
    parts = [sums[0]] + [to_z(sums[dz], dz) for dz in others_z]
    activations, input_grad = run(finish_kernel, [((width, tok), BF16)] * 2, [VM] * 10)(
        middle,
        act_own,
        act_sib,
        act_far,
        dx1,
        dn1,
        carried[0].astype(BF16),
        coming.astype(BF16),
        tokens,
        norms,
    )
    grad_fc, send, hold = run(
        unpack_ffn_second_kernel,
        [(fc_weight.shape, F32), ((no, 2 * sub), BF16), ((no, 2 * sub), F32)],
        [SM, VM, VM])(pos, keep, got)
    (grad_proj,) = run(unpack_ffn_third_kernel, [(proj_weight.shape[::-1], F32)], [SM, VM, VM])(
        pos, hold, to_core(send)
    )
    parts = barrier(parts, (grad_fc, grad_proj, activations, input_grad))
    norm_grads = sum(norms_of(part[None]) for part in parts)
    norm_grads = norm_grads + lax.ppermute(norm_grads, "fsdp", [(i, i ^ 1) for i in range(n_f)])
    norm_grads = norm_grads + lax.ppermute(norm_grads, "dp", [(i, i ^ 1) for i in range(n_dp)])
    norm_grads = lax.dynamic_slice_in_dim(norm_grads, dp * k_rows, k_rows, axis=1)
    grad_qkv, grad_attn_out = run(
        functools.partial(unpack_attn_kernel, n_z, rows),
        [(qkv_weight.shape, F32), (out_weight.shape[::-1], F32)],
        [VM] * n_z,
        [pltpu.VMEM(out_weight.shape, F32)],
    )(*parts)
    return (activations.T, input_grad.T, grad_qkv, grad_attn_out.T, grad_fc, grad_proj.T, norm_grads)


def solution(mesh):
    in_specs = (
        P(("dp", "fsdp"), None),
        P("dp", "fsdp"),
        P("dp", "fsdp"),
        P("dp", "fsdp"),
        P("dp", "fsdp"),
        P(None, "dp"),
        P(("dp", "fsdp"), None),
        P("dp", None, None),
        P("dp", None),
    )
    out_specs = (
        P(("dp", "fsdp"), None),
        P(("dp", "fsdp"), None),
        P("dp", "fsdp"),
        P("dp", "fsdp"),
        P("dp", "fsdp"),
        P("dp", "fsdp"),
        P(None, "dp"),
    )
    return jax.shard_map(
        per_device, mesh=mesh, in_specs=in_specs, out_specs=out_specs, check_vma=False
    )
```

```python
import functools
import math

import jax
import jax.numpy as jnp
from jax import lax
from jax.experimental import pallas as pl
from jax.experimental.pallas import tpu as pltpu
from jax.sharding import PartitionSpec as P

HEAD_DIM = 64
EPS = 1e-05
NEG = -1e30
F32 = jnp.float32
BF16 = jnp.bfloat16
VMEM_ALL = 60 * 2**20

ANY = pl.BlockSpec(memory_space=pl.ANY)
VM = pl.BlockSpec(memory_space=pltpu.VMEM)
SM = pl.BlockSpec(memory_space=pltpu.SMEM)


def call(kernel, outs, in_specs, scratch=()):
    return pl.pallas_call(
        kernel,
        name=getattr(kernel, "func", kernel).__name__,
        out_shape=tuple(jax.ShapeDtypeStruct(s, d) for s, d in outs),
        in_specs=list(in_specs),
        out_specs=tuple(VM for _ in outs),
        scratch_shapes=list(scratch),
        compiler_params=pltpu.CompilerParams(vmem_limit_bytes=VMEM_ALL),
        cost_estimate=pl.CostEstimate(flops=0, bytes_accessed=0, transcendentals=0),
    )


def dot(a, b, ca, cb):
    return lax.dot_general(a, b, (((ca,), (cb,)), ((), ())), preferred_element_type=F32)


def nn(a, b):
    return dot(a, b, 1, 0)


def nt(a, b):
    return dot(a, b, 1, 1)


def tn(a, b):
    return dot(a, b, 0, 0)


def repeat(count, looped, body):
    if not looped:
        for i in range(count):
            body(i)
        return

    def step(i, carry):
        body(i)
        return carry

    lax.fori_loop(0, count, step, 0)


def split_cols(lo, hi, width):
    pieces = []
    while lo < hi:
        which, start = divmod(lo, width)
        stop = min(width, start + hi - lo)
        pieces.append((which, start, stop))
        lo += stop - start
    return pieces


def pack_attn_kernel(wq_ref, wo_ref, first_ref, second_ref):
    half = wq_ref.shape[0] // 2
    rows = first_ref.shape[0]
    wo = wo_ref[...].astype(F32).T.astype(BF16)
    for out_ref, row in ((first_ref, 0), (second_ref, half - rows)):
        vals = []
        for h in range(2):
            at = h * half + row
            vals += [wq_ref[at : at + rows, :], wo[at : at + rows, :]]
        out_ref[...] = jnp.concatenate(vals, axis=1)


def pack_ffn_first_kernel(pos_ref, fc_ref, projt_ref, send_ref, keep_ref):
    x = pos_ref[0]
    half = fc_ref.shape[1] // 2
    sub = projt_ref.shape[1] // 4
    sides = []
    for h in range(2):
        fct = fc_ref[:, h * half : (h + 1) * half].astype(F32).T
        projt = [
            projt_ref[:, (2 * s + h) * sub : (2 * s + h + 1) * sub].astype(F32) for s in range(2)
        ]
        sides.append(jnp.concatenate([fct, jnp.concatenate(projt, axis=0)], axis=1))
    send_ref[...] = jnp.where(x == 0, sides[1], sides[0]).astype(BF16)
    keep_ref[...] = jnp.where(x == 0, sides[0], sides[1]).astype(BF16)


def pack_ffn_second_kernel(pos_ref, keep_ref, got_ref, fct_ref, send_ref, hold_ref):
    x, c = pos_ref[0], pos_ref[1]
    keep, got = keep_ref[...], got_ref[...]
    first = jnp.where(x == 0, keep, got)
    second = jnp.where(x == 0, got, keep)
    k = fct_ref.shape[1] // 2
    rows = send_ref.shape[0]
    fct_ref[...] = jnp.concatenate([first[:, :k], second[:, :k]], axis=1)
    projt = jnp.concatenate([first[:, k:], second[:, k:]], axis=1)
    top, low = projt[:rows, :], projt[rows:, :]
    send_ref[...] = jnp.where(c == 0, low, top)
    hold_ref[...] = jnp.where(c == 0, top, low)


def pack_ffn_third_kernel(pos_ref, fct_ref, hold_ref, got_ref, out_ref):
    c = pos_ref[1]
    hold, got = hold_ref[...], got_ref[...]
    top = jnp.where(c == 0, hold, got)
    low = jnp.where(c == 0, got, hold)
    projt = jnp.concatenate([top, low], axis=0)
    out_ref[...] = jnp.concatenate([fct_ref[...], projt], axis=1)


def place(pieces, buf, sem, slots):
    copies = [
        pltpu.make_async_copy(piece, buf.at[slot], sem.at[i])
        for i, (piece, slot) in enumerate(zip(pieces, slots))
    ]
    for copy in copies:
        copy.start()
    for copy in copies:
        copy.wait()


def assemble_attn_kernel(stacks, dims, pos_ref, *refs):
    n_dp, n_f, nq, no = dims
    n_z = n_f // 2
    ins = refs[: len(stacks)]
    w_refs = refs[len(stacks) : len(stacks) + 3]
    wo_ref, buf, sem = refs[len(stacks) + 3 :]
    dp, f = pos_ref[2], pos_ref[3]
    copies = []
    for ref, groups in zip(ins, stacks):
        for i, (part, dy, dx, dc) in enumerate(groups):
            for dz in range(n_z):
                slot = (dp ^ (2 * dy + dx)) * n_f + (f ^ (2 * dz + dc))
                copies.append(
                    pltpu.make_async_copy(
                        ref.at[i * n_z + dz], buf.at[part, slot], sem.at[len(copies)]
                    )
                )
    for copy in copies:
        copy.start()
    for copy in copies:
        copy.wait()
    rows = buf.shape[2]
    wide = nq + no
    width = wo_ref.shape[1]
    half = width // n_dp // 2
    for d in range(n_dp):
        for h in range(2):
            base = h * wide
            for part, skip in ((0, 0), (1, 2 * rows - half)):
                row = (2 * d + h) * half + part * rows
                stop = row + rows - skip
                for third in range(3):
                    vals = [
                        buf[part, d * n_f + which][skip:, base + lo : base + hi]
                        for which, lo, hi in split_cols(third * width, (third + 1) * width, nq)
                    ]
                    w_refs[third][row:stop, :] = jnp.concatenate(vals, axis=1)
                wo_ref[row:stop, :] = jnp.concatenate(
                    [
                        buf[part, d * n_f + g][skip:, base + nq : base + wide]
                        for g in range(n_f)
                    ],
                    axis=1,
                )


def assemble_ffn_kernel(keys, dims, pos_ref, *refs):
    n_y, n_z = dims
    pieces = refs[: len(keys)]
    fct_ref, projt_ref, buf, sem = refs[len(keys) :]
    dp, f = pos_ref[2], pos_ref[3]
    slots = [((dp >> 1) ^ dy) * n_z + ((f >> 1) ^ dz) for dy, dz in keys]
    place(pieces, buf, sem, slots)
    rows, wide = buf.shape[1:]
    half = wide // 2
    for z in range(n_z):
        vals = [buf[y * n_z + z] for y in range(n_y)]
        fct_ref[z * rows : (z + 1) * rows, :] = jnp.concatenate(
            [v[:, :half] for v in vals], axis=1
        )
        projt_ref[z * rows : (z + 1) * rows, :] = jnp.concatenate(
            [v[:, half:] for v in vals], axis=1
        )


def attn_grads_kernel(dims, pos_ref, *refs):
    n_dp, n_f, nq, no = dims
    n_z = n_f // 2
    c, dp, f = pos_ref[1], pos_ref[2], pos_ref[3]
    n1_ref, ob_ref, dq_ref, dk_ref, dv_ref, dy_ref = refs[:6]
    outs_by_x, (n1t, obt) = (refs[6:8], refs[8:10]), refs[10:]
    n1t[...] = n1_ref[...].astype(F32).T.astype(BF16)
    obt[...] = ob_ref[...].astype(F32).T.astype(BF16)
    width = n1t.shape[0]
    k_rows = width // n_dp
    half = k_rows // 2
    rows = refs[6].shape[1]
    own = n1t.shape[1] - dq_ref.shape[0]

    def one(dy, dx):
        keep_ref, send_ref = outs_by_x[dx]
        at = pl.ds(((2 * dy + dx) ^ dp) * k_rows, k_rows)
        left = n1t[at, :]
        parts = [
            nn(left[:, own:], dq_ref[...]).astype(BF16),
            nn(left, dk_ref[...]).astype(BF16),
            nn(left, dv_ref[...]).astype(BF16),
        ]
        outs = nn(obt[at, :], dy_ref[...]).astype(BF16)
        for k in range(n_z):
            for part in range(2):
                both = []
                for g in (2 * k, 2 * k + 1):
                    vals = []
                    for h in range(2):
                        row = h * half + part * (half - rows)
                        for which, lo, hi in split_cols(g * nq, (g + 1) * nq, width):
                            vals.append(parts[which][row : row + rows, lo:hi])
                        vals.append(outs[row : row + rows, g * no : (g + 1) * no])
                    both.append(jnp.concatenate(vals, axis=1))
                slot = (part * n_dp // 2 + dy) * n_z + ((f >> 1) ^ k)
                keep_ref[slot] = jnp.where(c == 0, both[0], both[1])
                send_ref[slot] = jnp.where(c == 0, both[1], both[0])

    for dx in range(2):
        repeat(n_dp // 2, k_rows % 16 == 0, functools.partial(one, dx=dx))


def qkv_kernel(n1_ref, wq_ref, wk_ref, wv_ref, q_ref, k_ref, v_ref):
    tok = q_ref.shape[0]
    first = n1_ref.shape[0] - tok
    q_ref[...] = nn(n1_ref[first:, :], wq_ref[...]).astype(BF16)

    def one(i):
        at = pl.ds(pl.multiple_of(i * tok, tok), tok)
        k_ref[at, :] = nn(n1_ref[at, :], wk_ref[...]).astype(BF16)
        v_ref[at, :] = nn(n1_ref[at, :], wv_ref[...]).astype(BF16)

    repeat(n1_ref.shape[0] // tok, True, one)


def dn1_kernel(
    dq_ref, dk_ref, dv_ref, wq_ref, wk_ref, wv_ref, x_ref, own_ref, halo_ref, sums_ref
):
    tok = dq_ref.shape[0]
    cut = halo_ref.shape[0]
    sums_ref[...] = jnp.zeros(sums_ref.shape, F32)

    def tally(grads, at):
        xhat, _ = xhat_of(x_ref[at, :].astype(F32))
        sums_ref[0:1, :] += jnp.sum(grads * xhat, axis=0, keepdims=True)
        sums_ref[1:2, :] += jnp.sum(grads, axis=0, keepdims=True)

    def rows_of(at):
        return nt(dk_ref[at, :], wk_ref[...]) + nt(dv_ref[at, :], wv_ref[...])

    def step(r, carry):
        at = pl.ds(pl.multiple_of(r * tok, tok), tok)
        grads = rows_of(at)
        halo_ref[at, :] = grads.astype(BF16)
        tally(grads, at)
        return carry

    lax.fori_loop(0, cut // tok, step, 0)
    last = pl.ds(cut, tok)
    grads = nt(dq_ref[...], wq_ref[...]) + rows_of(last)
    own_ref[...] = grads
    tally(grads, last)


def members_of(tok):
    return [slice(i * tok, (i + 1) * tok) for i in range(4)]


def ffn_kernel(*refs):
    n2_refs, gz_refs = refs[:4], refs[4:8]
    fct_ref, projt_ref, act_ref, dh_ref = refs[8:12]
    dn2_refs = refs[12:16]
    n2s, gzs, dn2s = refs[16:]
    tok = n2_refs[0].shape[0]
    for i, at in enumerate(members_of(tok)):
        n2s[at, :] = n2_refs[i][...]
        gzs[at, :] = gz_refs[i][...]

    def one(i):
        at = pl.ds(pl.multiple_of(i * tok, tok), tok)
        hidden = nt(n2s[at, :], fct_ref[...])
        cdf = 0.5 * (1.0 + lax.erf(hidden * math.sqrt(0.5)))
        act_ref[at, :] = (hidden * cdf).astype(BF16)
        slope = cdf + hidden * jnp.exp(-0.5 * hidden * hidden) * (1.0 / math.sqrt(2.0 * math.pi))
        dh_ref[at, :] = (nn(gzs[at, :], projt_ref[...]) * slope).astype(BF16)
        dn2s[at, :] = nn(dh_ref[at, :], fct_ref[...]).astype(BF16)

    repeat(4, True, one)
    for dn2_ref, at in zip(dn2_refs, members_of(tok)):
        dn2_ref[...] = dn2s[at, :]


def ffn_grads_kernel(dims, pos_ref, dh_ref, *refs):
    n2_refs, gz_refs = refs[:4], refs[4:8]
    act_ref, out_ref, dht, gzt, n2_ref = refs[8:]
    n_y, n_z = dims
    tok = n2_refs[0].shape[0]
    dp, f = pos_ref[2], pos_ref[3]
    rows, wide = out_ref.shape[1:]
    half = wide // 2
    dht[...] = dh_ref[...].astype(F32).T.astype(BF16)
    for i in range(4):
        at = slice(i * tok, (i + 1) * tok)
        gzt[:, at] = gz_refs[i][...].astype(F32).T.astype(BF16)
        n2_ref[at, :] = n2_refs[i][...]

    def one(z):
        at = pl.ds(z * rows, rows)
        gfc = nn(dht[at, :], n2_ref[...]).astype(BF16)
        gproj = nn(gzt[at, :], act_ref[...]).astype(BF16)
        for y in range(n_y):
            slot = ((dp >> 1) ^ y) * n_z + ((f >> 1) ^ z)
            lanes = slice(y * half, (y + 1) * half)
            out_ref[slot] = jnp.concatenate([gfc[:, lanes], gproj[:, lanes]], axis=1)

    repeat(n_z, rows % 16 == 0, one)


def total(refs):
    acc = refs[0][...].astype(F32)
    for ref in refs[1:]:
        acc = acc + ref[...].astype(F32)
    return acc


def unpack_attn_kernel(count, rows, *refs):
    gq_ref, got_ref, go_ref = refs[count:]
    half = gq_ref.shape[0] // 2
    nq, no = gq_ref.shape[1], go_ref.shape[1]
    for part in range(2):
        summed = total([ref.at[part * rows : (part + 1) * rows] for ref in refs[:count]])
        skip = part * (2 * rows - half)
        for h in range(2):
            base = h * (nq + no)
            row = h * half + part * rows
            stop = row + rows - skip
            gq_ref[row:stop, :] = summed[skip:, base : base + nq]
            go_ref[row:stop, :] = summed[skip:, base + nq : base + nq + no]
    got_ref[...] = go_ref[...].T


def unpack_ffn_first_kernel(pos_ref, own_ref, up_ref, down_ref, send_ref, keep_ref):
    x, f = pos_ref[0], pos_ref[3]
    up = jnp.where(f >= 2, up_ref[...].astype(F32), 0.0)
    summed = own_ref[...].astype(F32) + up + down_ref[...].astype(F32)
    q = summed.shape[1] // 4
    first = jnp.concatenate([summed[:, :q], summed[:, 2 * q : 3 * q]], axis=1)
    second = jnp.concatenate([summed[:, q : 2 * q], summed[:, 3 * q :]], axis=1)
    send_ref[...] = jnp.where(x == 0, second, first).astype(BF16)
    keep_ref[...] = jnp.where(x == 0, first, second)


def unpack_ffn_second_kernel(pos_ref, keep_ref, got_ref, gfc_ref, send_ref, hold_ref):
    x, c = pos_ref[0], pos_ref[1]
    keep, got = keep_ref[...], got_ref[...].astype(F32)
    h = keep.shape[1] // 2
    rows = keep.shape[0] // 2
    first = jnp.where(x == 0, keep, got)
    second = jnp.where(x == 0, got, keep)
    gfc_ref[...] = jnp.concatenate([first[:, :h].T, second[:, :h].T], axis=1)
    both = jnp.concatenate([first[:, h:], second[:, h:]], axis=1)
    top, low = both[:rows, :], both[rows:, :]
    send_ref[...] = jnp.where(c == 0, low, top).astype(BF16)
    hold_ref[...] = jnp.where(c == 0, top, low)


def unpack_ffn_third_kernel(pos_ref, hold_ref, got_ref, gprojt_ref):
    c = pos_ref[1]
    hold, got = hold_ref[...], got_ref[...].astype(F32)
    gprojt_ref[...] = jnp.concatenate(
        [jnp.where(c == 0, hold, got), jnp.where(c == 0, got, hold)], axis=1
    )


def finish_kernel(
    middle_ref,
    act_own_ref,
    act_sib_ref,
    act_far_ref,
    dx1_ref,
    dn1_ref,
    near_ref,
    coming_ref,
    x_ref,
    norms_ref,
    act_ref,
    grad_ref,
):
    act_ref[...] = (middle_ref[...] + total((act_own_ref, act_sib_ref, act_far_ref))).T.astype(BF16)
    dn1 = total((dn1_ref, near_ref, coming_ref))
    xhat, factor = xhat_of(x_ref[...].astype(F32))
    grads = dx1_ref[...] + norm_back(dn1, norms_ref[0:1, :], xhat, factor)
    grad_ref[...] = grads.T.astype(BF16)


def fill_bias(start_ref, bias_ref):
    keys, rows = bias_ref.shape
    key_ids = lax.broadcasted_iota(jnp.int32, (keys, rows), 0)
    row_ids = lax.broadcasted_iota(jnp.int32, (keys, rows), 1) + (keys - rows)
    allowed = (key_ids >= start_ref[...]) & (key_ids <= row_ids)
    bias_ref[...] = jnp.where(allowed, 0.0, NEG)


def head_slices(width):
    pairs = width // (2 * HEAD_DIM)
    return pairs, width - pairs * 2 * HEAD_DIM


def attn_fwd_kernel(
    q_ref,
    k_ref,
    v_ref,
    start_ref,
    x_ref,
    wo_ref,
    norms_ref,
    o_ref,
    lse_ref,
    middle_ref,
    n2_ref,
    qt,
    vt,
    ot,
    bias,
):
    width = q_ref.shape[1]
    fill_bias(start_ref, bias)
    qt[...] = (q_ref[...].astype(F32) * HEAD_DIM ** (-0.5)).T.astype(BF16)
    vt[...] = v_ref[...].astype(F32).T.astype(BF16)
    pairs, rest = head_slices(width)

    def one(keys, queries, values, row, head):
        scores = nn(keys, queries) + bias[...]
        peak = jnp.max(scores, axis=0, keepdims=True)
        terms = jnp.exp(scores - peak)
        summed = jnp.sum(terms, axis=0, keepdims=True)
        ot[pl.ds(row, HEAD_DIM), :] = nn(values, terms.astype(BF16)) / summed
        lse_ref[pl.ds(head, 1), :] = peak + jnp.log(summed)

    def pair(p, _):
        at = pl.multiple_of(p * 128, 128)
        keys = k_ref[:, pl.ds(at, 128)]
        queries = qt[pl.ds(at, 128), :]
        rows = lax.broadcasted_iota(jnp.int32, queries.shape, 0)
        for h in range(2):
            row = pl.multiple_of(at + h * HEAD_DIM, HEAD_DIM)
            one(
                keys,
                jnp.where((rows < HEAD_DIM) == (h == 0), queries, jnp.zeros_like(queries)),
                vt[pl.ds(row, HEAD_DIM), :],
                row,
                2 * p + h,
            )
        return 0

    lax.fori_loop(0, pairs, pair, 0)
    if rest:
        at = pairs * 128
        one(k_ref[:, at:], qt[at:, :], vt[at:, :], at, 2 * pairs)
    o_ref[...] = ot[...].T.astype(BF16)
    middle = x_ref[...].astype(F32) + nn(o_ref[...], wo_ref[...])
    middle_ref[...] = middle
    xhat, _ = xhat_of(middle)
    n2_ref[...] = (xhat * norms_ref[2:3, :] + norms_ref[3:4, :]).astype(BF16)


def attn_bwd_kernel(
    dn2_own_ref,
    dn2_sib_ref,
    dn2_far_ref,
    gz_ref,
    middle_ref,
    norms_ref,
    wo_ref,
    q_ref,
    k_ref,
    v_ref,
    lse_ref,
    start_ref,
    act_ref,
    projt_ref,
    dx1_ref,
    dy_ref,
    sums_ref,
    dq_ref,
    dk_ref,
    dv_ref,
    act_own_ref,
    act_far_ref,
    act_sib_ref,
    act_far_sib_ref,
    do_ref,
    qt,
    dot_s,
    kt,
    dqt,
    bias,
    rows_all,
):
    width = q_ref.shape[1]
    scale = HEAD_DIM ** (-0.5)
    dn2 = total((dn2_own_ref, dn2_sib_ref, dn2_far_ref))
    xhat, factor = xhat_of(middle_ref[...])
    sums_ref[0:1, :] = jnp.sum(dn2 * xhat, axis=0, keepdims=True)
    sums_ref[1:2, :] = jnp.sum(dn2, axis=0, keepdims=True)
    dx1 = gz_ref[...].astype(F32) + norm_back(dn2, norms_ref[2:3, :], xhat, factor)
    dx1_ref[...] = dx1
    dy_ref[...] = dx1.astype(BF16)
    do_ref[...] = nt(dy_ref[...], wo_ref[...]).astype(BF16)
    fill_bias(start_ref, bias)
    qt[...] = (q_ref[...].astype(F32) * scale).T.astype(BF16)
    dot_s[...] = do_ref[...].astype(F32).T.astype(BF16)
    kt[...] = k_ref[...].astype(F32).T.astype(BF16)
    pairs, rest = head_slices(width)

    def one(keys, values, queries_t, douts_t, keys_t, queries, douts, row, head):
        scores = nn(keys, queries_t) + bias[...]
        probs = jnp.exp(scores - lse_ref[pl.ds(head, 1), :])
        dprobs = nn(values, douts_t)
        delta = jnp.sum(probs * dprobs, axis=0, keepdims=True)
        dscores = (probs * (dprobs - delta)).astype(BF16)
        dqt[pl.ds(row, HEAD_DIM), :] = nn(keys_t, dscores)
        return nn(dscores, queries), nn(probs.astype(BF16), douts)

    def scaled(values):
        return (values.astype(F32) * scale).astype(BF16)

    def pair(p, _):
        at = pl.multiple_of(p * 128, 128)
        keys = k_ref[:, pl.ds(at, 128)]
        values = v_ref[:, pl.ds(at, 128)]
        queries = scaled(q_ref[:, pl.ds(at, 128)])
        douts = do_ref[:, pl.ds(at, 128)]
        queries_t = qt[pl.ds(at, 128), :]
        douts_t = dot_s[pl.ds(at, 128), :]
        rows = lax.broadcasted_iota(jnp.int32, queries_t.shape, 0)
        lanes = lax.broadcasted_iota(jnp.int32, queries.shape, 1)
        dk_sum = dv_sum = None
        for h in range(2):
            row = pl.multiple_of(at + h * HEAD_DIM, HEAD_DIM)
            in_rows = (rows < HEAD_DIM) == (h == 0)
            in_lanes = (lanes < HEAD_DIM) == (h == 0)
            zero_t, zero = jnp.zeros_like(queries_t), jnp.zeros_like(queries)
            dk_part, dv_part = one(
                keys,
                values,
                jnp.where(in_rows, queries_t, zero_t),
                jnp.where(in_rows, douts_t, zero_t),
                kt[pl.ds(row, HEAD_DIM), :],
                jnp.where(in_lanes, queries, zero),
                jnp.where(in_lanes, douts, zero),
                row,
                2 * p + h,
            )
            dk_sum = dk_part if h == 0 else dk_sum + dk_part
            dv_sum = dv_part if h == 0 else dv_sum + dv_part
        dk_ref[:, pl.ds(at, 128)] = dk_sum.astype(BF16)
        dv_ref[:, pl.ds(at, 128)] = dv_sum.astype(BF16)
        return 0

    lax.fori_loop(0, pairs, pair, 0)
    if rest:
        at = pairs * 128
        dk_part, dv_part = one(
            k_ref[:, at:],
            v_ref[:, at:],
            qt[at:, :],
            dot_s[at:, :],
            kt[at:, :],
            scaled(q_ref[:, at:]),
            do_ref[:, at:],
            at,
            2 * pairs,
        )
        dk_ref[:, at:] = dk_part.astype(BF16)
        dv_ref[:, at:] = dv_part.astype(BF16)
    dq_ref[...] = (dqt[...].T * scale).astype(BF16)
    tok = q_ref.shape[0]

    def forward(i):
        at = pl.ds(pl.multiple_of(i * tok, tok), tok)
        rows_all[at, :] = nt(act_ref[at, :], projt_ref[...]).astype(BF16)

    repeat(4, True, forward)
    y_refs = (act_own_ref, act_far_ref, act_sib_ref, act_far_sib_ref)
    for y_ref, at in zip(y_refs, members_of(tok)):
        y_ref[...] = rows_all[at, :]


def xhat_of(values):
    center = jnp.mean(values, axis=-1, keepdims=True)
    centered = values - center
    variance = jnp.mean(centered * centered, axis=-1, keepdims=True)
    factor = lax.rsqrt(variance + EPS)
    return centered * factor, factor


def norm_back(grads, gain, xhat, factor):
    e = grads * gain
    return factor * (
        e
        - jnp.mean(e, axis=-1, keepdims=True)
        - xhat * jnp.mean(e * xhat, axis=-1, keepdims=True)
    )


def add(*terms):
    acc = terms[0].astype(F32)
    for term in terms[1:]:
        acc = acc + term.astype(F32)
    return acc


def segment_starts(dealt_lengths, seq_order, first_row, rows):
    lengths = dealt_lengths[0].reshape(-1)
    order = seq_order[0]
    count = lengths.shape[0]
    arrival = jnp.arange(count, dtype=jnp.int32)
    before = (order[:, None] < arrival[None, :]).astype(jnp.int32)
    begins = jnp.sum(before * lengths[:, None], axis=0)
    ids = first_row + jnp.arange(rows, dtype=jnp.int32)
    reached = begins[:, None] <= ids[None, :]
    return jnp.max(jnp.where(reached, begins[:, None], 0), axis=0)


def tiled(value):
    if value.ndim == 2 and value.shape[0] % 128 == 0 and value.shape[1] % 128:
        return value.reshape(value.shape[0] // 8, 8, value.shape[1])
    return value


def barrier(value, fence):
    leaves, tree = jax.tree.flatten(value)
    kept = lax.optimization_barrier(([tiled(v) for v in leaves], fence))[0]
    return tree.unflatten([k.reshape(v.shape) for k, v in zip(kept, leaves)])


def permute(value, axis, pairs):
    return lax.ppermute(tiled(value), axis, pairs).reshape(value.shape)


class Clock:
    def __init__(self):
        self.fence = ()

    def __call__(self, value):
        if not self.fence:
            return value
        return barrier(value, self.fence)

    def tick(self, *done):
        self.fence = tuple(tiled(v) for v in jax.tree.leaves(done))


def per_device(
    tokens,
    qkv_weight,
    out_weight,
    fc_weight,
    proj_weight,
    norm_params,
    grad_out,
    dealt_lengths,
    seq_order,
):
    n_dp, n_f = lax.axis_size("dp"), lax.axis_size("fsdp")
    n_y, n_z = n_dp // 2, n_f // 2
    dp, f = lax.axis_index("dp"), lax.axis_index("fsdp")
    x, c = dp & 1, f & 1
    pos = jnp.stack([x, c, dp, f]).astype(jnp.int32)
    tok, width = tokens.shape
    seq_longest = n_f * tok // dealt_lengths.shape[1] // 2
    halo = -(-seq_longest // tok)
    halo += halo % 2

    now = Clock()

    def run(*args, **kwargs):
        made = call(*args, **kwargs)
        return lambda *operands: made(*now(operands))

    def xor(value, axis, bits):
        size = n_dp if axis == "dp" else n_f
        return permute(now(value), axis, [(i, i ^ bits) for i in range(size)])

    def to_core(value):
        return xor(value, "fsdp", 1)

    def to_x(value):
        return xor(value, "dp", 1)

    def to_y(value, k):
        return xor(value, "dp", 2 * k)

    def to_z(value, k):
        return xor(value, "fsdp", 2 * k)

    def along_z(value, step, senders):
        pairs = [(2 * z + i, 2 * (z + step) + i) for z in senders for i in range(2)]
        return permute(now(value), "fsdp", pairs)

    def joined(*values):
        return jnp.concatenate(values, axis=0)

    z_at = f >> 1
    others_z, others_y = range(1, n_z), range(1, n_y)

    def by_z(choose):
        choices = [choose(z) for z in range(n_z)]
        value = choices[0]
        for z in range(1, n_z):
            if choices[z] is not choices[z - 1]:
                value = jnp.where(z_at >= z, choices[z], value)
        return value

    k_rows, nq = qkv_weight.shape
    no = out_weight.shape[1]
    half, wide = k_rows // 2, 2 * (nq + no)
    rows = (half // 2 + 7) // 8 * 8
    own_first, own_second = run(pack_attn_kernel, [((rows, wide), BF16)] * 2, [VM, VM])(
        qkv_weight, out_weight.T
    )
    now.tick(own_first, own_second)

    firsts = [own_first] + [to_z(own_first, dz) for dz in others_z]
    ff_half = fc_weight.shape[1] // 2
    sub = proj_weight.shape[0] // 4
    send, keep = run(
        pack_ffn_first_kernel, [((ff_half, k_rows + sub), BF16)] * 2, [SM, VM, VM])(pos, fc_weight, proj_weight.T)
    got = to_x(send)
    norm_x = to_x(norm_params)
    now.tick(firsts, got, norm_x)

    stack = {(0, 0, 0): jnp.stack(firsts)}
    seconds = [own_second] + [to_z(own_second, dz) for dz in others_z]
    for dy in others_y:
        stack[0, dy, 0] = to_y(stack[0, 0, 0], dy)
    stack[0, 0, 1] = to_x(stack[0, 0, 0])
    fct, send, hold = run(
        pack_ffn_second_kernel,
        [((ff_half, 2 * k_rows), BF16)] + [((no, 2 * sub), BF16)] * 2,
        [SM, VM, VM])(pos, keep, got)
    now.tick(seconds, stack, send)

    got = to_core(send)
    norm_pairs = jnp.stack([norm_params, norm_x])
    norm_pairs = [norm_pairs] + [to_y(norm_pairs, dy) for dy in others_y]
    stack[1, 0, 0] = jnp.stack(seconds)
    stack[1, 0, 1] = to_x(stack[1, 0, 0])
    for dy in others_y:
        stack[1, dy, 0] = to_y(stack[1, 0, 0], dy)
    grad_out = now(grad_out)
    even = [tokens]
    for _ in range(halo // 2):
        even.append(along_z(even[-1], 1, range(n_z - 1)))
    stacks, arrays = [], []

    def cross(*keys):
        stacks.extend([(key + (0,),) for key in keys])
        arrays.extend(stack[key] for key in keys)
        stacks.append(tuple(key + (1,) for key in keys))
        arrays.append(to_core(joined(*[stack[key] for key in keys])))

    cross((0, 0, 0), (0, 0, 1), (1, 0, 0), *[(0, dy, 0) for dy in others_y])
    (own_ffn,) = run(
        pack_ffn_third_kernel, [((ff_half, 2 * (k_rows + sub)), BF16)], [SM, VM, VM, VM])(pos, fct, hold, got)
    now.tick(stack, even[-1], arrays[-1], own_ffn, norm_pairs, grad_out)

    ups, downs, ffn = [own_ffn], [own_ffn], {(0, 0): own_ffn}

    def ffn_over_z(t):
        ups.append(along_z(ups[-1], 1, range(t - 1, n_z - 1)))
        downs.append(along_z(downs[-1], -1, range(1, n_z - t + 1)))

    def pick(t):
        return by_z(lambda z: ups[z - (z ^ t)] if z ^ t < z else downs[(z ^ t) - z])

    for dy in others_y:
        stack[0, dy, 1] = to_x(stack[0, dy, 0])
        stack[1, dy, 1] = to_y(stack[1, 0, 1], dy)
    rows_before = []
    for distance in range(1, halo + 1):
        if distance % 2:
            near = distance // 2
            rows_before.append(to_core(jnp.where(c == 0, even[near], even[near + 1])))
        else:
            rows_before.append(even[distance // 2])
    x_rows = joined(*rows_before[::-1], tokens)
    cross((1, 0, 1))
    for dy in others_y:
        cross((1, dy, 0))
    norms = jnp.concatenate(
        [
            sum(
                jnp.where((dp ^ r) == j, norm_pairs[r >> 1][r & 1].astype(F32), 0.0)
                for r in range(n_dp)
            )
            for j in range(n_dp)
        ],
        axis=1,
    )
    xhat_one, factor_one = xhat_of(x_rows.astype(F32))
    normed = (xhat_one * norms[0] + norms[1]).astype(BF16)
    now.tick(arrays, stack, normed)

    cross(*[(part, dy, 1) for dy in others_y for part in range(2)])
    now.tick(arrays[-1])
    ffn_over_z(1)
    for dy in others_y:
        ffn[dy, 0] = to_y(own_ffn, dy)
    gz_far = to_x(grad_out)
    gz_sib = to_core(grad_out)
    square = ((width, width), BF16)
    dims = (n_dp, n_f, nq, no)
    wq, wk, wv, wo = run(
        functools.partial(assemble_attn_kernel, stacks, dims),
        [square] * 4,
        [SM] + [ANY] * len(arrays),
        [
            pltpu.VMEM((2, n_dp * n_f, rows, wide), BF16),
            pltpu.SemaphoreType.DMA((2 * n_dp * n_f,)),
        ])(pos, *arrays)
    now.tick(wq, wk, wv, wo, ups, downs, ffn, gz_far, gz_sib)

    ffn[0, 1] = pick(1)
    ffn_over_z(2)
    for dy in others_y:
        ffn[dy, 1] = to_y(ffn[0, 1], dy)
    gz_far_sib = to_core(gz_far)
    queries, all_keys, values = run(
        qkv_kernel, [((tok, width), BF16)] + [(normed.shape, BF16)] * 2, [VM] * 4)(normed, wq, wk, wv)
    now.tick(queries, all_keys, values, ups, downs, ffn, gz_far_sib)

    ffn[0, 2] = pick(2)
    for t in others_z[2:]:
        ffn_over_z(t)
    for dy in others_y:
        ffn[dy, 2] = to_y(ffn[0, 2], dy)
    span = (halo + 1) * tok
    starts = segment_starts(dealt_lengths, seq_order, f * tok, tok) - (f - halo) * tok
    starts = starts.reshape(1, tok).astype(jnp.int32)
    heads = width // HEAD_DIM
    attended, lse, middle, normed_two = run(
        attn_fwd_kernel,
        [((tok, width), BF16), ((heads, tok), F32), ((tok, width), F32), ((tok, width), BF16)],
        [VM] * 7,
        [
            pltpu.VMEM((width, tok), BF16),
            pltpu.VMEM((width, span), BF16),
            pltpu.VMEM((width, tok), F32),
            pltpu.VMEM((span, tok), F32),
        ])(queries, all_keys, values, starts, tokens, wo, norms)
    now.tick(attended, lse, middle, normed_two, ups, downs, ffn)

    n2_far = to_x(normed_two)
    n2_sib = to_core(normed_two)
    for t in others_z[2:]:
        ffn[0, t] = pick(t)
        for dy in others_y:
            ffn[dy, t] = to_y(ffn[0, t], dy)
    now.tick(n2_far, n2_sib, ffn)
    n2_far_sib = to_core(n2_far)
    n2_rows = [normed_two, n2_far, n2_sib, n2_far_sib]
    gz_rows = [grad_out, gz_far, gz_sib, gz_far_sib]

    ffn_keys = sorted(ffn)
    fct_full, projt_full = run(
        functools.partial(assemble_ffn_kernel, ffn_keys, (n_y, n_z)),
        [((n_z * ff_half, n_y * 2 * k_rows), BF16), ((n_z * 2 * no, n_y * 2 * sub), BF16)],
        [SM] + [ANY] * len(ffn_keys),
        [
            pltpu.VMEM((len(ffn_keys),) + own_ffn.shape, BF16),
            pltpu.SemaphoreType.DMA((len(ffn_keys),)),
        ])(pos, *[ffn[key] for key in ffn_keys])
    ff = fct_full.shape[0]
    rows_all = pltpu.VMEM((4 * tok, width), BF16)
    activated, dhidden, own, far, sib, far_sib = run(
        ffn_kernel,
        [((4 * tok, ff), BF16)] * 2 + [((tok, width), BF16)] * 4,
        [VM] * 10,
        [rows_all] * 3,
    )(*n2_rows, *gz_rows, fct_full, projt_full)
    now.tick(activated, dhidden, own, far, sib, far_sib)
    far = add(far, to_core(far_sib)).astype(BF16)
    now.tick(far)

    dn2_far = to_x(far)
    dn2_sib = to_core(sib)
    (ffn_grads,) = run(
        functools.partial(ffn_grads_kernel, (n_y, n_z)),
        [((n_y * n_z,) + own_ffn.shape, BF16)],
        [SM] + [VM] * 10,
        [
            pltpu.VMEM((n_z * ff_half, 4 * tok), BF16),
            pltpu.VMEM((width, 4 * tok), BF16),
            pltpu.VMEM((4 * tok, width), BF16),
        ])(pos, dhidden, *n2_rows, *gz_rows, activated)
    now.tick(ffn_grads, dn2_far, dn2_sib)

    part_of = {}
    far_y = {
        dz: [to_y(ffn_grads[dy * n_z + dz], dy) for dy in others_y] for dz in others_z[::-1][:-1]
    }
    big, small = (span, width), (tok, width)
    dx1, dy_low, norm_sums, dq, dk, dv, act_own, act_far, act_sib, act_far_sib = run(
        attn_bwd_kernel,
        [(small, F32), (small, BF16), ((2, width), F32), (small, BF16), (big, BF16), (big, BF16)]
        + [(small, BF16)] * 4,
        [VM] * 14,
        [
            pltpu.VMEM(small, BF16),
            pltpu.VMEM((width, tok), BF16),
            pltpu.VMEM((width, tok), BF16),
            pltpu.VMEM((width, span), BF16),
            pltpu.VMEM((width, tok), F32),
            pltpu.VMEM((span, tok), F32),
            rows_all,
        ])(own, dn2_sib, dn2_far, grad_out, middle, norms, wo, queries, all_keys, values, lse, starts, activated, projt_full)
    now.tick(dq, dk, dv, far_y, act_own, act_far, act_sib, act_far_sib)

    carry = [None, None]

    def ffn_back_z(s):
        reach = n_z - s
        for way, (step, senders) in enumerate(
            ((1, range(0, s)), (-1, range(n_z - s, n_z)))
        ):
            value = by_z(
                lambda z: part_of[z ^ (z + step * reach)]
                if 0 <= z + step * reach < n_z
                else part_of[n_z - 1]
            )
            if carry[way] is not None:
                value = add(value, carry[way]).astype(BF16)
            carry[way] = along_z(value, step, senders)

    ffn_grads = now(ffn_grads)
    next_y = [to_y(ffn_grads[dy * n_z + 1], dy) for dy in others_y]
    act_far_sib = to_core(act_far_sib)
    count = 2 * n_y * n_z
    block = ((count, rows, wide), BF16)
    keeps, sent, gots = {}, {}, {}
    keeps[0], sent[0], keeps[1], sent[1] = run(
        functools.partial(attn_grads_kernel, dims),
        [block] * 4,
        [SM] + [VM] * 6,
        [pltpu.VMEM((width, span), BF16), pltpu.VMEM((width, tok), BF16)],
    )(pos, normed, attended, dq, dk, dv, dy_low)
    now.tick(keeps, sent, next_y, act_far_sib)

    gots[1], gots[0] = to_core(sent[1]), to_core(sent[0])
    act_sib = to_core(act_sib)
    for dz, pieces in now(far_y).items():
        part_of[dz] = add(ffn_grads[dz], *pieces).astype(BF16)
    ffn_back_z(1)

    def core_sum(part, dy, dx, count=1):
        at = (part * n_y + dy) * n_z
        stop = at + count * n_z
        return add(keeps[dx][at:stop], gots[dx][at:stop])

    x_send = core_sum(0, 0, 1, n_y).astype(BF16)
    y_send = [core_sum(1, dy, 1).astype(BF16) for dy in others_y]
    now.tick(x_send, y_send, gots, act_sib)
    next_y = now(next_y)

    part_of[1] = add(ffn_grads[1], *next_y).astype(BF16)
    last_y = [to_y(ffn_grads[dy * n_z], dy) for dy in others_y]
    got_x = to_x(x_send)
    got_y = [to_y(value, dy) for dy, value in zip(others_y, y_send)]
    for s in range(2, n_z - 1):
        ffn_back_z(s)
    cut = halo * tok
    dn1, dn1_halo, norm_first = run(
        dn1_kernel, [(small, F32), ((cut, width), BF16), ((2, width), F32)], [VM] * 7
    )(dq, dk, dv, wq, wk, wv, x_rows)
    norm_rows = -(-4 * width // wide // 8) * 8

    def with_norms(value, norms):
        extra = norms.astype(BF16).reshape(-1, wide)
        extra = jnp.pad(extra, ((0, norm_rows - extra.shape[0]), (0, 0)))
        extra = jnp.broadcast_to(extra, value.shape[:-2] + extra.shape)
        return jnp.concatenate([value, extra], axis=-2)

    def norms_of(value):
        return value[0, -norm_rows:][: 4 * width // wide].reshape(4, width).astype(F32)

    now.tick(got_x, got_y, carry, dn1, dn1_halo, norm_first, last_y)
    got_x, got_y, dn1, dn1_halo, norm_first, last_y, act_far_sib = now(
        (got_x, got_y, dn1, dn1_halo, norm_first, last_y, act_far_sib)
    )
    part_of[0] = add(ffn_grads[0], *last_y).astype(BF16)

    norm_grads = joined(norm_first, norm_sums)
    first_x = [got_x[dy * n_z : (dy + 1) * n_z] for dy in range(n_y)]
    both = []
    for dy in others_y:
        value = [add(core_sum(0, dy, 0), first_x[dy]), core_sum(1, dy, 0)]
        value = jnp.concatenate([v.astype(BF16) for v in value], axis=1)
        both.append(to_y(with_norms(value, norm_grads), dy))
    act_far = add(act_far, act_far_sib).astype(BF16)
    second_x = add(core_sum(1, 0, 1), *got_y).astype(BF16)
    got_x = to_x(joined(second_x.reshape(-1, wide), act_far.reshape(-1, wide)))
    if n_z > 2:
        ffn_back_z(n_z - 1)
    def back(distance):
        return dn1_halo[cut - distance * tok : cut - (distance - 1) * tok]

    carried = [None] * (halo // 2 + 1)
    for near in range(halo // 2):
        got = to_core(back(2 * near + 1)).astype(F32)
        for level, wanted in ((near, 1), (near + 1, 0)):
            term = jnp.where(c != wanted, got, 0.0)
            carried[level] = term if carried[level] is None else carried[level] + term
    outgoing = [back(2 * level).astype(F32) + carried[level] for level in range(1, halo // 2 + 1)]
    coming = None
    for level in range(halo // 2, 0, -1):
        out = outgoing[level - 1]
        if coming is not None:
            out = out + coming
        coming = along_z(out.astype(BF16), -1, range(1, n_z)).astype(F32)
    now.tick(got_x, both, carry, coming)
    got_x, both, coming = now((got_x, both, coming))
    act_far = got_x[n_z * rows :].reshape(small)
    second_x = got_x[: n_z * rows].reshape(n_z, rows, wide)
    send, keep = run(
        unpack_ffn_first_kernel,
        [((ff_half, k_rows + sub), BF16), ((ff_half, k_rows + sub), F32)],
        [SM] + [VM] * 3,
    )(pos, part_of[0], *carry)
    norm_grads = norm_grads + sum(norms_of(value) for value in both)
    first_sum = add(core_sum(0, 0, 0), first_x[0], *[value[:, :rows] for value in both])
    second_sum = add(
        core_sum(1, 0, 0), second_x, *[value[:, rows : 2 * rows] for value in both]
    )
    sums = jnp.concatenate([first_sum.astype(BF16), second_sum.astype(BF16)], axis=1)
    sums = with_norms(sums, norm_grads)
    now.tick(sums)

    got = to_x(send)
    parts = [sums[0]] + [to_z(sums[dz], dz) for dz in others_z]
    activations, input_grad = run(finish_kernel, [((width, tok), BF16)] * 2, [VM] * 10)(
        middle,
        act_own,
        act_sib,
        act_far,
        dx1,
        dn1,
        carried[0].astype(BF16),
        coming.astype(BF16),
        tokens,
        norms,
    )
    grad_fc, send, hold = run(
        unpack_ffn_second_kernel,
        [(fc_weight.shape, F32), ((no, 2 * sub), BF16), ((no, 2 * sub), F32)],
        [SM, VM, VM])(pos, keep, got)
    (grad_proj,) = run(unpack_ffn_third_kernel, [(proj_weight.shape[::-1], F32)], [SM, VM, VM])(
        pos, hold, to_core(send)
    )
    parts = barrier(parts, (grad_fc, grad_proj, activations, input_grad))
    norm_grads = sum(norms_of(part[None]) for part in parts)
    norm_grads = norm_grads + lax.ppermute(norm_grads, "fsdp", [(i, i ^ 1) for i in range(n_f)])
    norm_grads = norm_grads + lax.ppermute(norm_grads, "dp", [(i, i ^ 1) for i in range(n_dp)])
    norm_grads = lax.dynamic_slice_in_dim(norm_grads, dp * k_rows, k_rows, axis=1)
    grad_qkv, grad_attn_out = run(
        functools.partial(unpack_attn_kernel, n_z, rows),
        [(qkv_weight.shape, F32), (out_weight.shape[::-1], F32)],
        [VM] * n_z,
        [pltpu.VMEM(out_weight.shape, F32)],
    )(*parts)
    return (activations.T, input_grad.T, grad_qkv, grad_attn_out.T, grad_fc, grad_proj.T, norm_grads)


def solution(mesh):
    in_specs = (
        P(("dp", "fsdp"), None),
        P("dp", "fsdp"),
        P("dp", "fsdp"),
        P("dp", "fsdp"),
        P("dp", "fsdp"),
        P(None, "dp"),
        P(("dp", "fsdp"), None),
        P("dp", None, None),
        P("dp", None),
    )
    out_specs = (
        P(("dp", "fsdp"), None),
        P(("dp", "fsdp"), None),
        P("dp", "fsdp"),
        P("dp", "fsdp"),
        P("dp", "fsdp"),
        P("dp", "fsdp"),
        P(None, "dp"),
    )
    return jax.shard_map(
        per_device, mesh=mesh, in_specs=in_specs, out_specs=out_specs, check_vma=False
    )
```
